32 devices in a mesh: row: 8 (over y, x, core), col: 4 (over z).
Axes of the slice: x: 2, y: 2, z: 4, core: 2. Of those that a mesh axis runs over, the one named last changes fastest.
Arguments:
- covariance: float32 [8192, 8192], P('row', 'col'), as said below
- innovations: float32 [512, 8, 1024], P('row', None, 'col'), may hold values from -6 to 6
- block_owner: int32 [32], replicated, may hold values from 0 to 31, as said below
- panel_index: int32 [1], replicated, may hold values from 0 to 15
Outputs:
- factor: float32 [8192, 8192], P('row', 'col')
- solved: float32 [512, 8192], P('col', 'row')
The draws below stay inside these ranges and needn't reach their ends.
Inputs may be any that keep to these rules, and one draw needn't show every extreme that they name: Storage block s holds global block block_owner[s]; every global block appears once; the storage blocks s with one value of s // 4 hold the blocks of one residue modulo 8, rising with s. `covariance`: symmetric positive definite.
All inputs are finite; a program needn't handle non-finite values.
Results may differ from the reference program's by a relative error of at most 0.0016.
Values may be sent and summed in bfloat16 or wider, within the bound.
A program may use at most 128 MiB of HBM per device.

```python
import jax
import jax.numpy as jnp
from jax import lax

B = 256
BR = 4
PANELS = 2
GROUPS = 8
ROWS_DEV = 1024
M = 8192
NBLK = 32
P_SIZE = 512


def draw_covariance(key, part):
    base_key = jax.random.fold_in(key, 11)
    load_key, nugget_key = jax.random.split(base_key)
    shared_key = jax.random.fold_in(base_key, 37)
    latent = 2 * B
    loadings = jax.random.normal(load_key, (M, latent), jnp.float32)
    weights = jax.random.uniform(shared_key, (M,), jnp.float32, 0.7, 1.3)
    nugget = jnp.exp(jax.random.uniform(nugget_key, (M,), jnp.float32, -0.6931472, 0.6931472))
    row_block = jnp.arange(M, dtype=jnp.int32) // B
    indicator = (row_block[:, None] == jnp.arange(NBLK, dtype=jnp.int32)[None, :]).astype(jnp.float32)
    shared = indicator * (1.7320508 * weights)[:, None]
    combined = jnp.concatenate([loadings * (1.0 / latent ** 0.5), shared], axis=1)
    matrix = jnp.dot(combined, combined.T, precision=lax.Precision.HIGHEST)
    matrix = 0.5 * (matrix + matrix.T)
    return matrix + jnp.diag(nugget)


def draw_block_owner(key, part):
    row_order = jax.random.permutation(jax.random.fold_in(key, 23), GROUPS)
    positions = jnp.arange(NBLK, dtype=jnp.int32)
    return (positions % BR * GROUPS + row_order[positions // BR]).astype(jnp.int32)


def level_of(key, dims, cuts, least, largest):
    gain, own = 1.0, jax.random.fold_in(key, 6)
    for position, shards_of in cuts:
        steps = jnp.exp(jax.random.uniform(jax.random.fold_in(own, position), (shards_of,), jnp.float32, least / len(cuts), largest / len(cuts)))
        gain = gain * jnp.repeat(steps, dims[position] // shards_of).reshape([-1 if axis == position else 1 for axis in range(len(dims))])
    return gain


def bell_draw(own_key, extent, deviation, reach, cuts=(), held_as=jnp.bfloat16):
    entries = deviation * jax.random.normal(own_key, extent, jnp.float32)
    if cuts:
        entries = entries * level_of(own_key, extent, cuts, -0.22, 0.18)
    return jnp.clip(entries, -reach, reach).astype(held_as)


def setup_inputs(seed: int = 0) -> dict:
    splits = jax.random.split(jax.random.key(seed), 5)
    covariance = draw_covariance(jax.random.fold_in(splits[4], 71), 0)
    innovations = bell_draw(splits[1], (P_SIZE, GROUPS, ROWS_DEV), 1.0, 6.0, ((0, 8), (2, 4)), jnp.float32)
    block_owner = draw_block_owner(jax.random.fold_in(splits[4], 71), 0)
    panel_index = jax.random.randint(splits[3], (1,), 0, NBLK // 2).astype(jnp.int32)
    return dict(covariance=covariance, innovations=innovations, block_owner=block_owner, panel_index=panel_index)


CONTRACT_LAST = (((1,), (1,)), ((), ()))

def lower_solve(factor, right_side):
    return jax.scipy.linalg.solve_triangular(factor, right_side, lower=True)

def reference(covariance, innovations, block_owner, panel_index):
    matrix_order = covariance.shape[0]
    blocks = matrix_order // B
    matrix = covariance
    solved = innovations.reshape(innovations.shape[0], matrix_order)
    row_owner = jnp.repeat(block_owner, B)
    positions = jnp.arange(blocks, dtype=jnp.int32)
    for panel_turn in range(PANELS):
        target = panel_index[0] + panel_turn
        slot_index = jnp.sum(jnp.where(block_owner == target, positions, 0)).astype(jnp.int32)
        panel_start = slot_index * B
        column = lax.dynamic_slice_in_dim(matrix, panel_start, B, 1)
        diagonal = lax.dynamic_slice_in_dim(column, panel_start, B, 0)
        factor = jnp.linalg.cholesky(diagonal)
        live_rows = row_owner > target
        panel_rows = jnp.where(live_rows[:, None], lower_solve(factor, column.T).T, 0.0)
        panel_half = panel_rows.astype(jnp.bfloat16)
        matrix = matrix - lax.dot_general(panel_half.astype(jnp.float32), panel_half.astype(jnp.float32), CONTRACT_LAST, preferred_element_type=jnp.float32)
        innovation_block = lax.dynamic_slice_in_dim(solved, panel_start, B, 1)
        whitened = lower_solve(factor, innovation_block.T).T
        solved = solved - lax.dot_general(whitened.astype(jnp.bfloat16).astype(jnp.float32), panel_half.astype(jnp.float32), CONTRACT_LAST, preferred_element_type=jnp.float32)
        solved = lax.dynamic_update_slice_in_dim(solved, whitened, panel_start, 1)
        row_block = lax.dynamic_slice_in_dim(matrix, panel_start, B, 0)
        row_block = jnp.where(live_rows[None, :], 0.0, row_block)
        matrix = lax.dynamic_update_slice_in_dim(matrix, row_block, panel_start, 0)
        column_old = lax.dynamic_slice_in_dim(matrix, panel_start, B, 1)
        column_new = jnp.where(live_rows[:, None], panel_rows, column_old)
        column_new = lax.dynamic_update_slice_in_dim(column_new, factor, panel_start, 0)
        matrix = lax.dynamic_update_slice_in_dim(matrix, column_new, panel_start, 1)
    return (matrix, solved)
```

```python
import functools

import jax
import jax.numpy as jnp
from jax import lax
from jax.experimental import pallas as pl
from jax.experimental.pallas import tpu as pltpu
from jax.sharding import PartitionSpec as P

B = 256
PANELS = 2
SUB = 64
G8 = SUB // 8
LANES = 128
TW = 2 * B // LANES
HIGHEST = lax.Precision.HIGHEST

LAST = (((1,), (1,)), ((), ()))
FIRST = (((0,), (0,)), ((), ()))
PLAIN = (((1,), (0,)), ((), ()))


def dot(a, b, dims=PLAIN, precision=None):
    return lax.dot_general(a, b, dims, precision=precision, preferred_element_type=jnp.float32)


def split_bf16(x):
    hi = x.astype(jnp.bfloat16)
    lo = (x - hi.astype(jnp.float32)).astype(jnp.bfloat16)
    return hi, lo


def dot3(a, b, dims=PLAIN):
    ah, al = split_bf16(a)
    bh, bl = split_bf16(b)
    return dot(ah, bh, dims) + (dot(ah, bl, dims) + dot(al, bh, dims))


def lanes(x):
    return jnp.broadcast_to(x, (8, LANES))


def factor_panel(s_ref, p_ref):
    sub_iota = lax.broadcasted_iota(jnp.int32, (8, LANES), 0)
    rows = [[s_ref[8 * g : 8 * g + 8, LANES * t : LANES * (t + 1)] for t in range(TW)] for g in range(G8)]
    for b in range(G8):
        c0 = 8 * b
        col = [[lanes(rows[g][0][:, c0 + j : c0 + j + 1]) for j in range(8)] for g in range(b, G8)]
        e = [[lanes(col[0][j][i : i + 1, :]) for j in range(i + 1)] for i in range(8)]
        r = []
        l = [[None] * 8 for _ in range(8)]
        for j in range(8):
            rj = lax.rsqrt(e[j][j])
            r.append(rj)
            for i in range(j + 1, 8):
                l[i][j] = e[i][j] * rj
            for i in range(j + 1, 8):
                for k in range(j + 1, i + 1):
                    e[i][k] = e[i][k] - l[i][j] * l[k][j]
        y = []
        for i in range(8):
            yi = []
            for t in range(TW):
                v = lanes(rows[b][t][i : i + 1, :])
                for j in range(i):
                    v = v - l[i][j] * y[j][t]
                yi.append(v * r[i])
            y.append(yi)
        for t in range(TW):
            u = y[0][t]
            for i in range(1, 8):
                u = jnp.where(sub_iota == i, y[i][t], u)
            p_ref[8 * b : 8 * b + 8, LANES * t : LANES * (t + 1)] = u
        for g in range(b + 1, G8):
            cs = []
            for j in range(8):
                v = col[g - b][j]
                for k in range(j):
                    v = v - l[j][k] * cs[k]
                cs.append(v * r[j])
            for t in range(TW):
                v = rows[g][t]
                for j in range(8):
                    v = v - cs[j] * y[j][t]
                rows[g][t] = v


MESH = pl.DeviceIdType.MESH
CHUNKS = 16
LAG = 2
CODE = 32767.0
TINY = 1e-37
STEPS = PANELS * (B // SUB)


def factor_step(k, turn, s_ref, p_ref, u_ref, z_ref):
    factor_panel(s_ref, p_ref)
    start = pl.multiple_of(k * SUB, SUB)
    u_ref[pl.ds(start, SUB), :] = pltpu.roll(p_ref[:, :B], start, 1)
    z_ref[turn, pl.ds(start, SUB), :] = p_ref[:, B:]
    left = p_ref[:, :B]
    rolled = pltpu.roll(left, B - SUB, 1)
    lane = lax.broadcasted_iota(jnp.int32, (SUB, B), 1)
    rolled = jnp.where(lane < B - SUB, rolled, 0.0)
    upd_a = dot(rolled, rolled, FIRST, HIGHEST)
    upd_z = dot(rolled, p_ref[:, B:], FIRST, HIGHEST)
    keep = B - SUB
    old = pltpu.roll(s_ref[SUB:, :B], B - SUB, 1)
    lane2 = lax.broadcasted_iota(jnp.int32, (keep, B), 1)
    old = jnp.where(lane2 < keep, old, 0.0)
    old_z = s_ref[SUB:, B:]
    s_ref[:keep, :B] = old - upd_a[:keep]
    s_ref[:keep, B:] = old_z - upd_z[:keep]
    s_ref[keep:, :] = jnp.zeros((SUB, 2 * B), jnp.float32)


def remote(src, dst, send, recv, where):
    return pltpu.make_async_remote_copy(
        src_ref=src, dst_ref=dst, send_sem=send, recv_sem=recv, device_id=where, device_id_type=MESH
    )


def rows_at(start, count):
    return pl.ds(pl.multiple_of(start, count), count)


class Spread:
    def __init__(self, buf, out, hop, send, recv, base, size, bits, hop_at=0, sem_at=0, whole=(), cross=None):
        me = lax.axis_index("row")
        self.buf, self.out, self.hop, self.send, self.recv = buf, out, hop, send, recv
        self.sem_at, self.cross = sem_at, cross
        self.stages = []
        start = base
        for bit in bits:
            digit = lax.rem(me // bit, 2)
            where = {"row": me + bit - 2 * bit * digit}
            if bit in whole:
                count, give = size, start
            else:
                count = size // 2
                give, start = start + (1 - digit) * count, start + digit * count
            self.stages.append((where, give, start, count, hop_at, bit in whole))
            hop_at += count
            size = count
        self.last, self.size = start, size

    def down(self, i):
        where, give, keep, count, at, _ = self.stages[i]
        n = self.sem_at + i
        return remote(self.buf.at[rows_at(give, count)], self.hop.at[pl.ds(at, count)], self.send.at[n], self.recv.at[n], where)

    def up(self, i):
        where, give, keep, count, at, _ = self.stages[i]
        n = self.sem_at + len(self.stages) + i
        rows = self.out.at[rows_at(keep, count)]
        return remote(rows, rows, self.send.at[n], self.recv.at[n], where)

    def over(self, shift):
        land, send, recv, nc = self.cross
        c = lax.axis_index("col")
        part = pl.ds((shift - 1) * self.size, self.size)
        return remote(
            self.buf.at[rows_at(self.last, self.size)], land.at[part], send.at[shift - 1], recv.at[shift - 1],
            {"col": lax.rem(c + shift, nc)},
        )

    def acts(self):
        steps = []

        def add(i):
            self.down(i).wait()
            _, _, keep, count, at, _ = self.stages[i]
            rows = rows_at(keep, count)
            self.buf[rows] = self.buf[rows] + self.hop[pl.ds(at, count)]

        for i in range(len(self.stages)):
            steps.append((lambda: None) if i == 0 else functools.partial(add, i - 1))
            steps.append(functools.partial(lambda i: self.down(i).start(), i))
        steps.append(functools.partial(add, len(self.stages) - 1))
        last = rows_at(self.last, self.size)
        if self.cross is not None:
            nc = self.cross[3]

            def send_over():
                for shift in range(1, nc):
                    self.over(shift).start()

            def add_over():
                total = self.buf[last]
                for shift in range(1, nc):
                    self.over(shift).wait()
                    total = total + self.cross[0][pl.ds((shift - 1) * self.size, self.size)]
                self.out[last] = total

            steps += [send_over, add_over]
            tail_steps = []
        else:
            def keep_last():
                self.out[last] = self.buf[last]

            inner = steps.pop()
            steps.append(lambda: (inner(), keep_last()))
        ups = [i for i in reversed(range(len(self.stages))) if not self.stages[i][5]]
        for i in ups:
            steps.append(functools.partial(lambda i: self.up(i).start(), i))
            steps.append(functools.partial(lambda i: self.up(i).wait(), i))
        pairs = []
        for i in range(0, len(steps) - 1, 2):
            pairs.append((steps[i], steps[i + 1]))
        acts = [lambda a=a, b=b: (a(), b()) for a, b in pairs]
        if len(steps) % 2:
            acts.append(steps[-1])
        return acts


def spread_pair(buf, out, hop, send, recv, size, nr, whole=(), cross=None):
    bits = [1 << b for b in range(nr.bit_length() - 1)]
    orders = [bits, [1] + bits[:0:-1]]
    half = size // 2
    whole_bits = bits[1:] if whole else ()
    both = []
    for part in range(2):
        land = None
        if cross is not None:
            ref, zs, zr, nc = cross
            land = (ref.at[part], zs.at[part], zr.at[part], nc)
        both.append(
            Spread(buf, out, hop.at[part], send.at[part], recv.at[part], part * half, half, orders[part], whole=whole_bits, cross=land).acts()
        )
    return [lambda a=a, b=b: (a(), b()) for a, b in zip(*both)]


def spread_scratch(size, width, dtype, nr, nc=None, whole=False):
    half, n = size // 2, nr.bit_length() - 1
    hop = half // 2 * n if whole else half
    out = [pltpu.VMEM((2, hop, width), dtype), pltpu.SemaphoreType.DMA((2, 2 * n)), pltpu.SemaphoreType.DMA((2, 2 * n))]
    if nc is not None:
        out += [
            pltpu.VMEM((2, (nc - 1) * (half // nr), width), dtype),
            pltpu.SemaphoreType.DMA((2, nc - 1)),
            pltpu.SemaphoreType.DMA((2, nc - 1)),
        ]
    return out


def choose(owner, wanted, value, otherwise):
    return jnp.where(jnp.full(value.shape, owner, jnp.int32) == wanted, value, otherwise)


def encode(x, top):
    part = jnp.sqrt(jnp.abs(x) * (1.0 / jnp.maximum(top, TINY)))
    code = (part * CODE + 0.5).astype(jnp.int32)
    return jnp.where(x < 0.0, -code, code).astype(jnp.int16)


def decode(code, top):
    part = code.astype(jnp.int32).astype(jnp.float32) * (1.0 / CODE)
    return part * jnp.abs(part) * top


def largest(x):
    top = jnp.max(jnp.abs(x), axis=0, keepdims=True)
    return jnp.max(top, axis=1, keepdims=True)


def front_kernel(
    nr, nc, own_ref, idx_ref, cov, inn,
    cols_o, tops_o, rowp_o, v_o, vs_o, f_o, z_o, x_o,
    w, wsem, vin, vinsem, outsem, zsem, fsem,
    cbuf, cols, rin, lin, rtx, ltx, rs, rr, ls, lr, tops, topland, topsend, toprecv, topsum,
    rbuf, rowp, rhop, rsend, rrecv,
    d0buf, d0, d0hop, d0send, d0recv, d0land, d0zs, d0zr,
    d1buf, d1, d1hop, d1send, d1recv, d1land, d1zs, d1zr,
    vsbuf, vs, vshop, vssend, vsrecv,
    vt, vst, vq, v, vtop, vtst, vtq, v1send, v1recv, v2send, v2recv, t1send, t1recv, t2send, t2recv,
    a_ref, s_ref, p_ref, u_ref, f_ref, z_ref, x_ref,
):
    r = lax.axis_index("row")
    c = lax.axis_index("col")
    rows, width = w.shape
    rb, cb = rows // B, width // B
    load = pltpu.make_async_copy(cov, w, wsem)
    vload = pltpu.make_async_copy(inn, vin, vinsem)
    vload.start()
    load.start()
    barrier = pltpu.get_barrier_semaphore()
    for shift in range(1, nr):
        pl.semaphore_signal(barrier, inc=1, device_id={"row": lax.rem(r + shift, nr)}, device_id_type=MESH)
    for shift in range(1, nc):
        pl.semaphore_signal(barrier, inc=1, device_id={"col": lax.rem(c + shift, nc)}, device_id_type=MESH)

    part_p, iw = inn.shape[0], inn.shape[2]
    ratio = nr // nc
    h = ratio * part_p

    def first_stop(shift):
        to = {"row": lax.rem(r + shift, nr)}
        return (
            remote(vt.at[lax.rem(r + shift, nr)], vst.at[rows_at(r * part_p, part_p)], v1send.at[shift], v1recv.at[shift], to),
            remote(vtop, vtst.at[rows_at(r * 8, 8)], t1send.at[shift], t1recv.at[shift], to),
        )

    def second_stop(shift):
        at = lax.rem(c + shift, nc)
        to = {"col": at}
        return (
            remote(vst.at[rows_at(at * h, h)], vq.at[:, rows_at(c * iw, iw)], v2send.at[shift], v2recv.at[shift], to),
            remote(
                vtst.at[rows_at(at * ratio * 8, ratio * 8)], vtq.at[rows_at(c * ratio * 8, ratio * 8)],
                t2send.at[shift], t2recv.at[shift], to,
            ),
        )

    with jax.named_scope("innovations"):
        vload.wait()
        top = largest(vin[:, 0, :])
        for group in range(1, nr):
            top = jnp.maximum(top, largest(vin[:, group, :]))
        vtop[...] = jnp.broadcast_to(top, vtop.shape)
        for group in range(nr):
            vt[group] = encode(vin[:, group, :], top)

    g = idx_ref[0]
    d0buf[...] = jnp.zeros_like(d0buf)
    d1buf[...] = jnp.zeros_like(d1buf)
    zero = jnp.zeros((B, B), jnp.float32)

    with jax.named_scope("load"):
        load.wait()

    def fill_cols(i, carry):
        span = rows_at(i * B, B)
        own = own_ref[r * rb + i]
        picked = []
        for t in range(PANELS):
            tile = zero
            for j in range(cb):
                tile = choose(own_ref[c * cb + j], g + t, w[span, j * B : (j + 1) * B], tile)
            top = largest(tile)
            tops[pl.ds(i * PANELS + t, 1), :] = jnp.broadcast_to(top, (1, LANES))
            cbuf[span, t * B : (t + 1) * B] = encode(tile, top)
            picked.append(tile)
        d0buf[...] = choose(own, g, picked[0], d0buf[...])
        d1buf[:B] = choose(own, g + 1, picked[0], d1buf[:B])
        d1buf[B:] = choose(own, g + 1, picked[1], d1buf[B:])
        return carry

    with jax.named_scope("columns"):
        lax.fori_loop(0, rb, fill_cols, 0)
    act0 = spread_pair(d0buf, d0, d0hop, d0send, d0recv, B, nr, cross=(d0land, d0zs, d0zr, nc))
    act1 = spread_pair(d1buf, d1, d1hop, d1send, d1recv, 2 * B, nr, cross=(d1land, d1zs, d1zr, nc))
    with jax.named_scope("barrier"):
        pl.semaphore_wait(barrier, nr - 1 + nc - 1)
    act0[0]()
    act1[0]()

    size = rows // CHUNKS

    def chunk(q):
        return rows_at(q * size, size)

    def right(src, q):
        return remote(src.at[chunk(q)], rin.at[chunk(q)], rs.at[q], rr.at[q], {"col": c + 1})

    def left(src, q):
        return remote(src.at[chunk(q)], lin.at[chunk(q)], ls.at[q], lr.at[q], {"col": c - 1})

    def relay(t, carry):
        q = t - LAG * c
        live = (q >= 0) & (q < CHUNKS)

        @pl.when(live & (c == 0))
        def _():
            right(cbuf, q).start()

        @pl.when(live & (c > 0))
        def _():
            right(cbuf, q).wait_recv()

            @pl.when(c < nc - 1)
            def _():
                rtx[chunk(q)] = rin[chunk(q)] + cbuf[chunk(q)]
                right(rtx, q).start()

        p = t - LAG * (nc - 1 - c)
        alive = (p >= 0) & (p < CHUNKS)

        @pl.when(alive & (c == nc - 1))
        def _():
            left(cbuf, p).start()

        @pl.when(alive & (c < nc - 1))
        def _():
            left(cbuf, p).wait_recv()

            @pl.when(c > 0)
            def _():
                ltx[chunk(p)] = lin[chunk(p)] + cbuf[chunk(p)]
                left(ltx, p).start()

        return carry

    def share_top(shift):
        count = tops.shape[0]
        return remote(
            tops, topland.at[pl.ds((shift - 1) * count, count)], topsend.at[shift], toprecv.at[shift],
            {"col": lax.rem(c + shift, nc)},
        )

    def fill_rows(i, carry):
        span = rows_at(i * B, B)
        for t in range(PANELS):
            tile = zero
            for k in range(rb):
                tile = choose(own_ref[r * rb + k], g + t, w[k * B : (k + 1) * B, span], tile)
            rbuf[t * B : (t + 1) * B, span] = tile.astype(jnp.bfloat16)
        return carry

    with jax.named_scope("rows"):
        lax.fori_loop(0, cb, fill_rows, 0)
    act_rows = spread_pair(rbuf, rowp, rhop, rsend, rrecv, PANELS * B, nr)

    @pl.when(c == 0)
    def _():
        rin[...] = jnp.zeros_like(rin)

    @pl.when(c == nc - 1)
    def _():
        lin[...] = jnp.zeros_like(lin)

    def leave():
        for shift in range(1, nr):
            for copy in first_stop(shift):
                copy.start()
        vst[rows_at(r * part_p, part_p)] = vt[r]
        vtst[rows_at(r * 8, 8)] = vtop[...]
        for shift in range(1, nc):
            share_top(shift).start()

    def pass_on():
        for shift in range(1, nr):
            for copy in first_stop(shift):
                copy.wait()
        for shift in range(1, nc):
            for copy in second_stop(shift):
                copy.start()
        vq[:, rows_at(c * iw, iw)] = vst[rows_at(c * h, h)]
        vtq[rows_at(c * ratio * 8, ratio * 8)] = vtst[rows_at(c * ratio * 8, ratio * 8)]

    crossed = nr.bit_length()
    for i in range(1, len(act0)):
        with jax.named_scope(f"diagonal{i}"):
            act0[i]()
        if i < crossed:
            with jax.named_scope(f"second{i}"):
                act1[i]()
        with jax.named_scope(f"early{i}"):
            if i == 1:
                leave()
            if i == 2:
                act_rows[0]()
            if i == crossed:
                pass_on()
            relay(i - 1, 0)
    early = len(act0) - 1

    outs = [
        pltpu.make_async_copy(src, dst, outsem.at[i])
        for i, (src, dst) in enumerate(
            [(rowp, rowp_o), (v, v_o), (vs, vs_o), (x_ref, x_o), (cols, cols_o), (topsum, tops_o)]
        )
    ]
    act_vs = spread_pair(vsbuf, vs, vshop, vssend, vsrecv, PANELS * h, nr, whole=True)

    def arrived():
        for shift in range(1, nc):
            for copy in second_stop(shift):
                copy.wait()
        for b in range(nc):
            for a in range(ratio):
                at, block = slice(a * part_p, (a + 1) * part_p), slice(b * iw, (b + 1) * iw)
                n = (b * ratio + a) * 8
                v[at, block] = decode(vq[at, block], vtq[n : n + 1, :1])
        outs[1].start()
        for t in range(PANELS):
            part = jnp.zeros((h, B), jnp.float32)
            for k in range(rb):
                part = choose(own_ref[r * rb + k], g + t, v[:, k * B : (k + 1) * B], part)
            vsbuf[t * h : (t + 1) * h] = part
        act_vs[0]()

    events = [[] for _ in range(STEPS)]
    later = act1[crossed:]
    for i, act in enumerate(later):
        events[i * (STEPS // PANELS) // len(later)].append(act)
    later = act_rows[1:]
    for i, act in enumerate(later):
        events[i * STEPS // len(later)].append(act)
        if i == len(later) - 1:
            events[i * STEPS // len(later)].append(outs[0].start)
    later = [arrived] + act_vs[1:]
    first = max(STEPS - len(later), 0)
    for i, act in enumerate(later):
        events[min(first + i, STEPS - 1)].append(act)

    total = CHUNKS + LAG * (nc - 1)
    each = -(-(total - early) // STEPS)
    row_i = lax.broadcasted_iota(jnp.int32, (B, B), 0)
    col_i = lax.broadcasted_iota(jnp.int32, (B, B), 1)
    a_ref[...] = d0[...]

    def panel(turn, carry):
        s_ref[:, :B] = a_ref[...]
        s_ref[:, B:] = jnp.where(row_i == col_i, 1.0, 0.0)

        def step(k, carry):
            now = turn * (B // SUB) + k
            with jax.named_scope("factor"):
                factor_step(k, turn, s_ref, p_ref, u_ref, z_ref)
            at = early + now * each
            with jax.named_scope("relay"):
                lax.fori_loop(at, at + each, relay, 0)
            for i, acts in enumerate(events):
                if acts:
                    @pl.when(now == i)
                    def _():
                        for m, act in enumerate(acts):
                            with jax.named_scope(f"event{i}_{m}"):
                                act()
            return carry

        lax.fori_loop(0, B // SUB, step, 0)
        z_ref[turn] = jnp.where(row_i >= col_i, z_ref[turn], 0.0)
        f_ref[turn] = jnp.where(row_i >= col_i, u_ref[...].T, 0.0)
        pltpu.make_async_copy(z_ref.at[turn], z_o.at[turn], zsem.at[turn]).start()
        pltpu.make_async_copy(f_ref.at[turn], f_o.at[turn], fsem.at[turn]).start()

        @pl.when(turn == 0)
        def _():
            low = dot3(d1[:B], z_ref[0], LAST)
            half = low.astype(jnp.bfloat16)
            x_ref[...] = half
            a_ref[...] = d1[B:] - dot(half, half, LAST)

        return carry

    lax.fori_loop(0, PANELS, panel, 0)
    outs[2].start()
    outs[3].start()

    with jax.named_scope("sum"):
        def add(q, carry):
            cols[chunk(q)] = cbuf[chunk(q)] + (rin[chunk(q)] + lin[chunk(q)])
            return carry

        lax.fori_loop(0, CHUNKS, add, 0)
        outs[4].start()
        count = tops.shape[0]
        top = tops[...]
        for shift in range(1, nc):
            share_top(shift).wait()
            top = top + topland[pl.ds((shift - 1) * count, count)]
        topsum[...] = top
        outs[5].start()

    with jax.named_scope("sent"):
        @pl.when(c < nc - 1)
        def _():
            lax.fori_loop(0, CHUNKS, lambda q, k: (right(cbuf, q).wait_send(), k)[1], 0)

        @pl.when(c > 0)
        def _():
            lax.fori_loop(0, CHUNKS, lambda q, k: (left(cbuf, q).wait_send(), k)[1], 0)

    with jax.named_scope("written"):
        for turn in range(PANELS):
            pltpu.make_async_copy(z_ref.at[turn], z_o.at[turn], zsem.at[turn]).wait()
            pltpu.make_async_copy(f_ref.at[turn], f_o.at[turn], fsem.at[turn]).wait()
        for out in outs:
            out.wait()


def front(nr, nc, owner, index, cov, inn):
    rows, width = cov.shape
    part_p, groups, iw = inn.shape
    ratio = nr // nc
    h = ratio * part_p
    f32, bf16, i16 = jnp.float32, jnp.bfloat16, jnp.int16
    smem = pl.BlockSpec(memory_space=pltpu.SMEM)
    anywhere = pl.BlockSpec(memory_space=pl.ANY)
    vmem = pltpu.VMEM
    dma = pltpu.SemaphoreType.DMA
    both = PANELS * B
    count = PANELS * (rows // B)
    scratch = [vmem((rows, width), f32), dma, vmem(inn.shape, f32), dma, dma((6,)), dma((PANELS,)), dma((PANELS,))]
    scratch += [vmem((rows, both), i16)] * 6 + [dma((CHUNKS,))] * 4
    scratch += [vmem((count, LANES), f32), vmem(((nc - 1) * count, LANES), f32), dma((nc,)), dma((nc,)), vmem((count, LANES), f32)]
    scratch += [vmem((both, width), bf16)] * 2 + spread_scratch(both, width, bf16, nr)
    for size in (B, 2 * B):
        scratch += [vmem((size, B), f32)] * 2 + spread_scratch(size, B, f32, nr, nc)
    scratch += [vmem((PANELS * h, B), f32)] * 2 + spread_scratch(PANELS * h, B, f32, nr, whole=True)
    scratch += [vmem((groups, part_p, iw), i16), vmem((nr * part_p, iw), i16), vmem((h, nc * iw), i16), vmem((h, nc * iw), f32)]
    scratch += [vmem((8, LANES), f32), vmem((nr * 8, LANES), f32), vmem((nr * 8, LANES), f32)]
    scratch += [dma((nr,)), dma((nr,)), dma((nc,)), dma((nc,))] * 2
    scratch += [vmem((B, B), f32), vmem((B, 2 * B), f32), vmem((SUB, 2 * B), f32), vmem((B, B), f32)]
    scratch += [vmem((PANELS, B, B), f32)] * 2 + [vmem((B, B), bf16)]
    return pl.pallas_call(
        functools.partial(front_kernel, nr, nc),
        out_shape=(
            jax.ShapeDtypeStruct((rows, both), i16),
            jax.ShapeDtypeStruct((count, LANES), f32),
            jax.ShapeDtypeStruct((both, width), bf16),
            jax.ShapeDtypeStruct((h, nc * iw), f32),
            jax.ShapeDtypeStruct((PANELS * h, B), f32),
            jax.ShapeDtypeStruct((PANELS, B, B), f32),
            jax.ShapeDtypeStruct((PANELS, B, B), f32),
            jax.ShapeDtypeStruct((B, B), bf16),
        ),
        in_specs=[smem, smem, anywhere, anywhere],
        out_specs=(anywhere,) * 8,
        scratch_shapes=scratch,
        compiler_params=pltpu.CompilerParams(
            collective_id=0, has_side_effects=True, vmem_limit_bytes=56 * 1024 * 1024
        ),
    )(owner, index, cov, inn)


def tail_kernel(
    own_ref, idx_ref, w_ref, cols_ref, tops_ref, rowp_ref, f_ref, z_ref, x_ref, vs_ref, v_ref,
    o_ref, vout_ref, q_ref, half_ref, *, rb, cb,
):
    j = pl.program_id(0)
    g = idx_ref[0]
    row0 = lax.axis_index("row") * rb
    col0 = lax.axis_index("col") * cb

    @pl.when(j == 0)
    def _():
        h = v_ref.shape[0]
        x = x_ref[...]
        zh, zl = split_bf16(z_ref[0])
        for k in range(cb):
            span = slice(k * B, (k + 1) * B)
            own = own_ref[col0 + k]
            q0 = dot(zh, rowp_ref[:B, span]) + dot(zl, rowp_ref[:B, span])
            q0 = jnp.where(own > g, q0, 0.0).astype(jnp.bfloat16)
            r1 = rowp_ref[B:, span].astype(jnp.float32) - dot(x, q0)
            q1 = dot3(z_ref[1], r1)
            q_ref[:B, span] = q0
            q_ref[B:, span] = jnp.where(own > g + 1, q1, 0.0).astype(jnp.bfloat16)
        for i in range(rb):
            span = slice(i * B, (i + 1) * B)
            own = own_ref[row0 + i]
            c0 = decode(cols_ref[span, :B], tops_ref[PANELS * i : PANELS * i + 1, :1])
            p0 = dot3(c0, z_ref[0], LAST)
            h0 = jnp.where(own > g, p0, 0.0).astype(jnp.bfloat16)
            c1 = decode(cols_ref[span, B:], tops_ref[PANELS * i + 1 : PANELS * i + 2, :1]) - dot(h0, x, LAST)
            p1 = dot3(c1, z_ref[1], LAST)
            half_ref[span, :B] = h0
            half_ref[span, B:] = jnp.where(own > g + 1, p1, 0.0).astype(jnp.bfloat16)
        w0 = dot(vs_ref[:h], z_ref[0], LAST, HIGHEST)
        w0h = w0.astype(jnp.bfloat16)
        w1 = dot(vs_ref[h:] - dot(w0h, x, LAST), z_ref[1], LAST, HIGHEST)
        w1h = w1.astype(jnp.bfloat16)
        for i in range(rb):
            span = slice(i * B, (i + 1) * B)
            own = own_ref[row0 + i]
            new = v_ref[:, span] - (dot(w0h, half_ref[span, :B], LAST) + dot(w1h, half_ref[span, B:], LAST))
            new = jnp.where(own == g, w0, new)
            vout_ref[:, span] = jnp.where(own == g + 1, w1, new)

    cown = own_ref[col0 + j]
    start = pl.multiple_of(j * B, B)
    o_ref[...] = w_ref[...] - dot(half_ref[...], q_ref[:, pl.ds(start, B)])

    @pl.when(cown > g)
    def _():
        for i in range(rb):
            rown = own_ref[row0 + i]

            @pl.when((rown == g) | ((rown == g + 1) & (cown > g + 1)))
            def _():
                o_ref[i * B : (i + 1) * B] = jnp.zeros((B, B), jnp.float32)

    for turn in range(PANELS):
        @pl.when(cown == g + turn)
        def _():
            for i in range(rb):
                span = slice(i * B, (i + 1) * B)
                rown = own_ref[row0 + i]

                @pl.when(rown > g + turn)
                def _():
                    left = w_ref[span]
                    if turn:
                        left = left - dot(half_ref[span, :B], x_ref[...], LAST)
                    o_ref[span] = dot3(left, z_ref[turn], LAST)

                @pl.when(rown == g + turn)
                def _():
                    o_ref[span] = f_ref[turn]


def tail(owner, index, w, cols, tops, rowp, factors, z, x, vs, v):
    rows, width = w.shape
    stripe = lambda j, a, b: (0, j)
    whole = lambda x: pl.BlockSpec(x.shape, lambda j, a, b: (0,) * x.ndim)
    return pl.pallas_call(
        functools.partial(tail_kernel, rb=rows // B, cb=width // B),
        grid_spec=pltpu.PrefetchScalarGridSpec(
            num_scalar_prefetch=2,
            grid=(width // B,),
            in_specs=[
                pl.BlockSpec((rows, B), stripe),
                whole(cols),
                whole(tops),
                whole(rowp),
                whole(factors),
                whole(z),
                whole(x),
                whole(vs),
                whole(v),
            ],
            out_specs=[pl.BlockSpec((rows, B), stripe), whole(v)],
            scratch_shapes=[
                pltpu.VMEM((2 * B, width), jnp.bfloat16),
                pltpu.VMEM((rows, 2 * B), jnp.bfloat16),
            ],
        ),
        out_shape=(jax.ShapeDtypeStruct(w.shape, w.dtype), jax.ShapeDtypeStruct(v.shape, v.dtype)),
    )(owner, index, w, cols, tops, rowp, factors, z, x, vs, v)


def per_device(covariance, innovations, block_owner, panel_index):
    nr, nc = lax.axis_size("row"), lax.axis_size("col")
    cols, tops, rowp, v, vs, factors, z, x = front(nr, nc, block_owner, panel_index, covariance, innovations)
    return tail(block_owner, panel_index, covariance, cols, tops, rowp, factors, z, x, vs, v)


def solution(mesh):
    placed = (P("row", "col"), P("row", None, "col"), P(), P())
    return jax.shard_map(
        per_device,
        mesh=mesh,
        in_specs=placed,
        out_specs=(P("row", "col"), P("col", "row")),
        check_vma=False,
    )
```

```python
import functools

import jax
import jax.numpy as jnp
from jax import lax
from jax.experimental import pallas as pl
from jax.experimental.pallas import tpu as pltpu
from jax.sharding import PartitionSpec as P

B = 256
PANELS = 2
SUB = 64
G8 = SUB // 8
LANES = 128
TW = 2 * B // LANES
HIGHEST = lax.Precision.HIGHEST

LAST = (((1,), (1,)), ((), ()))
FIRST = (((0,), (0,)), ((), ()))
PLAIN = (((1,), (0,)), ((), ()))


def dot(a, b, dims=PLAIN, precision=None):
    return lax.dot_general(a, b, dims, precision=precision, preferred_element_type=jnp.float32)


def split_bf16(x):
    hi = x.astype(jnp.bfloat16)
    lo = (x - hi.astype(jnp.float32)).astype(jnp.bfloat16)
    return hi, lo


def dot3(a, b, dims=PLAIN):
    ah, al = split_bf16(a)
    bh, bl = split_bf16(b)
    return dot(ah, bh, dims) + (dot(ah, bl, dims) + dot(al, bh, dims))


def lanes(x):
    return jnp.broadcast_to(x, (8, LANES))


def factor_panel(s_ref, p_ref):
    sub_iota = lax.broadcasted_iota(jnp.int32, (8, LANES), 0)
    rows = [[s_ref[8 * g : 8 * g + 8, LANES * t : LANES * (t + 1)] for t in range(TW)] for g in range(G8)]
    for b in range(G8):
        c0 = 8 * b
        col = [[lanes(rows[g][0][:, c0 + j : c0 + j + 1]) for j in range(8)] for g in range(b, G8)]
        e = [[lanes(col[0][j][i : i + 1, :]) for j in range(i + 1)] for i in range(8)]
        r = []
        l = [[None] * 8 for _ in range(8)]
        for j in range(8):
            rj = lax.rsqrt(e[j][j])
            r.append(rj)
            for i in range(j + 1, 8):
                l[i][j] = e[i][j] * rj
            for i in range(j + 1, 8):
                for k in range(j + 1, i + 1):
                    e[i][k] = e[i][k] - l[i][j] * l[k][j]
        y = []
        for i in range(8):
            yi = []
            for t in range(TW):
                v = lanes(rows[b][t][i : i + 1, :])
                for j in range(i):
                    v = v - l[i][j] * y[j][t]
                yi.append(v * r[i])
            y.append(yi)
        for t in range(TW):
            u = y[0][t]
            for i in range(1, 8):
                u = jnp.where(sub_iota == i, y[i][t], u)
            p_ref[8 * b : 8 * b + 8, LANES * t : LANES * (t + 1)] = u
        for g in range(b + 1, G8):
            cs = []
            for j in range(8):
                v = col[g - b][j]
                for k in range(j):
                    v = v - l[j][k] * cs[k]
                cs.append(v * r[j])
            for t in range(TW):
                v = rows[g][t]
                for j in range(8):
                    v = v - cs[j] * y[j][t]
                rows[g][t] = v


MESH = pl.DeviceIdType.MESH
CHUNKS = 16
LAG = 4
EARLY = 2
CODE = 32767.0
TINY = 1e-37
STEPS = PANELS * (B // SUB)


def factor_step(k, turn, s_ref, p_ref, u_ref, z_ref):
    factor_panel(s_ref, p_ref)
    start = pl.multiple_of(k * SUB, SUB)
    u_ref[pl.ds(start, SUB), :] = pltpu.roll(p_ref[:, :B], start, 1)
    z_ref[turn, pl.ds(start, SUB), :] = p_ref[:, B:]
    left = p_ref[:, :B]
    rolled = pltpu.roll(left, B - SUB, 1)
    lane = lax.broadcasted_iota(jnp.int32, (SUB, B), 1)
    rolled = jnp.where(lane < B - SUB, rolled, 0.0)
    upd_a = dot3(rolled, rolled, FIRST)
    upd_z = dot3(rolled, p_ref[:, B:], FIRST)
    keep = B - SUB
    old = pltpu.roll(s_ref[SUB:, :B], B - SUB, 1)
    lane2 = lax.broadcasted_iota(jnp.int32, (keep, B), 1)
    old = jnp.where(lane2 < keep, old, 0.0)
    old_z = s_ref[SUB:, B:]
    s_ref[:keep, :B] = old - upd_a[:keep]
    s_ref[:keep, B:] = old_z - upd_z[:keep]
    s_ref[keep:, :] = jnp.zeros((SUB, 2 * B), jnp.float32)


def remote(src, dst, send, recv, where):
    return pltpu.make_async_remote_copy(
        src_ref=src, dst_ref=dst, send_sem=send, recv_sem=recv, device_id=where, device_id_type=MESH
    )


def rows_at(start, count):
    return pl.ds(pl.multiple_of(start, count), count)


class Spread:
    def __init__(self, buf, out, hop, send, recv, base, size, bits):
        self.buf, self.out, self.hop, self.send, self.recv = buf, out, hop, send, recv
        self.stages = []
        start, hop_at = base, 0
        for axis, bit, whole in bits:
            me = lax.axis_index(axis)
            digit = lax.rem(me // bit, 2)
            where = {axis: me + bit - 2 * bit * digit}
            if whole:
                count, give = size, start
            else:
                count = size // 2
                give, start = start + (1 - digit) * count, start + digit * count
            self.stages.append((where, give, start, count, hop_at, whole))
            hop_at += count
            size = count
        self.last, self.size = start, size

    def down(self, i):
        where, give, keep, count, at, _ = self.stages[i]
        return remote(self.buf.at[rows_at(give, count)], self.hop.at[pl.ds(at, count)], self.send.at[i], self.recv.at[i], where)

    def up(self, i):
        where, give, keep, count, at, _ = self.stages[i]
        n = len(self.stages) + i
        rows = self.out.at[rows_at(keep, count)]
        return remote(rows, rows, self.send.at[n], self.recv.at[n], where)

    def add(self, i):
        self.down(i).wait()
        _, _, keep, count, at, _ = self.stages[i]
        rows = rows_at(keep, count)
        to = self.out if i == len(self.stages) - 1 else self.buf
        to[rows] = self.buf[rows] + self.hop[pl.ds(at, count)]

    def acts(self):
        count = len(self.stages)
        ends = [functools.partial(self.add, i) for i in range(count)]
        starts = [lambda i=i: self.down(i).start() for i in range(count)]
        for i in reversed(range(count)):
            if not self.stages[i][5]:
                starts.append(lambda i=i: self.up(i).start())
                ends.append(lambda i=i: self.up(i).wait())
        acts = [starts[0]]
        acts += [lambda a=a, b=b: (a(), b()) for a, b in zip(ends, starts[1:])]
        return acts + [ends[-1]]


def bits_of(axis, size, whole=False):
    return [(axis, 1 << b, whole) for b in range(size.bit_length() - 1)]


def spread_pair(buf, out, hop, send, recv, size, nr, after=()):
    bits = bits_of("row", nr)
    orders = [bits, bits[:1] + bits[:0:-1]]
    half = size // 2
    both = [
        Spread(buf, out, hop.at[part], send.at[part], recv.at[part], part * half, half, orders[part] + list(after)).acts()
        for part in range(2)
    ]
    return [lambda a=a, b=b: (a(), b()) for a, b in zip(*both)]


class Direct:
    def __init__(self, nr, nc, buf, out, land, crossland, sends, recvs):
        self.nr, self.nc = nr, nc
        self.buf, self.out, self.land, self.crossland = buf, out, land, crossland
        self.sends, self.recvs = sends, recvs
        self.r, self.c = lax.axis_index("row"), lax.axis_index("col")
        self.size = buf.shape[0] // nr
        self.mine = rows_at(self.r * self.size, self.size)

    def part(self, shift):
        return pl.ds((shift - 1) * self.size, self.size)

    def down(self, shift):
        to = lax.rem(self.r + shift, self.nr)
        return remote(
            self.buf.at[rows_at(to * self.size, self.size)], self.land.at[self.part(shift)],
            self.sends[0].at[shift], self.recvs[0].at[shift], {"row": to},
        )

    def over(self, shift):
        return remote(
            self.buf.at[self.mine], self.crossland.at[self.part(shift)],
            self.sends[1].at[shift], self.recvs[1].at[shift], {"col": lax.rem(self.c + shift, self.nc)},
        )

    def up(self, shift):
        rows = self.out.at[self.mine]
        return remote(rows, rows, self.sends[2].at[shift], self.recvs[2].at[shift], {"row": lax.rem(self.r + shift, self.nr)})

    def begin(self):
        for shift in range(1, self.nr):
            self.down(shift).start()

    def total(self, copy, count, land):
        for shift in range(1, count):
            copy(shift).wait()
        value = self.buf[self.mine]
        for shift in range(1, count):
            value = value + land[self.part(shift)]
        return value

    def cross(self):
        self.buf[self.mine] = self.total(self.down, self.nr, self.land)
        for shift in range(1, self.nc):
            self.over(shift).start()

    def crossed(self):
        self.out[self.mine] = self.total(self.over, self.nc, self.crossland)
        self.raise_all()

    def flat(self):
        self.out[self.mine] = self.total(self.down, self.nr, self.land)
        self.raise_all()

    def raise_all(self):
        for shift in range(1, self.nr):
            self.up(shift).start()

    def end(self):
        for shift in range(1, self.nr):
            self.up(shift).wait()


def direct_scratch(size, width, nr, nc):
    part = size // nr
    dma = pltpu.SemaphoreType.DMA
    return [
        pltpu.VMEM(((nr - 1) * part, width), jnp.float32),
        pltpu.VMEM(((nc - 1) * part, width), jnp.float32),
        dma((nr,)), dma((nc,)), dma((nr,)), dma((nr,)), dma((nc,)), dma((nr,)),
    ]


def spread_scratch(size, width, dtype, nr, nc=1):
    half, n, m = size // 2, nr.bit_length() - 1, nc.bit_length() - 1
    dma = pltpu.SemaphoreType.DMA
    return [pltpu.VMEM((2, half + m * (half // nr), width), dtype), dma((2, 2 * n + m)), dma((2, 2 * n + m))]


def choose(owner, wanted, value, otherwise):
    return jnp.where(jnp.full(value.shape, owner, jnp.int32) == wanted, value, otherwise)


def encode(x, top):
    part = jnp.sqrt(jnp.abs(x) * (1.0 / jnp.maximum(top, TINY)))
    code = (part * CODE + 0.5).astype(jnp.int32)
    return jnp.where(x < 0.0, -code, code).astype(jnp.int16)


def decode(code, top):
    part = code.astype(jnp.int32).astype(jnp.float32) * (1.0 / CODE)
    return part * jnp.abs(part) * top


def largest(x):
    top = jnp.max(jnp.abs(x), axis=0, keepdims=True)
    return jnp.max(top, axis=1, keepdims=True)


def front_kernel(
    nr, nc, own_ref, idx_ref, cov, inn,
    cols_o, tops_o, rowp_o, v_o, vs_o, f_o, z_o, x_o,
    w, wsem, vin, vinsem, outsem, zsem, fsem,
    cbuf, cols, rin, lin, rtx, ltx, rs, rr, ls, lr, tops, topland, topsend, toprecv, topsum,
    rbuf, rowp, rhop, rsend, rrecv,
    d0buf, d0, d0land, d0over, d0s0, d0s1, d0s2, d0r0, d0r1, d0r2,
    d1buf, d1, d1land, d1over, d1s0, d1s1, d1s2, d1r0, d1r1, d1r2,
    vsbuf, vs, vsland, vsover, vss0, vss1, vss2, vsr0, vsr1, vsr2,
    vt, vst, vq, v, vtop, vtst, vtq, v1send, v1recv, v2send, v2recv, t1send, t1recv, t2send, t2recv,
    a_ref, s_ref, p_ref, u_ref, f_ref, z_ref, x_ref, picks,
):
    r = lax.axis_index("row")
    c = lax.axis_index("col")
    rows, width = w.shape
    rb, cb = rows // B, width // B
    load = pltpu.make_async_copy(cov, w, wsem)
    vload = pltpu.make_async_copy(inn, vin, vinsem)
    vload.start()
    load.start()
    barrier = pltpu.get_barrier_semaphore()
    for shift in range(1, nr):
        pl.semaphore_signal(barrier, inc=1, device_id={"row": lax.rem(r + shift, nr)}, device_id_type=MESH)
    for shift in range(1, nc):
        pl.semaphore_signal(barrier, inc=1, device_id={"col": lax.rem(c + shift, nc)}, device_id_type=MESH)

    part_p, iw = inn.shape[0], inn.shape[2]
    ratio = nr // nc
    h = ratio * part_p

    def first_stop(shift):
        to = {"row": lax.rem(r + shift, nr)}
        return (
            remote(vt.at[lax.rem(r + shift, nr)], vst.at[rows_at(r * part_p, part_p)], v1send.at[shift], v1recv.at[shift], to),
            remote(vtop, vtst.at[rows_at(r * 8, 8)], t1send.at[shift], t1recv.at[shift], to),
        )

    def second_stop(shift):
        at = lax.rem(c + shift, nc)
        to = {"col": at}
        return (
            remote(vst.at[rows_at(at * h, h)], vq.at[:, rows_at(c * iw, iw)], v2send.at[shift], v2recv.at[shift], to),
            remote(
                vtst.at[rows_at(at * ratio * 8, ratio * 8)], vtq.at[rows_at(c * ratio * 8, ratio * 8)],
                t2send.at[shift], t2recv.at[shift], to,
            ),
        )

    def code_innovations():
        vload.wait()
        top = largest(vin[:, 0, :])
        for group in range(1, nr):
            top = jnp.maximum(top, largest(vin[:, group, :]))
        vtop[...] = jnp.broadcast_to(top, vtop.shape)
        for group in range(nr):
            vt[group] = encode(vin[:, group, :], top)

    g = idx_ref[0]
    d0buf[...] = jnp.zeros_like(d0buf)
    d1buf[...] = jnp.zeros_like(d1buf)
    zero = jnp.zeros((B, B), jnp.float32)

    @pl.when(c == 0)
    def _():
        rin[...] = jnp.zeros_like(rin)

    @pl.when(c == nc - 1)
    def _():
        lin[...] = jnp.zeros_like(lin)

    with jax.named_scope("load"):
        load.wait()

    def pick_cols(i, carry):
        span = rows_at(i * B, B)
        own = own_ref[r * rb + i]
        picked = []
        for t in range(PANELS):
            tile = zero
            for j in range(cb):
                tile = choose(own_ref[c * cb + j], g + t, w[span, j * B : (j + 1) * B], tile)
            picks[span, t * B : (t + 1) * B] = tile
            picked.append(tile)
        d0buf[...] = choose(own, g, picked[0], d0buf[...])
        d1buf[:B] = choose(own, g + 1, picked[0], d1buf[:B])
        d1buf[B:] = choose(own, g + 1, picked[1], d1buf[B:])
        return carry

    def code_cols(i, carry):
        span = rows_at(i * B, B)
        for t in range(PANELS):
            tile = picks[span, t * B : (t + 1) * B]
            top = largest(tile)
            tops[pl.ds(i * PANELS + t, 1), :] = jnp.broadcast_to(top, (1, LANES))
            cbuf[span, t * B : (t + 1) * B] = encode(tile, top)
        return carry

    with jax.named_scope("columns"):
        lax.fori_loop(0, rb, pick_cols, 0)
    first = Direct(nr, nc, d0buf, d0, d0land, d0over, (d0s0, d0s1, d0s2), (d0r0, d0r1, d0r2))
    second = Direct(nr, nc, d1buf, d1, d1land, d1over, (d1s0, d1s1, d1s2), (d1r0, d1r1, d1r2))
    with jax.named_scope("barrier"):
        pl.semaphore_wait(barrier, nr - 1 + nc - 1)
    first.begin()
    with jax.named_scope("code"):
        lax.fori_loop(0, rb, code_cols, 0)

    size = rows // CHUNKS

    def chunk(q):
        return rows_at(q * size, size)

    def right(src, q):
        return remote(src.at[chunk(q)], rin.at[chunk(q)], rs.at[q], rr.at[q], {"col": c + 1})

    def left(src, q):
        return remote(src.at[chunk(q)], lin.at[chunk(q)], ls.at[q], lr.at[q], {"col": c - 1})

    def push(begin, end):
        def one(q, carry):
            @pl.when(c == 0)
            def _():
                right(cbuf, q).start()

            @pl.when(c == nc - 1)
            def _():
                left(cbuf, q).start()

            return carry

        lax.fori_loop(begin, end, one, 0)

    def relay(t, carry):
        q = t - LAG * (c - 1)

        @pl.when((q >= 0) & (q < CHUNKS) & (c > 0))
        def _():
            right(cbuf, q).wait_recv()

            @pl.when(c < nc - 1)
            def _():
                rtx[chunk(q)] = rin[chunk(q)] + cbuf[chunk(q)]
                right(rtx, q).start()

        p = t - LAG * (nc - 2 - c)

        @pl.when((p >= 0) & (p < CHUNKS) & (c < nc - 1))
        def _():
            left(cbuf, p).wait_recv()

            @pl.when(c > 0)
            def _():
                ltx[chunk(p)] = lin[chunk(p)] + cbuf[chunk(p)]
                left(ltx, p).start()

        return carry

    def share_top(shift):
        count = tops.shape[0]
        return remote(
            tops, topland.at[pl.ds((shift - 1) * count, count)], topsend.at[shift], toprecv.at[shift],
            {"col": lax.rem(c + shift, nc)},
        )

    def fill_rows(i, carry):
        span = rows_at(i * B, B)
        for t in range(PANELS):
            tile = zero
            for k in range(rb):
                tile = choose(own_ref[r * rb + k], g + t, w[k * B : (k + 1) * B, span], tile)
            rbuf[t * B : (t + 1) * B, span] = tile.astype(jnp.bfloat16)
        return carry

    act_rows = spread_pair(rbuf, rowp, rhop, rsend, rrecv, PANELS * B, nr)

    def leave():
        for shift in range(1, nr):
            for copy in first_stop(shift):
                copy.start()
        vst[rows_at(r * part_p, part_p)] = vt[r]
        vtst[rows_at(r * 8, 8)] = vtop[...]
        for shift in range(1, nc):
            share_top(shift).start()

    def pass_on():
        for shift in range(1, nr):
            for copy in first_stop(shift):
                copy.wait()
        for shift in range(1, nc):
            for copy in second_stop(shift):
                copy.start()
        vq[:, rows_at(c * iw, iw)] = vst[rows_at(c * h, h)]
        vtq[rows_at(c * ratio * 8, ratio * 8)] = vtst[rows_at(c * ratio * 8, ratio * 8)]

    with jax.named_scope("first1"):
        push(0, 2)
        first.cross()
        second.begin()
    with jax.named_scope("rows"):
        lax.fori_loop(0, cb, fill_rows, 0)
        act_rows[0]()
    with jax.named_scope("innovations"):
        code_innovations()
    with jax.named_scope("first2"):
        first.crossed()
    with jax.named_scope("leave"):
        push(2, 4)
        leave()
    with jax.named_scope("second1"):
        second.cross()
    with jax.named_scope("early"):
        push(4, 8)
        lax.fori_loop(0, EARLY, relay, 0)
    with jax.named_scope("first3"):
        first.end()
        push(8, CHUNKS)

    outs = [
        pltpu.make_async_copy(src, dst, outsem.at[i])
        for i, (src, dst) in enumerate(
            [(rowp, rowp_o), (v, v_o), (vs, vs_o), (x_ref, x_o), (cols, cols_o), (topsum, tops_o)]
        )
    ]
    heads = Direct(nr, nc, vsbuf, vs, vsland, vsover, (vss0, vss1, vss2), (vsr0, vsr1, vsr2))

    def arrived():
        for shift in range(1, nc):
            for copy in second_stop(shift):
                copy.wait()
        for b in range(nc):
            for a in range(ratio):
                at, block = slice(a * part_p, (a + 1) * part_p), slice(b * iw, (b + 1) * iw)
                n = (b * ratio + a) * 8
                v[at, block] = decode(vq[at, block], vtq[n : n + 1, :1])
        outs[1].start()
        for t in range(PANELS):
            part = jnp.zeros((h, B), jnp.float32)
            for k in range(rb):
                part = choose(own_ref[r * rb + k], g + t, v[:, k * B : (k + 1) * B], part)
            vsbuf[t * h : (t + 1) * h] = part
        heads.begin()

    events = [[] for _ in range(STEPS)]
    half = STEPS // PANELS
    events[0].append(act_rows[1])
    events[1].append(second.crossed)
    events[2].append(pass_on)
    events[3].append(second.end)
    later = act_rows[2:-1]
    for i, act in enumerate(later):
        events[3 + i * (STEPS - 3) // len(later)].append(act)
    events[half + 1].append(arrived)
    events[half + 3].append(heads.flat)
    total = CHUNKS + LAG * (nc - 2)
    each = -(-(total - EARLY) // STEPS)
    row_i = lax.broadcasted_iota(jnp.int32, (B, B), 0)
    col_i = lax.broadcasted_iota(jnp.int32, (B, B), 1)
    a_ref[...] = d0[...]

    def panel(turn, carry):
        s_ref[:, :B] = a_ref[...]
        s_ref[:, B:] = jnp.where(row_i == col_i, 1.0, 0.0)

        def step(k, carry):
            now = turn * (B // SUB) + k
            with jax.named_scope("factor"):
                factor_step(k, turn, s_ref, p_ref, u_ref, z_ref)
            at = EARLY + now * each
            with jax.named_scope("relay"):
                lax.fori_loop(at, at + each, relay, 0)
            for i, acts in enumerate(events):
                if acts:
                    @pl.when(now == i)
                    def _():
                        for m, act in enumerate(acts):
                            with jax.named_scope(f"event{i}_{m}"):
                                act()
            return carry

        lax.fori_loop(0, B // SUB, step, 0)
        z_ref[turn] = jnp.where(row_i >= col_i, z_ref[turn], 0.0)
        f_ref[turn] = jnp.where(row_i >= col_i, u_ref[...].T, 0.0)
        pltpu.make_async_copy(z_ref.at[turn], z_o.at[turn], zsem.at[turn]).start()
        pltpu.make_async_copy(f_ref.at[turn], f_o.at[turn], fsem.at[turn]).start()

        @pl.when(turn == 0)
        def _():
            low = dot3(d1[:B], z_ref[0], LAST)
            half = low.astype(jnp.bfloat16)
            x_ref[...] = half
            a_ref[...] = d1[B:] - dot(half, half, LAST)

        return carry

    lax.fori_loop(0, PANELS, panel, 0)
    outs[3].start()
    with jax.named_scope("rowend"):
        act_rows[-1]()
        outs[0].start()
    with jax.named_scope("headend"):
        heads.end()
        outs[2].start()

    with jax.named_scope("sum"):
        def add(q, carry):
            cols[chunk(q)] = cbuf[chunk(q)] + (rin[chunk(q)] + lin[chunk(q)])
            return carry

        lax.fori_loop(0, CHUNKS, add, 0)
        outs[4].start()
        count = tops.shape[0]
        top = tops[...]
        for shift in range(1, nc):
            share_top(shift).wait()
            top = top + topland[pl.ds((shift - 1) * count, count)]
        topsum[...] = top
        outs[5].start()

    with jax.named_scope("sent"):
        @pl.when(c < nc - 1)
        def _():
            lax.fori_loop(0, CHUNKS, lambda q, k: (right(cbuf, q).wait_send(), k)[1], 0)

        @pl.when(c > 0)
        def _():
            lax.fori_loop(0, CHUNKS, lambda q, k: (left(cbuf, q).wait_send(), k)[1], 0)

    with jax.named_scope("written"):
        for turn in range(PANELS):
            pltpu.make_async_copy(z_ref.at[turn], z_o.at[turn], zsem.at[turn]).wait()
            pltpu.make_async_copy(f_ref.at[turn], f_o.at[turn], fsem.at[turn]).wait()
        for out in outs:
            out.wait()


def front(nr, nc, owner, index, cov, inn):
    rows, width = cov.shape
    part_p, groups, iw = inn.shape
    ratio = nr // nc
    h = ratio * part_p
    f32, bf16, i16 = jnp.float32, jnp.bfloat16, jnp.int16
    smem = pl.BlockSpec(memory_space=pltpu.SMEM)
    anywhere = pl.BlockSpec(memory_space=pl.ANY)
    vmem = pltpu.VMEM
    dma = pltpu.SemaphoreType.DMA
    both = PANELS * B
    count = PANELS * (rows // B)
    scratch = [vmem((rows, width), f32), dma, vmem(inn.shape, f32), dma, dma((6,)), dma((PANELS,)), dma((PANELS,))]
    scratch += [vmem((rows, both), i16)] * 6 + [dma((CHUNKS,))] * 4
    scratch += [vmem((count, LANES), f32), vmem(((nc - 1) * count, LANES), f32), dma((nc,)), dma((nc,)), vmem((count, LANES), f32)]
    scratch += [vmem((both, width), bf16)] * 2 + spread_scratch(both, width, bf16, nr)
    scratch += [vmem((B, B), f32)] * 2 + direct_scratch(B, B, nr, nc)
    scratch += [vmem((2 * B, B), f32)] * 2 + direct_scratch(2 * B, B, nr, nc)
    scratch += [vmem((PANELS * h, B), f32)] * 2 + direct_scratch(PANELS * h, B, nr, nc)
    scratch += [vmem((groups, part_p, iw), i16), vmem((nr * part_p, iw), i16), vmem((h, nc * iw), i16), vmem((h, nc * iw), f32)]
    scratch += [vmem((8, LANES), f32), vmem((nr * 8, LANES), f32), vmem((nr * 8, LANES), f32)]
    scratch += [dma((nr,)), dma((nr,)), dma((nc,)), dma((nc,))] * 2
    scratch += [vmem((B, B), f32), vmem((B, 2 * B), f32), vmem((SUB, 2 * B), f32), vmem((B, B), f32)]
    scratch += [vmem((PANELS, B, B), f32)] * 2 + [vmem((B, B), bf16), vmem((rows, both), f32)]
    return pl.pallas_call(
        functools.partial(front_kernel, nr, nc),
        out_shape=(
            jax.ShapeDtypeStruct((rows, both), i16),
            jax.ShapeDtypeStruct((count, LANES), f32),
            jax.ShapeDtypeStruct((both, width), bf16),
            jax.ShapeDtypeStruct((h, nc * iw), f32),
            jax.ShapeDtypeStruct((PANELS * h, B), f32),
            jax.ShapeDtypeStruct((PANELS, B, B), f32),
            jax.ShapeDtypeStruct((PANELS, B, B), f32),
            jax.ShapeDtypeStruct((B, B), bf16),
        ),
        in_specs=[smem, smem, anywhere, anywhere],
        out_specs=(anywhere,) * 8,
        scratch_shapes=scratch,
        compiler_params=pltpu.CompilerParams(
            collective_id=0, has_side_effects=True, vmem_limit_bytes=56 * 1024 * 1024
        ),
    )(owner, index, cov, inn)


def tail_kernel(
    own_ref, idx_ref, w_ref, cols_ref, tops_ref, rowp_ref, f_ref, z_ref, x_ref, vs_ref, v_ref,
    o_ref, vout_ref, q_ref, half_ref, *, rb, cb,
):
    j = pl.program_id(0)
    g = idx_ref[0]
    row0 = lax.axis_index("row") * rb
    col0 = lax.axis_index("col") * cb

    @pl.when(j == 0)
    def _():
        h = v_ref.shape[0]
        x = x_ref[...]
        zh, zl = split_bf16(z_ref[0])
        for k in range(cb):
            span = slice(k * B, (k + 1) * B)
            own = own_ref[col0 + k]
            q0 = dot(zh, rowp_ref[:B, span]) + dot(zl, rowp_ref[:B, span])
            q0 = jnp.where(own > g, q0, 0.0).astype(jnp.bfloat16)
            r1 = rowp_ref[B:, span].astype(jnp.float32) - dot(x, q0)
            q1 = dot3(z_ref[1], r1)
            q_ref[:B, span] = q0
            q_ref[B:, span] = jnp.where(own > g + 1, q1, 0.0).astype(jnp.bfloat16)
        for i in range(rb):
            span = slice(i * B, (i + 1) * B)
            own = own_ref[row0 + i]
            c0 = decode(cols_ref[span, :B], tops_ref[PANELS * i : PANELS * i + 1, :1])
            p0 = dot3(c0, z_ref[0], LAST)
            h0 = jnp.where(own > g, p0, 0.0).astype(jnp.bfloat16)
            c1 = decode(cols_ref[span, B:], tops_ref[PANELS * i + 1 : PANELS * i + 2, :1]) - dot(h0, x, LAST)
            p1 = dot3(c1, z_ref[1], LAST)
            half_ref[span, :B] = h0
            half_ref[span, B:] = jnp.where(own > g + 1, p1, 0.0).astype(jnp.bfloat16)
        w0 = dot(vs_ref[:h], z_ref[0], LAST, HIGHEST)
        w0h = w0.astype(jnp.bfloat16)
        w1 = dot(vs_ref[h:] - dot(w0h, x, LAST), z_ref[1], LAST, HIGHEST)
        w1h = w1.astype(jnp.bfloat16)
        for i in range(rb):
            span = slice(i * B, (i + 1) * B)
            own = own_ref[row0 + i]
            new = v_ref[:, span] - (dot(w0h, half_ref[span, :B], LAST) + dot(w1h, half_ref[span, B:], LAST))
            new = jnp.where(own == g, w0, new)
            vout_ref[:, span] = jnp.where(own == g + 1, w1, new)

    cown = own_ref[col0 + j]
    start = pl.multiple_of(j * B, B)
    o_ref[...] = w_ref[...] - dot(half_ref[...], q_ref[:, pl.ds(start, B)])

    @pl.when(cown > g)
    def _():
        for i in range(rb):
            rown = own_ref[row0 + i]

            @pl.when((rown == g) | ((rown == g + 1) & (cown > g + 1)))
            def _():
                o_ref[i * B : (i + 1) * B] = jnp.zeros((B, B), jnp.float32)

    for turn in range(PANELS):
        @pl.when(cown == g + turn)
        def _():
            for i in range(rb):
                span = slice(i * B, (i + 1) * B)
                rown = own_ref[row0 + i]

                @pl.when(rown > g + turn)
                def _():
                    left = w_ref[span]
                    if turn:
                        left = left - dot(half_ref[span, :B], x_ref[...], LAST)
                    o_ref[span] = dot3(left, z_ref[turn], LAST)

                @pl.when(rown == g + turn)
                def _():
                    o_ref[span] = f_ref[turn]


def tail(owner, index, w, cols, tops, rowp, factors, z, x, vs, v):
    rows, width = w.shape
    stripe = lambda j, a, b: (0, j)
    whole = lambda x: pl.BlockSpec(x.shape, lambda j, a, b: (0,) * x.ndim)
    return pl.pallas_call(
        functools.partial(tail_kernel, rb=rows // B, cb=width // B),
        grid_spec=pltpu.PrefetchScalarGridSpec(
            num_scalar_prefetch=2,
            grid=(width // B,),
            in_specs=[
                pl.BlockSpec((rows, B), stripe),
                whole(cols),
                whole(tops),
                whole(rowp),
                whole(factors),
                whole(z),
                whole(x),
                whole(vs),
                whole(v),
            ],
            out_specs=[pl.BlockSpec((rows, B), stripe), whole(v)],
            scratch_shapes=[
                pltpu.VMEM((2 * B, width), jnp.bfloat16),
                pltpu.VMEM((rows, 2 * B), jnp.bfloat16),
            ],
        ),
        out_shape=(jax.ShapeDtypeStruct(w.shape, w.dtype), jax.ShapeDtypeStruct(v.shape, v.dtype)),
    )(owner, index, w, cols, tops, rowp, factors, z, x, vs, v)


def per_device(covariance, innovations, block_owner, panel_index):
    nr, nc = lax.axis_size("row"), lax.axis_size("col")
    cols, tops, rowp, v, vs, factors, z, x = front(nr, nc, block_owner, panel_index, covariance, innovations)
    return tail(block_owner, panel_index, covariance, cols, tops, rowp, factors, z, x, vs, v)


def solution(mesh):
    placed = (P("row", "col"), P("row", None, "col"), P(), P())
    return jax.shard_map(
        per_device,
        mesh=mesh,
        in_specs=placed,
        out_specs=(P("row", "col"), P("col", "row")),
        check_vma=False,
    )
```

```python
import functools

import jax
import jax.numpy as jnp
from jax import lax
from jax.experimental import pallas as pl
from jax.experimental.pallas import tpu as pltpu
from jax.sharding import PartitionSpec as P

B = 256
PANELS = 2
SUB = 64
G8 = SUB // 8
LANES = 128
TW = 2 * B // LANES
HIGHEST = lax.Precision.HIGHEST

LAST = (((1,), (1,)), ((), ()))
FIRST = (((0,), (0,)), ((), ()))
PLAIN = (((1,), (0,)), ((), ()))


def dot(a, b, dims=PLAIN, precision=None):
    return lax.dot_general(a, b, dims, precision=precision, preferred_element_type=jnp.float32)


def split_bf16(x):
    hi = x.astype(jnp.bfloat16)
    lo = (x - hi.astype(jnp.float32)).astype(jnp.bfloat16)
    return hi, lo


def dot3(a, b, dims=PLAIN):
    ah, al = split_bf16(a)
    bh, bl = split_bf16(b)
    return dot(ah, bh, dims) + (dot(ah, bl, dims) + dot(al, bh, dims))


def lanes(x):
    return jnp.broadcast_to(x, (8, LANES))


def factor_panel(s_ref, p_ref):
    sub_iota = lax.broadcasted_iota(jnp.int32, (8, LANES), 0)
    rows = [[s_ref[8 * g : 8 * g + 8, LANES * t : LANES * (t + 1)] for t in range(TW)] for g in range(G8)]
    for b in range(G8):
        c0 = 8 * b
        col = [[lanes(rows[g][0][:, c0 + j : c0 + j + 1]) for j in range(8)] for g in range(b, G8)]
        e = [[lanes(col[0][j][i : i + 1, :]) for j in range(i + 1)] for i in range(8)]
        r = []
        l = [[None] * 8 for _ in range(8)]
        for j in range(8):
            rj = lax.rsqrt(e[j][j])
            r.append(rj)
            for i in range(j + 1, 8):
                l[i][j] = e[i][j] * rj
            for i in range(j + 1, 8):
                for k in range(j + 1, i + 1):
                    e[i][k] = e[i][k] - l[i][j] * l[k][j]
        y = []
        for i in range(8):
            yi = []
            for t in range(TW):
                v = lanes(rows[b][t][i : i + 1, :])
                for j in range(i):
                    v = v - l[i][j] * y[j][t]
                yi.append(v * r[i])
            y.append(yi)
        for t in range(TW):
            u = y[0][t]
            for i in range(1, 8):
                u = jnp.where(sub_iota == i, y[i][t], u)
            p_ref[8 * b : 8 * b + 8, LANES * t : LANES * (t + 1)] = u
        for g in range(b + 1, G8):
            cs = []
            for j in range(8):
                v = col[g - b][j]
                for k in range(j):
                    v = v - l[j][k] * cs[k]
                cs.append(v * r[j])
            for t in range(TW):
                v = rows[g][t]
                for j in range(8):
                    v = v - cs[j] * y[j][t]
                rows[g][t] = v


MESH = pl.DeviceIdType.MESH
CHUNKS = 16
LAG = 4
CODE = 32767.0
TINY = 1e-37
STEPS = PANELS * (B // SUB)


def factor_step(k, turn, s_ref, p_ref, u_ref, z_ref):
    factor_panel(s_ref, p_ref)
    start = pl.multiple_of(k * SUB, SUB)
    u_ref[pl.ds(start, SUB), :] = pltpu.roll(p_ref[:, :B], start, 1)
    z_ref[turn, pl.ds(start, SUB), :] = p_ref[:, B:]
    left = p_ref[:, :B]
    rolled = pltpu.roll(left, B - SUB, 1)
    lane = lax.broadcasted_iota(jnp.int32, (SUB, B), 1)
    rolled = jnp.where(lane < B - SUB, rolled, 0.0)
    upd_a = dot3(rolled, rolled, FIRST)
    upd_z = dot3(rolled, p_ref[:, B:], FIRST)
    keep = B - SUB
    old = pltpu.roll(s_ref[SUB:, :B], B - SUB, 1)
    lane2 = lax.broadcasted_iota(jnp.int32, (keep, B), 1)
    old = jnp.where(lane2 < keep, old, 0.0)
    old_z = s_ref[SUB:, B:]
    s_ref[:keep, :B] = old - upd_a[:keep]
    s_ref[:keep, B:] = old_z - upd_z[:keep]
    s_ref[keep:, :] = jnp.zeros((SUB, 2 * B), jnp.float32)


def remote(src, dst, send, recv, where):
    return pltpu.make_async_remote_copy(
        src_ref=src, dst_ref=dst, send_sem=send, recv_sem=recv, device_id=where, device_id_type=MESH
    )


def rows_at(start, count):
    return pl.ds(pl.multiple_of(start, count), count)


class Spread:
    def __init__(self, buf, out, hop, send, recv, base, size, bits, cross=None):
        self.buf, self.out, self.hop, self.send, self.recv = buf, out, hop, send, recv
        self.cross = cross
        self.stages = []
        start, hop_at = base, 0
        for axis, bit, whole in bits:
            me = lax.axis_index(axis)
            digit = lax.rem(me // bit, 2)
            where = {axis: me + bit - 2 * bit * digit}
            if whole:
                count, give = size, start
            else:
                count = size // 2
                give, start = start + (1 - digit) * count, start + digit * count
            self.stages.append((where, give, start, count, hop_at, whole))
            hop_at += count
            size = count
        self.last, self.size = start, size

    def down(self, i):
        where, give, keep, count, at, _ = self.stages[i]
        return remote(self.buf.at[rows_at(give, count)], self.hop.at[pl.ds(at, count)], self.send.at[i], self.recv.at[i], where)

    def up(self, i):
        where, give, keep, count, at, _ = self.stages[i]
        n = len(self.stages) + i
        rows = self.out.at[rows_at(keep, count)]
        return remote(rows, rows, self.send.at[n], self.recv.at[n], where)

    def add(self, i):
        self.down(i).wait()
        _, _, keep, count, at, _ = self.stages[i]
        rows = rows_at(keep, count)
        to = self.out if i == len(self.stages) - 1 and self.cross is None else self.buf
        to[rows] = self.buf[rows] + self.hop[pl.ds(at, count)]

    def over(self, shift):
        land, send, recv, nc = self.cross
        to = lax.rem(lax.axis_index("col") + shift, nc)
        part = pl.ds((shift - 1) * self.size, self.size)
        return remote(
            self.buf.at[rows_at(self.last, self.size)], land.at[part], send.at[shift], recv.at[shift], {"col": to}
        )

    def send_over(self):
        for shift in range(1, self.cross[3]):
            self.over(shift).start()

    def add_over(self):
        rows = rows_at(self.last, self.size)
        total = self.buf[rows]
        for shift in range(1, self.cross[3]):
            self.over(shift).wait()
            total = total + self.cross[0][pl.ds((shift - 1) * self.size, self.size)]
        self.out[rows] = total

    def acts(self):
        count = len(self.stages)
        ends = [functools.partial(self.add, i) for i in range(count)]
        starts = [lambda i=i: self.down(i).start() for i in range(count)]
        if self.cross is not None:
            starts.append(self.send_over)
            ends.append(self.add_over)
        for i in reversed(range(count)):
            if not self.stages[i][5]:
                starts.append(lambda i=i: self.up(i).start())
                ends.append(lambda i=i: self.up(i).wait())
        acts = [starts[0]]
        acts += [lambda a=a, b=b: (a(), b()) for a, b in zip(ends, starts[1:])]
        return acts + [ends[-1]]


def bits_of(axis, size, whole=False):
    return [(axis, 1 << b, whole) for b in range(size.bit_length() - 1)]


def spread_pair(buf, out, hop, send, recv, size, nr, cross=None):
    bits = bits_of("row", nr)
    orders = [bits, bits[:1] + bits[:0:-1]]
    half = size // 2
    both = []
    for part in range(2):
        over = None if cross is None else tuple(ref.at[part] for ref in cross[:3]) + (cross[3],)
        both.append(
            Spread(buf, out, hop.at[part], send.at[part], recv.at[part], part * half, half, orders[part], over).acts()
        )
    return [lambda a=a, b=b: (a(), b()) for a, b in zip(*both)]


class Direct:
    def __init__(self, nr, nc, buf, out, land, crossland, sends, recvs):
        self.nr, self.nc = nr, nc
        self.buf, self.out, self.land, self.crossland = buf, out, land, crossland
        self.sends, self.recvs = sends, recvs
        self.r, self.c = lax.axis_index("row"), lax.axis_index("col")
        self.size = buf.shape[0] // nr
        self.mine = rows_at(self.r * self.size, self.size)

    def part(self, shift):
        return pl.ds((shift - 1) * self.size, self.size)

    def down(self, shift):
        to = lax.rem(self.r + shift, self.nr)
        return remote(
            self.buf.at[rows_at(to * self.size, self.size)], self.land.at[self.part(shift)],
            self.sends[0].at[shift], self.recvs[0].at[shift], {"row": to},
        )

    def over(self, shift):
        return remote(
            self.buf.at[self.mine], self.crossland.at[self.part(shift)],
            self.sends[1].at[shift], self.recvs[1].at[shift], {"col": lax.rem(self.c + shift, self.nc)},
        )

    def up(self, shift):
        rows = self.out.at[self.mine]
        return remote(rows, rows, self.sends[2].at[shift], self.recvs[2].at[shift], {"row": lax.rem(self.r + shift, self.nr)})

    def begin(self):
        for shift in range(1, self.nr):
            self.down(shift).start()

    def total(self, copy, count, land):
        for shift in range(1, count):
            copy(shift).wait()
        value = self.buf[self.mine]
        for shift in range(1, count):
            value = value + land[self.part(shift)]
        return value

    def cross(self):
        self.buf[self.mine] = self.total(self.down, self.nr, self.land)
        for shift in range(1, self.nc):
            self.over(shift).start()

    def crossed(self):
        self.out[self.mine] = self.total(self.over, self.nc, self.crossland)
        self.raise_all()

    def flat(self):
        self.out[self.mine] = self.total(self.down, self.nr, self.land)
        self.raise_all()

    def raise_all(self):
        for shift in range(1, self.nr):
            self.up(shift).start()

    def end(self):
        for shift in range(1, self.nr):
            self.up(shift).wait()


def direct_scratch(size, width, nr, nc):
    part = size // nr
    dma = pltpu.SemaphoreType.DMA
    return [
        pltpu.VMEM(((nr - 1) * part, width), jnp.float32),
        pltpu.VMEM(((nc - 1) * part, width), jnp.float32),
        dma((nr,)), dma((nc,)), dma((nr,)), dma((nr,)), dma((nc,)), dma((nr,)),
    ]


def spread_scratch(size, width, dtype, nr, nc=None):
    half, n = size // 2, nr.bit_length() - 1
    dma = pltpu.SemaphoreType.DMA
    out = [pltpu.VMEM((2, half, width), dtype), dma((2, 2 * n)), dma((2, 2 * n))]
    if nc is not None:
        out += [pltpu.VMEM((2, (nc - 1) * (half // nr), width), dtype), dma((2, nc)), dma((2, nc))]
    return out


def choose(owner, wanted, value, otherwise):
    return jnp.where(jnp.full(value.shape, owner, jnp.int32) == wanted, value, otherwise)


def encode(x, top):
    part = jnp.sqrt(jnp.abs(x) * (1.0 / jnp.maximum(top, TINY)))
    code = (part * CODE + 0.5).astype(jnp.int32)
    return jnp.where(x < 0.0, -code, code).astype(jnp.int16)


def decode(code, top):
    part = code.astype(jnp.int32).astype(jnp.float32) * (1.0 / CODE)
    return part * jnp.abs(part) * top


def largest(x):
    top = jnp.max(jnp.abs(x), axis=0, keepdims=True)
    return jnp.max(top, axis=1, keepdims=True)


def front_kernel(
    nr, nc, own_ref, idx_ref, cov, inn,
    cols_o, tops_o, rowp_o, v_o, vs_o, f_o, z_o, x_o,
    w, wsem, vin, vinsem, outsem, zsem, fsem,
    cbuf, cols, rin, lin, rtx, ltx, rs, rr, ls, lr, tops, topland, topsend, toprecv, topsum,
    rbuf, rowp, rhop, rsend, rrecv,
    d0buf, d0, d0land, d0over, d0s0, d0s1, d0s2, d0r0, d0r1, d0r2,
    d1buf, d1, d1hop, d1send, d1recv, d1over, d1s, d1r,
    vsbuf, vs, vsland, vsover, vss0, vss1, vss2, vsr0, vsr1, vsr2,
    vt, vst, vq, v, vtop, vtst, vtq, v1send, v1recv, v2send, v2recv, t1send, t1recv, t2send, t2recv,
    a_ref, s_ref, p_ref, u_ref, f_ref, z_ref, x_ref, picks,
):
    r = lax.axis_index("row")
    c = lax.axis_index("col")
    rows, width = w.shape
    rb, cb = rows // B, width // B
    load = pltpu.make_async_copy(cov, w, wsem)
    vload = pltpu.make_async_copy(inn, vin, vinsem)
    vload.start()
    load.start()
    barrier = pltpu.get_barrier_semaphore()
    for shift in range(1, nr):
        pl.semaphore_signal(barrier, inc=1, device_id={"row": lax.rem(r + shift, nr)}, device_id_type=MESH)
    for shift in range(1, nc):
        pl.semaphore_signal(barrier, inc=1, device_id={"col": lax.rem(c + shift, nc)}, device_id_type=MESH)

    part_p, iw = inn.shape[0], inn.shape[2]
    ratio = nr // nc
    h = ratio * part_p

    def first_stop(shift):
        to = {"row": lax.rem(r + shift, nr)}
        return (
            remote(vt.at[lax.rem(r + shift, nr)], vst.at[rows_at(r * part_p, part_p)], v1send.at[shift], v1recv.at[shift], to),
            remote(vtop, vtst.at[rows_at(r * 8, 8)], t1send.at[shift], t1recv.at[shift], to),
        )

    def second_stop(shift):
        at = lax.rem(c + shift, nc)
        to = {"col": at}
        return (
            remote(vst.at[rows_at(at * h, h)], vq.at[:, rows_at(c * iw, iw)], v2send.at[shift], v2recv.at[shift], to),
            remote(
                vtst.at[rows_at(at * ratio * 8, ratio * 8)], vtq.at[rows_at(c * ratio * 8, ratio * 8)],
                t2send.at[shift], t2recv.at[shift], to,
            ),
        )

    def code_innovations():
        vload.wait()
        top = largest(vin[:, 0, :])
        for group in range(1, nr):
            top = jnp.maximum(top, largest(vin[:, group, :]))
        vtop[...] = jnp.broadcast_to(top, vtop.shape)
        for group in range(nr):
            vt[group] = encode(vin[:, group, :], top)

    g = idx_ref[0]
    d0buf[...] = jnp.zeros_like(d0buf)
    d1buf[...] = jnp.zeros_like(d1buf)
    zero = jnp.zeros((B, B), jnp.float32)

    @pl.when(c == 0)
    def _():
        rin[...] = jnp.zeros_like(rin)

    @pl.when(c == nc - 1)
    def _():
        lin[...] = jnp.zeros_like(lin)

    with jax.named_scope("load"):
        load.wait()

    def pick_cols(i, carry):
        span = rows_at(i * B, B)
        own = own_ref[r * rb + i]
        picked = []
        for t in range(PANELS):
            tile = zero
            for j in range(cb):
                tile = choose(own_ref[c * cb + j], g + t, w[span, j * B : (j + 1) * B], tile)
            picks[span, t * B : (t + 1) * B] = tile
            picked.append(tile)
        d0buf[...] = choose(own, g, picked[0], d0buf[...])
        d1buf[:B] = choose(own, g + 1, picked[0], d1buf[:B])
        d1buf[B:] = choose(own, g + 1, picked[1], d1buf[B:])
        return carry

    def code_cols(i, carry):
        span = rows_at(i * B, B)
        for t in range(PANELS):
            tile = picks[span, t * B : (t + 1) * B]
            top = largest(tile)
            tops[pl.ds(i * PANELS + t, 1), :] = jnp.broadcast_to(top, (1, LANES))
            cbuf[span, t * B : (t + 1) * B] = encode(tile, top)
        return carry

    with jax.named_scope("columns"):
        lax.fori_loop(0, rb, pick_cols, 0)
    first = Direct(nr, nc, d0buf, d0, d0land, d0over, (d0s0, d0s1, d0s2), (d0r0, d0r1, d0r2))
    second = spread_pair(d1buf, d1, d1hop, d1send, d1recv, 2 * B, nr, (d1over, d1s, d1r, nc))
    with jax.named_scope("barrier"):
        pl.semaphore_wait(barrier, nr - 1 + nc - 1)
    first.begin()
    second[0]()
    with jax.named_scope("code"):
        lax.fori_loop(0, rb, code_cols, 0)

    size = rows // CHUNKS

    def chunk(q):
        return rows_at(q * size, size)

    def right(src, q):
        return remote(src.at[chunk(q)], rin.at[chunk(q)], rs.at[q], rr.at[q], {"col": c + 1})

    def left(src, q):
        return remote(src.at[chunk(q)], lin.at[chunk(q)], ls.at[q], lr.at[q], {"col": c - 1})

    def push(begin, end):
        def one(q, carry):
            @pl.when(c == 0)
            def _():
                right(cbuf, q).start()

            @pl.when(c == nc - 1)
            def _():
                left(cbuf, q).start()

            return carry

        lax.fori_loop(begin, end, one, 0)

    def relay(t, carry):
        q = t - LAG * (c - 1)

        @pl.when((q >= 0) & (q < CHUNKS) & (c > 0))
        def _():
            right(cbuf, q).wait_recv()

            @pl.when(c < nc - 1)
            def _():
                rtx[chunk(q)] = rin[chunk(q)] + cbuf[chunk(q)]
                right(rtx, q).start()

        p = t - LAG * (nc - 2 - c)

        @pl.when((p >= 0) & (p < CHUNKS) & (c < nc - 1))
        def _():
            left(cbuf, p).wait_recv()

            @pl.when(c > 0)
            def _():
                ltx[chunk(p)] = lin[chunk(p)] + cbuf[chunk(p)]
                left(ltx, p).start()

        return carry

    def share_top(shift):
        count = tops.shape[0]
        return remote(
            tops, topland.at[pl.ds((shift - 1) * count, count)], topsend.at[shift], toprecv.at[shift],
            {"col": lax.rem(c + shift, nc)},
        )

    def fill_rows(i, carry):
        span = rows_at(i * B, B)
        for t in range(PANELS):
            tile = zero
            for k in range(rb):
                tile = choose(own_ref[r * rb + k], g + t, w[k * B : (k + 1) * B, span], tile)
            rbuf[t * B : (t + 1) * B, span] = tile.astype(jnp.bfloat16)
        return carry

    act_rows = spread_pair(rbuf, rowp, rhop, rsend, rrecv, PANELS * B, nr)

    def leave():
        for shift in range(1, nr):
            for copy in first_stop(shift):
                copy.start()
        vst[rows_at(r * part_p, part_p)] = vt[r]
        vtst[rows_at(r * 8, 8)] = vtop[...]
        for shift in range(1, nc):
            share_top(shift).start()

    def pass_on():
        for shift in range(1, nr):
            for copy in first_stop(shift):
                copy.wait()
        for shift in range(1, nc):
            for copy in second_stop(shift):
                copy.start()
        vq[:, rows_at(c * iw, iw)] = vst[rows_at(c * h, h)]
        vtq[rows_at(c * ratio * 8, ratio * 8)] = vtst[rows_at(c * ratio * 8, ratio * 8)]

    early = 0

    def relays(count):
        nonlocal early
        lax.fori_loop(early, early + count, relay, 0)
        early += count

    with jax.named_scope("first1"):
        push(0, 2)
        first.cross()
        second[1]()
    with jax.named_scope("innovations"):
        code_innovations()
        push(2, 4)
    with jax.named_scope("rows"):
        lax.fori_loop(0, cb, fill_rows, 0)
        act_rows[0]()
    with jax.named_scope("early1"):
        relays(2)
        second[2]()
    with jax.named_scope("first2"):
        first.crossed()
        push(4, 6)
    with jax.named_scope("second1"):
        second[3]()
        leave()
        push(6, 9)
    with jax.named_scope("early2"):
        relays(2)
    with jax.named_scope("first3"):
        first.end()
    with jax.named_scope("early3"):
        act_rows[1]()
        push(9, CHUNKS)
        relays(1)

    outs = [
        pltpu.make_async_copy(src, dst, outsem.at[i])
        for i, (src, dst) in enumerate(
            [(rowp, rowp_o), (v, v_o), (vs, vs_o), (x_ref, x_o), (cols, cols_o), (topsum, tops_o)]
        )
    ]
    heads = Direct(nr, nc, vsbuf, vs, vsland, vsover, (vss0, vss1, vss2), (vsr0, vsr1, vsr2))

    def arrived():
        for shift in range(1, nc):
            for copy in second_stop(shift):
                copy.wait()
        for b in range(nc):
            for a in range(ratio):
                at, block = slice(a * part_p, (a + 1) * part_p), slice(b * iw, (b + 1) * iw)
                n = (b * ratio + a) * 8
                v[at, block] = decode(vq[at, block], vtq[n : n + 1, :1])
        outs[1].start()
        for t in range(PANELS):
            part = jnp.zeros((h, B), jnp.float32)
            for k in range(rb):
                part = choose(own_ref[r * rb + k], g + t, v[:, k * B : (k + 1) * B], part)
            vsbuf[t * h : (t + 1) * h] = part
        heads.begin()

    events = [[] for _ in range(STEPS)]
    half = STEPS // PANELS
    later = second[4:]
    for i, act in enumerate(later):
        events[i * half // len(later)].append(act)
    events[1].append(pass_on)
    later = act_rows[2:-1]
    for i, act in enumerate(later):
        events[2 + i * (STEPS - 2) // len(later)].append(act)
    events[half + 1].append(arrived)
    events[half + 3].append(heads.flat)
    total = CHUNKS + LAG * (nc - 2)
    each = min(2, -(-(total - early) // STEPS))
    row_i = lax.broadcasted_iota(jnp.int32, (B, B), 0)
    col_i = lax.broadcasted_iota(jnp.int32, (B, B), 1)
    a_ref[...] = d0[...]

    def panel(turn, carry):
        s_ref[:, :B] = a_ref[...]
        s_ref[:, B:] = jnp.where(row_i == col_i, 1.0, 0.0)

        def step(k, carry):
            now = turn * (B // SUB) + k
            with jax.named_scope("factor"):
                factor_step(k, turn, s_ref, p_ref, u_ref, z_ref)
            at = early + now * each
            with jax.named_scope("relay"):
                lax.fori_loop(at, at + each, relay, 0)
            for i, acts in enumerate(events):
                if acts:
                    @pl.when(now == i)
                    def _():
                        for m, act in enumerate(acts):
                            with jax.named_scope(f"event{i}_{m}"):
                                act()
            return carry

        lax.fori_loop(0, B // SUB, step, 0)
        z_ref[turn] = jnp.where(row_i >= col_i, z_ref[turn], 0.0)
        f_ref[turn] = jnp.where(row_i >= col_i, u_ref[...].T, 0.0)
        pltpu.make_async_copy(z_ref.at[turn], z_o.at[turn], zsem.at[turn]).start()
        pltpu.make_async_copy(f_ref.at[turn], f_o.at[turn], fsem.at[turn]).start()

        @pl.when(turn == 0)
        def _():
            low = dot3(d1[:B], z_ref[0], LAST)
            half = low.astype(jnp.bfloat16)
            x_ref[...] = half
            a_ref[...] = d1[B:] - dot(half, half, LAST)

        return carry

    lax.fori_loop(0, PANELS, panel, 0)
    outs[3].start()
    with jax.named_scope("late"):
        lax.fori_loop(early + STEPS * each, total, relay, 0)
    with jax.named_scope("rowend"):
        act_rows[-1]()
        outs[0].start()
    with jax.named_scope("headend"):
        heads.end()
        outs[2].start()

    with jax.named_scope("sum"):
        def add(q, carry):
            cols[chunk(q)] = cbuf[chunk(q)] + (rin[chunk(q)] + lin[chunk(q)])
            return carry

        lax.fori_loop(0, CHUNKS, add, 0)
        outs[4].start()
        count = tops.shape[0]
        top = tops[...]
        for shift in range(1, nc):
            share_top(shift).wait()
            top = top + topland[pl.ds((shift - 1) * count, count)]
        topsum[...] = top
        outs[5].start()

    with jax.named_scope("sent"):
        @pl.when(c < nc - 1)
        def _():
            lax.fori_loop(0, CHUNKS, lambda q, k: (right(cbuf, q).wait_send(), k)[1], 0)

        @pl.when(c > 0)
        def _():
            lax.fori_loop(0, CHUNKS, lambda q, k: (left(cbuf, q).wait_send(), k)[1], 0)

    with jax.named_scope("written"):
        for turn in range(PANELS):
            pltpu.make_async_copy(z_ref.at[turn], z_o.at[turn], zsem.at[turn]).wait()
            pltpu.make_async_copy(f_ref.at[turn], f_o.at[turn], fsem.at[turn]).wait()
        for out in outs:
            out.wait()


def front(nr, nc, owner, index, cov, inn):
    rows, width = cov.shape
    part_p, groups, iw = inn.shape
    ratio = nr // nc
    h = ratio * part_p
    f32, bf16, i16 = jnp.float32, jnp.bfloat16, jnp.int16
    smem = pl.BlockSpec(memory_space=pltpu.SMEM)
    anywhere = pl.BlockSpec(memory_space=pl.ANY)
    vmem = pltpu.VMEM
    dma = pltpu.SemaphoreType.DMA
    both = PANELS * B
    count = PANELS * (rows // B)
    scratch = [vmem((rows, width), f32), dma, vmem(inn.shape, f32), dma, dma((6,)), dma((PANELS,)), dma((PANELS,))]
    scratch += [vmem((rows, both), i16)] * 6 + [dma((CHUNKS,))] * 4
    scratch += [vmem((count, LANES), f32), vmem(((nc - 1) * count, LANES), f32), dma((nc,)), dma((nc,)), vmem((count, LANES), f32)]
    scratch += [vmem((both, width), bf16)] * 2 + spread_scratch(both, width, bf16, nr)
    scratch += [vmem((B, B), f32)] * 2 + direct_scratch(B, B, nr, nc)
    scratch += [vmem((2 * B, B), f32)] * 2 + spread_scratch(2 * B, B, f32, nr, nc)
    scratch += [vmem((PANELS * h, B), f32)] * 2 + direct_scratch(PANELS * h, B, nr, nc)
    scratch += [vmem((groups, part_p, iw), i16), vmem((nr * part_p, iw), i16), vmem((h, nc * iw), i16), vmem((h, nc * iw), f32)]
    scratch += [vmem((8, LANES), f32), vmem((nr * 8, LANES), f32), vmem((nr * 8, LANES), f32)]
    scratch += [dma((nr,)), dma((nr,)), dma((nc,)), dma((nc,))] * 2
    scratch += [vmem((B, B), f32), vmem((B, 2 * B), f32), vmem((SUB, 2 * B), f32), vmem((B, B), f32)]
    scratch += [vmem((PANELS, B, B), f32)] * 2 + [vmem((B, B), bf16), vmem((rows, both), f32)]
    return pl.pallas_call(
        functools.partial(front_kernel, nr, nc),
        out_shape=(
            jax.ShapeDtypeStruct((rows, both), i16),
            jax.ShapeDtypeStruct((count, LANES), f32),
            jax.ShapeDtypeStruct((both, width), bf16),
            jax.ShapeDtypeStruct((h, nc * iw), f32),
            jax.ShapeDtypeStruct((PANELS * h, B), f32),
            jax.ShapeDtypeStruct((PANELS, B, B), f32),
            jax.ShapeDtypeStruct((PANELS, B, B), f32),
            jax.ShapeDtypeStruct((B, B), bf16),
        ),
        in_specs=[smem, smem, anywhere, anywhere],
        out_specs=(anywhere,) * 8,
        scratch_shapes=scratch,
        compiler_params=pltpu.CompilerParams(
            collective_id=0, has_side_effects=True, vmem_limit_bytes=56 * 1024 * 1024
        ),
    )(owner, index, cov, inn)


def tail_kernel(
    own_ref, idx_ref, w_any, cols_any, tops_any, rowp_any, f_any, z_any, x_any, vs_any, v_any,
    o_any, vout_any,
    w_ref, o_ref, cols_ref, tops_ref, rowp_ref, f_ref, z_ref, x_ref, vs_ref, v_ref, vout_ref, q_ref, half_ref,
    insem, wsem, osem, vsem, *, rb, cb,
):
    g = idx_ref[0]
    row0 = lax.axis_index("row") * rb
    col0 = lax.axis_index("col") * cb
    h = v_ref.shape[0]
    pairs = [
        (z_any, z_ref), (x_any, x_ref), (rowp_any, rowp_ref), (tops_any, tops_ref), (cols_any, cols_ref),
        (vs_any, vs_ref), (v_any, v_ref), (f_any, f_ref),
    ]
    ins = [pltpu.make_async_copy(src, dst, insem.at[i]) for i, (src, dst) in enumerate(pairs)]

    def stripe_in(j):
        span = rows_at(j * B, B)
        return pltpu.make_async_copy(w_any.at[:, span], w_ref.at[:, span], wsem.at[j])

    def stripe_out(j):
        span = rows_at(j * B, B)
        return pltpu.make_async_copy(o_ref.at[:, span], o_any.at[:, span], osem.at[j])

    for copy in ins[:5]:
        copy.start()
    for j in range(cb):
        stripe_in(j).start()
    for copy in ins[5:]:
        copy.start()
    for copy in ins[:3]:
        copy.wait()

    with jax.named_scope("qpanels"):
        x = x_ref[...]
        zh0, zl0 = split_bf16(z_ref[0])
        zh1, zl1 = split_bf16(z_ref[1])
        for k in range(cb):
            span = slice(k * B, (k + 1) * B)
            own = own_ref[col0 + k]
            q0 = dot(zh0, rowp_ref[:B, span]) + dot(zl0, rowp_ref[:B, span])
            q0 = jnp.where(own > g, q0, 0.0).astype(jnp.bfloat16)
            r1 = (rowp_ref[B:, span].astype(jnp.float32) - dot(x, q0)).astype(jnp.bfloat16)
            q1 = dot(zh1, r1) + dot(zl1, r1)
            q_ref[:B, span] = q0
            q_ref[B:, span] = jnp.where(own > g + 1, q1, 0.0).astype(jnp.bfloat16)

    for copy in ins[3:5]:
        copy.wait()

    with jax.named_scope("panels"):
        for i in range(rb):
            span = slice(i * B, (i + 1) * B)
            own = own_ref[row0 + i]
            c0 = decode(cols_ref[span, :B], tops_ref[PANELS * i : PANELS * i + 1, :1])
            p0 = dot3(c0, z_ref[0], LAST)
            h0 = jnp.where(own > g, p0, 0.0).astype(jnp.bfloat16)
            c1 = decode(cols_ref[span, B:], tops_ref[PANELS * i + 1 : PANELS * i + 2, :1]) - dot(h0, x, LAST)
            p1 = dot3(c1, z_ref[1], LAST)
            half_ref[span, :B] = h0
            half_ref[span, B:] = jnp.where(own > g + 1, p1, 0.0).astype(jnp.bfloat16)

    for copy in ins[5:]:
        copy.wait()

    def stripe(j, carry):
        span = rows_at(j * B, B)
        cown = own_ref[col0 + j]
        stripe_in(j).wait()
        with jax.named_scope("update"):
            o_ref[:, span] = w_ref[:, span] - dot(half_ref[...], q_ref[:, span])

        @pl.when(cown > g)
        def _():
            for i in range(rb):
                rown = own_ref[row0 + i]

                @pl.when((rown == g) | ((rown == g + 1) & (cown > g + 1)))
                def _():
                    o_ref[i * B : (i + 1) * B, span] = jnp.zeros((B, B), jnp.float32)

        for turn in range(PANELS):
            @pl.when(cown == g + turn)
            def _():
                for i in range(rb):
                    part = slice(i * B, (i + 1) * B)
                    rown = own_ref[row0 + i]

                    @pl.when(rown > g + turn)
                    def _():
                        left = w_ref[part, span]
                        if turn:
                            left = left - dot(half_ref[part, :B], x_ref[...], LAST)
                        o_ref[part, span] = dot3(left, z_ref[turn], LAST)

                    @pl.when(rown == g + turn)
                    def _():
                        o_ref[part, span] = f_ref[turn]

        stripe_out(j).start()
        return carry

    lax.fori_loop(0, cb, stripe, 0)

    with jax.named_scope("solve"):
        w0 = dot(vs_ref[:h], z_ref[0], LAST, HIGHEST)
        w0h = w0.astype(jnp.bfloat16)
        w1 = dot(vs_ref[h:] - dot(w0h, x, LAST), z_ref[1], LAST, HIGHEST)
        w1h = w1.astype(jnp.bfloat16)
        for i in range(rb):
            span = slice(i * B, (i + 1) * B)
            own = own_ref[row0 + i]
            new = v_ref[:, span] - (dot(w0h, half_ref[span, :B], LAST) + dot(w1h, half_ref[span, B:], LAST))
            new = jnp.where(own == g, w0, new)
            vout_ref[:, span] = jnp.where(own == g + 1, w1, new)
        done = pltpu.make_async_copy(vout_ref, vout_any, vsem)
        done.start()

    with jax.named_scope("drain"):
        lax.fori_loop(0, cb, lambda j, k: (stripe_out(j).wait(), k)[1], 0)
        done.wait()


def tail(owner, index, w, cols, tops, rowp, factors, z, x, vs, v):
    rows, width = w.shape
    cb = width // B
    smem = pl.BlockSpec(memory_space=pltpu.SMEM)
    anywhere = pl.BlockSpec(memory_space=pl.ANY)
    dma = pltpu.SemaphoreType.DMA
    arrays = [w, w, cols, tops, rowp, factors, z, x, vs, v, v]
    return pl.pallas_call(
        functools.partial(tail_kernel, rb=rows // B, cb=cb),
        in_specs=[smem, smem] + [anywhere] * 9,
        out_specs=[anywhere] * 2,
        scratch_shapes=[pltpu.VMEM(a.shape, a.dtype) for a in arrays]
        + [pltpu.VMEM((2 * B, width), jnp.bfloat16), pltpu.VMEM((rows, 2 * B), jnp.bfloat16)]
        + [dma((8,)), dma((cb,)), dma((cb,)), dma],
        out_shape=(jax.ShapeDtypeStruct(w.shape, w.dtype), jax.ShapeDtypeStruct(v.shape, v.dtype)),
        compiler_params=pltpu.CompilerParams(vmem_limit_bytes=60 * 1024 * 1024),
    )(owner, index, w, cols, tops, rowp, factors, z, x, vs, v)


def per_device(covariance, innovations, block_owner, panel_index):
    nr, nc = lax.axis_size("row"), lax.axis_size("col")
    cols, tops, rowp, v, vs, factors, z, x = front(nr, nc, block_owner, panel_index, covariance, innovations)
    return tail(block_owner, panel_index, covariance, cols, tops, rowp, factors, z, x, vs, v)


def solution(mesh):
    placed = (P("row", "col"), P("row", None, "col"), P(), P())
    return jax.shard_map(
        per_device,
        mesh=mesh,
        in_specs=placed,
        out_specs=(P("row", "col"), P("col", "row")),
        check_vma=False,
    )
```

```python
import functools

import jax
import jax.numpy as jnp
from jax import lax
from jax.experimental import pallas as pl
from jax.experimental.pallas import tpu as pltpu
from jax.sharding import PartitionSpec as P

B = 256
PANELS = 2
SUB = 64
G8 = SUB // 8
LANES = 128
TW = 2 * B // LANES
HIGHEST = lax.Precision.HIGHEST

LAST = (((1,), (1,)), ((), ()))
FIRST = (((0,), (0,)), ((), ()))
PLAIN = (((1,), (0,)), ((), ()))


def dot(a, b, dims=PLAIN, precision=None):
    return lax.dot_general(a, b, dims, precision=precision, preferred_element_type=jnp.float32)


def split_bf16(x):
    hi = x.astype(jnp.bfloat16)
    lo = (x - hi.astype(jnp.float32)).astype(jnp.bfloat16)
    return hi, lo


def dot3(a, b, dims=PLAIN):
    ah, al = split_bf16(a)
    bh, bl = split_bf16(b)
    return dot(ah, bh, dims) + (dot(ah, bl, dims) + dot(al, bh, dims))


def lanes(x):
    return jnp.broadcast_to(x, (8, LANES))


def factor_panel(s_ref, p_ref):
    sub_iota = lax.broadcasted_iota(jnp.int32, (8, LANES), 0)
    rows = [[s_ref[8 * g : 8 * g + 8, LANES * t : LANES * (t + 1)] for t in range(TW)] for g in range(G8)]
    for b in range(G8):
        c0 = 8 * b
        col = [[lanes(rows[g][0][:, c0 + j : c0 + j + 1]) for j in range(8)] for g in range(b, G8)]
        e = [[lanes(col[0][j][i : i + 1, :]) for j in range(i + 1)] for i in range(8)]
        r = []
        l = [[None] * 8 for _ in range(8)]
        for j in range(8):
            rj = lax.rsqrt(e[j][j])
            r.append(rj)
            for i in range(j + 1, 8):
                l[i][j] = e[i][j] * rj
            for i in range(j + 1, 8):
                for k in range(j + 1, i + 1):
                    e[i][k] = e[i][k] - l[i][j] * l[k][j]
        y = []
        for i in range(8):
            yi = []
            for t in range(TW):
                v = lanes(rows[b][t][i : i + 1, :])
                for j in range(i):
                    v = v - l[i][j] * y[j][t]
                yi.append(v * r[i])
            y.append(yi)
        for t in range(TW):
            u = y[0][t]
            for i in range(1, 8):
                u = jnp.where(sub_iota == i, y[i][t], u)
            p_ref[8 * b : 8 * b + 8, LANES * t : LANES * (t + 1)] = u
        for g in range(b + 1, G8):
            cs = []
            for j in range(8):
                v = col[g - b][j]
                for k in range(j):
                    v = v - l[j][k] * cs[k]
                cs.append(v * r[j])
            for t in range(TW):
                v = rows[g][t]
                for j in range(8):
                    v = v - cs[j] * y[j][t]
                rows[g][t] = v


MESH = pl.DeviceIdType.MESH
CHUNKS = 8
LAG = 2
CODE = 32767.0
TINY = 1e-37
STEPS = PANELS * (B // SUB)


def factor_step(k, turn, s_ref, p_ref, u_ref, z_ref):
    factor_panel(s_ref, p_ref)
    start = pl.multiple_of(k * SUB, SUB)
    u_ref[pl.ds(start, SUB), :] = pltpu.roll(p_ref[:, :B], start, 1)
    z_ref[turn, pl.ds(start, SUB), :] = p_ref[:, B:]
    left = p_ref[:, :B]
    rolled = pltpu.roll(left, B - SUB, 1)
    lane = lax.broadcasted_iota(jnp.int32, (SUB, B), 1)
    rolled = jnp.where(lane < B - SUB, rolled, 0.0)
    upd_a = dot3(rolled, rolled, FIRST)
    upd_z = dot3(rolled, p_ref[:, B:], FIRST)
    keep = B - SUB
    old = pltpu.roll(s_ref[SUB:, :B], B - SUB, 1)
    lane2 = lax.broadcasted_iota(jnp.int32, (keep, B), 1)
    old = jnp.where(lane2 < keep, old, 0.0)
    old_z = s_ref[SUB:, B:]
    s_ref[:keep, :B] = old - upd_a[:keep]
    s_ref[:keep, B:] = old_z - upd_z[:keep]
    s_ref[keep:, :] = jnp.zeros((SUB, 2 * B), jnp.float32)


def remote(src, dst, send, recv, where):
    return pltpu.make_async_remote_copy(
        src_ref=src, dst_ref=dst, send_sem=send, recv_sem=recv, device_id=where, device_id_type=MESH
    )


def rows_at(start, count):
    return pl.ds(pl.multiple_of(start, count), count)


class Spread:
    def __init__(self, buf, out, hop, send, recv, base, size, bits, cross=None):
        self.buf, self.out, self.hop, self.send, self.recv = buf, out, hop, send, recv
        self.cross = cross
        self.stages = []
        start, hop_at = base, 0
        for axis, bit, whole in bits:
            me = lax.axis_index(axis)
            digit = lax.rem(me // bit, 2)
            where = {axis: me + bit - 2 * bit * digit}
            if whole:
                count, give = size, start
            else:
                count = size // 2
                give, start = start + (1 - digit) * count, start + digit * count
            self.stages.append((where, give, start, count, hop_at, whole))
            hop_at += count
            size = count
        self.last, self.size = start, size

    def down(self, i):
        where, give, keep, count, at, _ = self.stages[i]
        return remote(self.buf.at[rows_at(give, count)], self.hop.at[pl.ds(at, count)], self.send.at[i], self.recv.at[i], where)

    def up(self, i):
        where, give, keep, count, at, _ = self.stages[i]
        n = len(self.stages) + i
        rows = self.out.at[rows_at(keep, count)]
        return remote(rows, rows, self.send.at[n], self.recv.at[n], where)

    def add(self, i):
        self.down(i).wait()
        _, _, keep, count, at, _ = self.stages[i]
        rows = rows_at(keep, count)
        to = self.out if i == len(self.stages) - 1 and self.cross is None else self.buf
        to[rows] = self.buf[rows] + self.hop[pl.ds(at, count)]

    def over(self, shift):
        land, send, recv, nc = self.cross
        to = lax.rem(lax.axis_index("col") + shift, nc)
        part = pl.ds((shift - 1) * self.size, self.size)
        return remote(
            self.buf.at[rows_at(self.last, self.size)], land.at[part], send.at[shift], recv.at[shift], {"col": to}
        )

    def send_over(self):
        for shift in range(1, self.cross[3]):
            self.over(shift).start()

    def add_over(self):
        rows = rows_at(self.last, self.size)
        total = self.buf[rows]
        for shift in range(1, self.cross[3]):
            self.over(shift).wait()
            total = total + self.cross[0][pl.ds((shift - 1) * self.size, self.size)]
        self.out[rows] = total

    def acts(self):
        count = len(self.stages)
        ends = [functools.partial(self.add, i) for i in range(count)]
        starts = [lambda i=i: self.down(i).start() for i in range(count)]
        if self.cross is not None:
            starts.append(self.send_over)
            ends.append(self.add_over)
        for i in reversed(range(count)):
            if not self.stages[i][5]:
                starts.append(lambda i=i: self.up(i).start())
                ends.append(lambda i=i: self.up(i).wait())
        acts = [starts[0]]
        acts += [lambda a=a, b=b: (a(), b()) for a, b in zip(ends, starts[1:])]
        return acts + [ends[-1]]


def bits_of(axis, size, whole=False):
    return [(axis, 1 << b, whole) for b in range(size.bit_length() - 1)]


def spread_pair(buf, out, hop, send, recv, size, nr, cross=None):
    bits = bits_of("row", nr)
    orders = [bits, bits[:1] + bits[:0:-1]]
    half = size // 2
    both = []
    for part in range(2):
        over = None if cross is None else tuple(ref.at[part] for ref in cross[:3]) + (cross[3],)
        both.append(
            Spread(buf, out, hop.at[part], send.at[part], recv.at[part], part * half, half, orders[part], over).acts()
        )
    return [lambda a=a, b=b: (a(), b()) for a, b in zip(*both)]


class Direct:
    def __init__(self, nr, nc, buf, out, land, crossland, sends, recvs):
        self.nr, self.nc = nr, nc
        self.buf, self.out, self.land, self.crossland = buf, out, land, crossland
        self.sends, self.recvs = sends, recvs
        self.r, self.c = lax.axis_index("row"), lax.axis_index("col")
        self.size = buf.shape[0] // nr
        self.mine = rows_at(self.r * self.size, self.size)

    def part(self, shift):
        return pl.ds((shift - 1) * self.size, self.size)

    def down(self, shift):
        to = lax.rem(self.r + shift, self.nr)
        return remote(
            self.buf.at[rows_at(to * self.size, self.size)], self.land.at[self.part(shift)],
            self.sends.at[0], self.recvs.at[0], {"row": to},
        )

    def over(self, shift):
        return remote(
            self.buf.at[self.mine], self.crossland.at[self.part(shift)],
            self.sends.at[1], self.recvs.at[1], {"col": lax.rem(self.c + shift, self.nc)},
        )

    def up(self, shift):
        rows = self.out.at[self.mine]
        return remote(rows, rows, self.sends.at[2], self.recvs.at[2], {"row": lax.rem(self.r + shift, self.nr)})

    def begin(self):
        for shift in range(1, self.nr):
            self.down(shift).start()

    def all_of(self, group, count, land):
        part = pl.ds(0, (count - 1) * self.size)
        remote(self.buf.at[part], land.at[part], self.sends.at[group], self.recvs.at[group], {"row": self.r}).wait()

    def total(self, group, count, land):
        self.all_of(group, count, land)
        value = self.buf[self.mine]
        for shift in range(1, count):
            value = value + land[self.part(shift)]
        return value

    def cross(self):
        self.buf[self.mine] = self.total(0, self.nr, self.land)
        for shift in range(1, self.nc):
            self.over(shift).start()

    def crossed(self):
        self.out[self.mine] = self.total(1, self.nc, self.crossland)
        self.raise_all()

    def flat(self):
        self.out[self.mine] = self.total(0, self.nr, self.land)
        self.raise_all()

    def raise_all(self):
        for shift in range(1, self.nr):
            self.up(shift).start()

    def end(self):
        self.all_of(2, self.nr, self.out)


def direct_scratch(size, width, nr, nc):
    part = size // nr
    dma = pltpu.SemaphoreType.DMA
    return [
        pltpu.VMEM(((nr - 1) * part, width), jnp.float32),
        pltpu.VMEM(((nc - 1) * part, width), jnp.float32),
        dma((3,)), dma((3,)),
    ]


def spread_scratch(size, width, dtype, nr, nc=None):
    half, n = size // 2, nr.bit_length() - 1
    dma = pltpu.SemaphoreType.DMA
    out = [pltpu.VMEM((2, half, width), dtype), dma((2, 2 * n)), dma((2, 2 * n))]
    if nc is not None:
        out += [pltpu.VMEM((2, (nc - 1) * (half // nr), width), dtype), dma((2, nc)), dma((2, nc))]
    return out


def choose(owner, wanted, value, otherwise):
    return jnp.where(jnp.full(value.shape, owner, jnp.int32) == wanted, value, otherwise)


def encode(x, top):
    part = jnp.sqrt(jnp.abs(x) * (1.0 / jnp.maximum(top, TINY)))
    code = (part * CODE + 0.5).astype(jnp.int32)
    return jnp.where(x < 0.0, -code, code).astype(jnp.int16)


def decode(code, top):
    part = code.astype(jnp.int32).astype(jnp.float32) * (1.0 / CODE)
    return part * jnp.abs(part) * top


def largest(x):
    top = jnp.max(jnp.abs(x), axis=0, keepdims=True)
    return jnp.max(top, axis=1, keepdims=True)


def front_kernel(
    nr, nc, own_ref, idx_ref, cov, inn,
    cols_o, tops_o, rowp_o, v_o, vs_o, f_o, z_o, x_o,
    w, wsem, vin, vinsem, outsem, zsem, fsem,
    cbuf, cols, rin, lin, rtx, ltx, rs, rr, ls, lr, tops, topland, topsend, toprecv, topsum,
    rbuf, rowp, rhop, rsend, rrecv,
    d0buf, d0, d0land, d0over, d0s, d0r,
    d1buf, d1, d1hop, d1send, d1recv, d1over, d1s, d1r,
    vsbuf, vs, vsland, vsover, vss, vsr,
    vt, vst, vq, v, vtop, vtst, vtq, v1send, v1recv, v2send, v2recv, t1send, t1recv, t2send, t2recv,
    a_ref, s_ref, p_ref, u_ref, f_ref, z_ref, x_ref, picks,
):
    r = lax.axis_index("row")
    c = lax.axis_index("col")
    rows, width = w.shape
    rb, cb = rows // B, width // B
    load = pltpu.make_async_copy(cov, w, wsem)
    vload = pltpu.make_async_copy(inn, vin, vinsem)
    vload.start()
    load.start()
    barrier = pltpu.get_barrier_semaphore()
    for shift in range(1, nr):
        pl.semaphore_signal(barrier, inc=1, device_id={"row": lax.rem(r + shift, nr)}, device_id_type=MESH)
    for shift in range(1, nc):
        pl.semaphore_signal(barrier, inc=1, device_id={"col": lax.rem(c + shift, nc)}, device_id_type=MESH)

    part_p, iw = inn.shape[0], inn.shape[2]
    ratio = nr // nc
    h = ratio * part_p

    def first_stop(shift):
        to = {"row": lax.rem(r + shift, nr)}
        return (
            remote(vt.at[lax.rem(r + shift, nr)], vst.at[rows_at(r * part_p, part_p)], v1send.at[shift], v1recv.at[shift], to),
            remote(vtop, vtst.at[rows_at(r * 8, 8)], t1send.at[shift], t1recv.at[shift], to),
        )

    def second_stop(shift):
        at = lax.rem(c + shift, nc)
        to = {"col": at}
        return (
            remote(vst.at[rows_at(at * h, h)], vq.at[:, rows_at(c * iw, iw)], v2send.at[shift], v2recv.at[shift], to),
            remote(
                vtst.at[rows_at(at * ratio * 8, ratio * 8)], vtq.at[rows_at(c * ratio * 8, ratio * 8)],
                t2send.at[shift], t2recv.at[shift], to,
            ),
        )

    def code_innovations():
        vload.wait()
        top = largest(vin[:, 0, :])
        for group in range(1, nr):
            top = jnp.maximum(top, largest(vin[:, group, :]))
        vtop[...] = jnp.broadcast_to(top, vtop.shape)
        for group in range(nr):
            vt[group] = encode(vin[:, group, :], top)

    g = idx_ref[0]
    d0buf[...] = jnp.zeros_like(d0buf)
    d1buf[...] = jnp.zeros_like(d1buf)
    zero = jnp.zeros((B, B), jnp.float32)

    @pl.when(c == 0)
    def _():
        rin[...] = jnp.zeros_like(rin)

    @pl.when(c == nc - 1)
    def _():
        lin[...] = jnp.zeros_like(lin)

    with jax.named_scope("load"):
        load.wait()

    def pick_cols(i, carry):
        span = rows_at(i * B, B)
        own = own_ref[r * rb + i]
        picked = []
        for t in range(PANELS):
            tile = zero
            for j in range(cb):
                tile = choose(own_ref[c * cb + j], g + t, w[span, j * B : (j + 1) * B], tile)
            picks[span, t * B : (t + 1) * B] = tile
            picked.append(tile)
        d0buf[...] = choose(own, g, picked[0], d0buf[...])
        d1buf[:B] = choose(own, g + 1, picked[0], d1buf[:B])
        d1buf[B:] = choose(own, g + 1, picked[1], d1buf[B:])
        return carry

    def code_cols(i, carry):
        span = rows_at(i * B, B)
        for t in range(PANELS):
            tile = picks[span, t * B : (t + 1) * B]
            top = largest(tile)
            tops[pl.ds(i * PANELS + t, 1), :] = jnp.broadcast_to(top, (1, LANES))
            cbuf[span, t * B : (t + 1) * B] = encode(tile, top)
        return carry

    with jax.named_scope("columns"):
        lax.fori_loop(0, rb, pick_cols, 0)
    first = Direct(nr, nc, d0buf, d0, d0land, d0over, d0s, d0r)
    second = spread_pair(d1buf, d1, d1hop, d1send, d1recv, 2 * B, nr, (d1over, d1s, d1r, nc))
    with jax.named_scope("barrier"):
        pl.semaphore_wait(barrier, nr - 1 + nc - 1)
    first.begin()
    second[0]()
    with jax.named_scope("code"):
        lax.fori_loop(0, rb, code_cols, 0)

    size = rows // CHUNKS

    def chunk(q):
        return rows_at(q * size, size)

    def right(src, q):
        return remote(src.at[chunk(q)], rin.at[chunk(q)], rs, rr.at[q], {"col": c + 1})

    def left(src, q):
        return remote(src.at[chunk(q)], lin.at[chunk(q)], ls, lr.at[q], {"col": c - 1})

    def push(begin, end):
        def one(q, carry):
            @pl.when(c == 0)
            def _():
                right(cbuf, q).start()

            @pl.when(c == nc - 1)
            def _():
                left(cbuf, q).start()

            return carry

        lax.fori_loop(begin, end, one, 0)

    def relay(t, carry):
        q = t - LAG * (c - 1)

        @pl.when((q >= 0) & (q < CHUNKS) & (c > 0))
        def _():
            right(cbuf, q).wait_recv()

            @pl.when(c < nc - 1)
            def _():
                rtx[chunk(q)] = rin[chunk(q)] + cbuf[chunk(q)]
                right(rtx, q).start()

        p = t - LAG * (nc - 2 - c)

        @pl.when((p >= 0) & (p < CHUNKS) & (c < nc - 1))
        def _():
            left(cbuf, p).wait_recv()

            @pl.when(c > 0)
            def _():
                ltx[chunk(p)] = lin[chunk(p)] + cbuf[chunk(p)]
                left(ltx, p).start()

        return carry

    def share_top(shift):
        count = tops.shape[0]
        return remote(
            tops, topland.at[pl.ds((shift - 1) * count, count)], topsend.at[shift], toprecv.at[shift],
            {"col": lax.rem(c + shift, nc)},
        )

    def fill_rows(i, carry):
        span = rows_at(i * B, B)
        for t in range(PANELS):
            tile = zero
            for k in range(rb):
                tile = choose(own_ref[r * rb + k], g + t, w[k * B : (k + 1) * B, span], tile)
            rbuf[t * B : (t + 1) * B, span] = tile.astype(jnp.bfloat16)
        return carry

    act_rows = spread_pair(rbuf, rowp, rhop, rsend, rrecv, PANELS * B, nr)

    def leave():
        for shift in range(1, nr):
            for copy in first_stop(shift):
                copy.start()
        vst[rows_at(r * part_p, part_p)] = vt[r]
        vtst[rows_at(r * 8, 8)] = vtop[...]
        for shift in range(1, nc):
            share_top(shift).start()

    def pass_on():
        for shift in range(1, nr):
            for copy in first_stop(shift):
                copy.wait()
        for shift in range(1, nc):
            for copy in second_stop(shift):
                copy.start()
        vq[:, rows_at(c * iw, iw)] = vst[rows_at(c * h, h)]
        vtq[rows_at(c * ratio * 8, ratio * 8)] = vtst[rows_at(c * ratio * 8, ratio * 8)]

    early = 0

    def relays(count):
        nonlocal early
        lax.fori_loop(early, early + count, relay, 0)
        early += count

    with jax.named_scope("first1"):
        push(0, 1)
        first.cross()
        second[1]()
    with jax.named_scope("innovations"):
        code_innovations()
        push(1, 2)
    with jax.named_scope("rows"):
        lax.fori_loop(0, cb, fill_rows, 0)
        act_rows[0]()
    with jax.named_scope("early1"):
        relays(1)
        second[2]()
    with jax.named_scope("first2"):
        first.crossed()
        push(2, 3)
    with jax.named_scope("second1"):
        second[3]()
        push(3, 5)
    with jax.named_scope("early2"):
        relays(1)
    with jax.named_scope("first3"):
        first.end()
    with jax.named_scope("early3"):
        act_rows[1]()
        leave()
        push(5, CHUNKS)
        relays(1)

    outs = [
        pltpu.make_async_copy(src, dst, outsem.at[i])
        for i, (src, dst) in enumerate(
            [(rowp, rowp_o), (v, v_o), (vs, vs_o), (x_ref, x_o), (cols, cols_o), (topsum, tops_o)]
        )
    ]
    heads = Direct(nr, nc, vsbuf, vs, vsland, vsover, vss, vsr)

    def arrived():
        for shift in range(1, nc):
            for copy in second_stop(shift):
                copy.wait()
        for b in range(nc):
            for a in range(ratio):
                at, block = slice(a * part_p, (a + 1) * part_p), slice(b * iw, (b + 1) * iw)
                n = (b * ratio + a) * 8
                v[at, block] = decode(vq[at, block], vtq[n : n + 1, :1])
        outs[1].start()
        for t in range(PANELS):
            part = jnp.zeros((h, B), jnp.float32)
            for k in range(rb):
                part = choose(own_ref[r * rb + k], g + t, v[:, k * B : (k + 1) * B], part)
            vsbuf[t * h : (t + 1) * h] = part
        heads.begin()

    events = [[] for _ in range(STEPS)]
    half = STEPS // PANELS
    later = second[4:]
    for i, act in enumerate(later):
        events[i * half // len(later)].append(act)
    events[1].append(pass_on)
    later = act_rows[2:-1]
    for i, act in enumerate(later):
        events[2 + i * (STEPS - 2) // len(later)].append(act)
    events[half].append(arrived)
    events[half + 2].append(heads.flat)
    total = CHUNKS + LAG * (nc - 2)
    each = min(1, -(-(total - early) // STEPS))
    row_i = lax.broadcasted_iota(jnp.int32, (B, B), 0)
    col_i = lax.broadcasted_iota(jnp.int32, (B, B), 1)
    a_ref[...] = d0[...]

    def panel(turn, carry):
        s_ref[:, :B] = a_ref[...]
        s_ref[:, B:] = jnp.where(row_i == col_i, 1.0, 0.0)

        def step(k, carry):
            now = turn * (B // SUB) + k
            with jax.named_scope("factor"):
                factor_step(k, turn, s_ref, p_ref, u_ref, z_ref)
            at = early + now * each
            with jax.named_scope("relay"):
                lax.fori_loop(at, at + each, relay, 0)
            for i, acts in enumerate(events):
                if acts:
                    @pl.when(now == i)
                    def _():
                        for m, act in enumerate(acts):
                            with jax.named_scope(f"event{i}_{m}"):
                                act()
            return carry

        lax.fori_loop(0, B // SUB, step, 0)
        z_ref[turn] = jnp.where(row_i >= col_i, z_ref[turn], 0.0)
        f_ref[turn] = jnp.where(row_i >= col_i, u_ref[...].T, 0.0)
        pltpu.make_async_copy(z_ref.at[turn], z_o.at[turn], zsem.at[turn]).start()
        pltpu.make_async_copy(f_ref.at[turn], f_o.at[turn], fsem.at[turn]).start()

        @pl.when(turn == 0)
        def _():
            low = dot3(d1[:B], z_ref[0], LAST)
            half = low.astype(jnp.bfloat16)
            x_ref[...] = half
            a_ref[...] = d1[B:] - dot(half, half, LAST)

        return carry

    lax.fori_loop(0, PANELS, panel, 0)
    outs[3].start()
    with jax.named_scope("late"):
        lax.fori_loop(early + STEPS * each, total, relay, 0)
    with jax.named_scope("rowend"):
        act_rows[-1]()
        outs[0].start()
    with jax.named_scope("headend"):
        heads.end()
        outs[2].start()

    with jax.named_scope("sum"):
        def add(q, carry):
            cols[chunk(q)] = cbuf[chunk(q)] + (rin[chunk(q)] + lin[chunk(q)])
            return carry

        lax.fori_loop(0, CHUNKS, add, 0)
        outs[4].start()
        count = tops.shape[0]
        top = tops[...]
        for shift in range(1, nc):
            share_top(shift).wait()
            top = top + topland[pl.ds((shift - 1) * count, count)]
        topsum[...] = top
        outs[5].start()

    with jax.named_scope("sent"):
        @pl.when(c < nc - 1)
        def _():
            remote(cbuf, rin, rs, rr.at[0], {"col": c + 1}).wait_send()

        @pl.when(c > 0)
        def _():
            remote(cbuf, lin, ls, lr.at[0], {"col": c - 1}).wait_send()

    with jax.named_scope("written"):
        for turn in range(PANELS):
            pltpu.make_async_copy(z_ref.at[turn], z_o.at[turn], zsem.at[turn]).wait()
            pltpu.make_async_copy(f_ref.at[turn], f_o.at[turn], fsem.at[turn]).wait()
        for out in outs:
            out.wait()


def front(nr, nc, owner, index, cov, inn):
    rows, width = cov.shape
    part_p, groups, iw = inn.shape
    ratio = nr // nc
    h = ratio * part_p
    f32, bf16, i16 = jnp.float32, jnp.bfloat16, jnp.int16
    smem = pl.BlockSpec(memory_space=pltpu.SMEM)
    anywhere = pl.BlockSpec(memory_space=pl.ANY)
    vmem = pltpu.VMEM
    dma = pltpu.SemaphoreType.DMA
    both = PANELS * B
    count = PANELS * (rows // B)
    scratch = [vmem((rows, width), f32), dma, vmem(inn.shape, f32), dma, dma((6,)), dma((PANELS,)), dma((PANELS,))]
    scratch += [vmem((rows, both), i16)] * 6 + [dma, dma((CHUNKS,))] * 2
    scratch += [vmem((count, LANES), f32), vmem(((nc - 1) * count, LANES), f32), dma((nc,)), dma((nc,)), vmem((count, LANES), f32)]
    scratch += [vmem((both, width), bf16)] * 2 + spread_scratch(both, width, bf16, nr)
    scratch += [vmem((B, B), f32)] * 2 + direct_scratch(B, B, nr, nc)
    scratch += [vmem((2 * B, B), f32)] * 2 + spread_scratch(2 * B, B, f32, nr, nc)
    scratch += [vmem((PANELS * h, B), f32)] * 2 + direct_scratch(PANELS * h, B, nr, nc)
    scratch += [vmem((groups, part_p, iw), i16), vmem((nr * part_p, iw), i16), vmem((h, nc * iw), i16), vmem((h, nc * iw), f32)]
    scratch += [vmem((8, LANES), f32), vmem((nr * 8, LANES), f32), vmem((nr * 8, LANES), f32)]
    scratch += [dma((nr,)), dma((nr,)), dma((nc,)), dma((nc,))] * 2
    scratch += [vmem((B, B), f32), vmem((B, 2 * B), f32), vmem((SUB, 2 * B), f32), vmem((B, B), f32)]
    scratch += [vmem((PANELS, B, B), f32)] * 2 + [vmem((B, B), bf16), vmem((rows, both), f32)]
    return pl.pallas_call(
        functools.partial(front_kernel, nr, nc),
        out_shape=(
            jax.ShapeDtypeStruct((rows, both), i16),
            jax.ShapeDtypeStruct((count, LANES), f32),
            jax.ShapeDtypeStruct((both, width), bf16),
            jax.ShapeDtypeStruct((h, nc * iw), f32),
            jax.ShapeDtypeStruct((PANELS * h, B), f32),
            jax.ShapeDtypeStruct((PANELS, B, B), f32),
            jax.ShapeDtypeStruct((PANELS, B, B), f32),
            jax.ShapeDtypeStruct((B, B), bf16),
        ),
        in_specs=[smem, smem, anywhere, anywhere],
        out_specs=(anywhere,) * 8,
        scratch_shapes=scratch,
        compiler_params=pltpu.CompilerParams(
            collective_id=0, has_side_effects=True, vmem_limit_bytes=56 * 1024 * 1024
        ),
    )(owner, index, cov, inn)


def tail_kernel(
    own_ref, idx_ref, w_any, cols_any, tops_any, rowp_any, f_any, z_any, x_any, vs_any, v_any,
    o_any, vout_any,
    w_ref, o_ref, cols_ref, tops_ref, rowp_ref, f_ref, z_ref, x_ref, vs_ref, v_ref, vout_ref, q_ref, half_ref,
    insem, wsem, osem, vsem, *, rb, cb,
):
    g = idx_ref[0]
    row0 = lax.axis_index("row") * rb
    col0 = lax.axis_index("col") * cb
    h = v_ref.shape[0]
    pairs = [
        (z_any, z_ref), (x_any, x_ref), (rowp_any, rowp_ref), (tops_any, tops_ref), (cols_any, cols_ref),
        (vs_any, vs_ref), (v_any, v_ref), (f_any, f_ref),
    ]
    ins = [pltpu.make_async_copy(src, dst, insem.at[i]) for i, (src, dst) in enumerate(pairs)]

    def stripe_in(j):
        span = rows_at(j * B, B)
        return pltpu.make_async_copy(w_any.at[:, span], w_ref.at[:, span], wsem.at[j])

    def stripe_out(j):
        span = rows_at(j * B, B)
        return pltpu.make_async_copy(o_ref.at[:, span], o_any.at[:, span], osem.at[j])

    for copy in ins[:5]:
        copy.start()
    for copy in ins[:3]:
        copy.wait()
    for j in range(cb):
        stripe_in(j).start()
    for copy in ins[5:]:
        copy.start()

    with jax.named_scope("qpanels"):
        x = x_ref[...]
        zh0, zl0 = split_bf16(z_ref[0])
        zh1, zl1 = split_bf16(z_ref[1])
        for k in range(cb):
            span = slice(k * B, (k + 1) * B)
            own = own_ref[col0 + k]
            q0 = dot(zh0, rowp_ref[:B, span]) + dot(zl0, rowp_ref[:B, span])
            q0 = jnp.where(own > g, q0, 0.0).astype(jnp.bfloat16)
            r1 = (rowp_ref[B:, span].astype(jnp.float32) - dot(x, q0)).astype(jnp.bfloat16)
            q1 = dot(zh1, r1) + dot(zl1, r1)
            q_ref[:B, span] = q0
            q_ref[B:, span] = jnp.where(own > g + 1, q1, 0.0).astype(jnp.bfloat16)

    for copy in ins[3:5]:
        copy.wait()

    with jax.named_scope("panels"):
        for i in range(rb):
            span = slice(i * B, (i + 1) * B)
            own = own_ref[row0 + i]
            c0 = decode(cols_ref[span, :B], tops_ref[PANELS * i : PANELS * i + 1, :1])
            p0 = dot3(c0, z_ref[0], LAST)
            h0 = jnp.where(own > g, p0, 0.0).astype(jnp.bfloat16)
            c1 = decode(cols_ref[span, B:], tops_ref[PANELS * i + 1 : PANELS * i + 2, :1]) - dot(h0, x, LAST)
            p1 = dot3(c1, z_ref[1], LAST)
            half_ref[span, :B] = h0
            half_ref[span, B:] = jnp.where(own > g + 1, p1, 0.0).astype(jnp.bfloat16)

    for copy in ins[5:]:
        copy.wait()

    def stripe(j, carry):
        span = rows_at(j * B, B)
        cown = own_ref[col0 + j]
        stripe_in(j).wait()
        with jax.named_scope("update"):
            o_ref[:, span] = w_ref[:, span] - dot(half_ref[...], q_ref[:, span])

        @pl.when(cown > g)
        def _():
            for i in range(rb):
                rown = own_ref[row0 + i]

                @pl.when((rown == g) | ((rown == g + 1) & (cown > g + 1)))
                def _():
                    o_ref[i * B : (i + 1) * B, span] = jnp.zeros((B, B), jnp.float32)

        for turn in range(PANELS):
            @pl.when(cown == g + turn)
            def _():
                for i in range(rb):
                    part = slice(i * B, (i + 1) * B)
                    rown = own_ref[row0 + i]

                    @pl.when(rown > g + turn)
                    def _():
                        left = w_ref[part, span]
                        if turn:
                            left = left - dot(half_ref[part, :B], x_ref[...], LAST)
                        o_ref[part, span] = dot3(left, z_ref[turn], LAST)

                    @pl.when(rown == g + turn)
                    def _():
                        o_ref[part, span] = f_ref[turn]

        stripe_out(j).start()
        return carry

    lax.fori_loop(0, cb, stripe, 0)

    with jax.named_scope("solve"):
        w0 = dot(vs_ref[:h], z_ref[0], LAST, HIGHEST)
        w0h = w0.astype(jnp.bfloat16)
        w1 = dot(vs_ref[h:] - dot(w0h, x, LAST), z_ref[1], LAST, HIGHEST)
        w1h = w1.astype(jnp.bfloat16)
        for i in range(rb):
            span = slice(i * B, (i + 1) * B)
            own = own_ref[row0 + i]
            new = v_ref[:, span] - (dot(w0h, half_ref[span, :B], LAST) + dot(w1h, half_ref[span, B:], LAST))
            new = jnp.where(own == g, w0, new)
            vout_ref[:, span] = jnp.where(own == g + 1, w1, new)
        done = pltpu.make_async_copy(vout_ref, vout_any, vsem)
        done.start()

    with jax.named_scope("drain"):
        lax.fori_loop(0, cb, lambda j, k: (stripe_out(j).wait(), k)[1], 0)
        done.wait()


def tail(owner, index, w, cols, tops, rowp, factors, z, x, vs, v):
    rows, width = w.shape
    cb = width // B
    smem = pl.BlockSpec(memory_space=pltpu.SMEM)
    anywhere = pl.BlockSpec(memory_space=pl.ANY)
    dma = pltpu.SemaphoreType.DMA
    arrays = [w, w, cols, tops, rowp, factors, z, x, vs, v, v]
    return pl.pallas_call(
        functools.partial(tail_kernel, rb=rows // B, cb=cb),
        in_specs=[smem, smem] + [anywhere] * 9,
        out_specs=[anywhere] * 2,
        scratch_shapes=[pltpu.VMEM(a.shape, a.dtype) for a in arrays]
        + [pltpu.VMEM((2 * B, width), jnp.bfloat16), pltpu.VMEM((rows, 2 * B), jnp.bfloat16)]
        + [dma((8,)), dma((cb,)), dma((cb,)), dma],
        out_shape=(jax.ShapeDtypeStruct(w.shape, w.dtype), jax.ShapeDtypeStruct(v.shape, v.dtype)),
        compiler_params=pltpu.CompilerParams(vmem_limit_bytes=60 * 1024 * 1024),
    )(owner, index, w, cols, tops, rowp, factors, z, x, vs, v)


def per_device(covariance, innovations, block_owner, panel_index):
    nr, nc = lax.axis_size("row"), lax.axis_size("col")
    cols, tops, rowp, v, vs, factors, z, x = front(nr, nc, block_owner, panel_index, covariance, innovations)
    return tail(block_owner, panel_index, covariance, cols, tops, rowp, factors, z, x, vs, v)


def solution(mesh):
    placed = (P("row", "col"), P("row", None, "col"), P(), P())
    return jax.shard_map(
        per_device,
        mesh=mesh,
        in_specs=placed,
        out_specs=(P("row", "col"), P("col", "row")),
        check_vma=False,
    )
```

```python
import functools

import jax
import jax.numpy as jnp
from jax import lax
from jax.experimental import pallas as pl
from jax.experimental.pallas import tpu as pltpu
from jax.sharding import PartitionSpec as P

B = 256
PANELS = 2
SUB = 64
G8 = SUB // 8
LANES = 128
TW = -(-(B + SUB) // LANES)
WIDE = TW * LANES

LAST = (((1,), (1,)), ((), ()))
FIRST = (((0,), (0,)), ((), ()))
PLAIN = (((1,), (0,)), ((), ()))


def dot(a, b, dims=PLAIN):
    return lax.dot_general(a, b, dims, preferred_element_type=jnp.float32)


def split_bf16(x):
    hi = x.astype(jnp.bfloat16)
    lo = (x - hi.astype(jnp.float32)).astype(jnp.bfloat16)
    return hi, lo


def dot3(a, b, dims=PLAIN):
    ah, al = split_bf16(a)
    bh, bl = split_bf16(b)
    return dot(ah, bh, dims) + (dot(ah, bl, dims) + dot(al, bh, dims))


def lanes(x):
    return jnp.broadcast_to(x, (8, LANES))


def factor_panel(s_ref, p_ref):
    sub_iota = lax.broadcasted_iota(jnp.int32, (8, LANES), 0)
    rows = [[s_ref[8 * g : 8 * g + 8, LANES * t : LANES * (t + 1)] for t in range(TW)] for g in range(G8)]
    for b in range(G8):
        c0 = 8 * b
        col = [[lanes(rows[g][0][:, c0 + j : c0 + j + 1]) for j in range(8)] for g in range(b, G8)]
        e = [[lanes(col[0][j][i : i + 1, :]) for j in range(i + 1)] for i in range(8)]
        r = []
        l = [[None] * 8 for _ in range(8)]
        for j in range(8):
            rj = lax.rsqrt(e[j][j])
            r.append(rj)
            for i in range(j + 1, 8):
                l[i][j] = e[i][j] * rj
            for i in range(j + 1, 8):
                for k in range(j + 1, i + 1):
                    e[i][k] = e[i][k] - l[i][j] * l[k][j]
        y = []
        for i in range(8):
            yi = []
            for t in range(TW):
                v = lanes(rows[b][t][i : i + 1, :])
                for j in range(i):
                    v = v - l[i][j] * y[j][t]
                yi.append(v * r[i])
            y.append(yi)
        for t in range(TW):
            u = y[0][t]
            for i in range(1, 8):
                u = jnp.where(sub_iota == i, y[i][t], u)
            p_ref[8 * b : 8 * b + 8, LANES * t : LANES * (t + 1)] = u
        for g in range(b + 1, G8):
            cs = []
            for j in range(8):
                v = col[g - b][j]
                for k in range(j):
                    v = v - l[j][k] * cs[k]
                cs.append(v * r[j])
            for t in range(TW):
                v = rows[g][t]
                for j in range(8):
                    v = v - cs[j] * y[j][t]
                rows[g][t] = v


MESH = pl.DeviceIdType.MESH
CHUNKS = 8
LAG = 2
CODE = 32767.0
TINY = 1e-37
STEPS = PANELS * (B // SUB)


def ones_at(shape, first):
    row = lax.broadcasted_iota(jnp.int32, shape, 0)
    lane = lax.broadcasted_iota(jnp.int32, shape, 1)
    return jnp.where((lane - first == row) & (lane < first + SUB), 1.0, 0.0)


def factor_step(k, s_ref, p_ref):
    p = p_ref.at[k]
    factor_panel(s_ref, p)
    keep = B - SUB
    rolled = pltpu.roll(p[:, :B], keep, 1)
    lane = lax.broadcasted_iota(jnp.int32, (SUB, B), 1)
    rolled = jnp.where(lane < keep, rolled, 0.0)
    update = dot3(rolled, p[...], FIRST)
    left = pltpu.roll(s_ref[SUB:, :] - update[:keep], WIDE - SUB, 1)
    lane = lax.broadcasted_iota(jnp.int32, (keep, WIDE), 1)
    s_ref[:keep, :] = jnp.where(lane < B, left, ones_at((keep, WIDE), B))


def remote(src, dst, send, recv, where):
    return pltpu.make_async_remote_copy(
        src_ref=src, dst_ref=dst, send_sem=send, recv_sem=recv, device_id=where, device_id_type=MESH
    )


def rows_at(start, count):
    return pl.ds(pl.multiple_of(start, count), count)


class Spread:
    def __init__(self, buf, out, hop, send, recv, base, size, bits, cross=None):
        self.buf, self.out, self.hop, self.send, self.recv = buf, out, hop, send, recv
        self.cross = cross
        self.stages = []
        start, hop_at = base, 0
        for axis, bit, whole in bits:
            me = lax.axis_index(axis)
            digit = lax.rem(me // bit, 2)
            where = {axis: me + bit - 2 * bit * digit}
            if whole:
                count, give = size, start
            else:
                count = size // 2
                give, start = start + (1 - digit) * count, start + digit * count
            self.stages.append((where, give, start, count, hop_at, whole))
            hop_at += count
            size = count
        self.last, self.size = start, size

    def down(self, i):
        where, give, keep, count, at, _ = self.stages[i]
        return remote(self.buf.at[rows_at(give, count)], self.hop.at[pl.ds(at, count)], self.send.at[i], self.recv.at[i], where)

    def up(self, i):
        where, give, keep, count, at, _ = self.stages[i]
        n = len(self.stages) + i
        rows = self.out.at[rows_at(keep, count)]
        return remote(rows, rows, self.send.at[n], self.recv.at[n], where)

    def add(self, i):
        self.down(i).wait()
        _, _, keep, count, at, _ = self.stages[i]
        rows = rows_at(keep, count)
        to = self.out if i == len(self.stages) - 1 and self.cross is None else self.buf
        to[rows] = self.buf[rows] + self.hop[pl.ds(at, count)]

    def over(self, shift):
        land, send, recv, nc = self.cross
        to = lax.rem(lax.axis_index("col") + shift, nc)
        part = pl.ds((shift - 1) * self.size, self.size)
        return remote(
            self.buf.at[rows_at(self.last, self.size)], land.at[part], send.at[shift], recv.at[shift], {"col": to}
        )

    def send_over(self):
        for shift in range(1, self.cross[3]):
            self.over(shift).start()

    def add_over(self):
        rows = rows_at(self.last, self.size)
        total = self.buf[rows]
        for shift in range(1, self.cross[3]):
            self.over(shift).wait()
            total = total + self.cross[0][pl.ds((shift - 1) * self.size, self.size)]
        self.out[rows] = total

    def acts(self):
        count = len(self.stages)
        ends = [functools.partial(self.add, i) for i in range(count)]
        starts = [lambda i=i: self.down(i).start() for i in range(count)]
        if self.cross is not None:
            starts.append(self.send_over)
            ends.append(self.add_over)
        for i in reversed(range(count)):
            if not self.stages[i][5]:
                starts.append(lambda i=i: self.up(i).start())
                ends.append(lambda i=i: self.up(i).wait())
        acts = [starts[0]]
        acts += [lambda a=a, b=b: (a(), b()) for a, b in zip(ends, starts[1:])]
        return acts + [ends[-1]]


def bits_of(axis, size, whole=False):
    return [(axis, 1 << b, whole) for b in range(size.bit_length() - 1)]


def spread_pair(buf, out, hop, send, recv, size, nr, cross=None):
    bits = bits_of("row", nr)
    orders = [bits, bits[:1] + bits[:0:-1]]
    half = size // 2
    both = []
    for part in range(2):
        over = None if cross is None else tuple(ref.at[part] for ref in cross[:3]) + (cross[3],)
        both.append(
            Spread(buf, out, hop.at[part], send.at[part], recv.at[part], part * half, half, orders[part], over).acts()
        )
    return [lambda a=a, b=b: (a(), b()) for a, b in zip(*both)]


class Direct:
    def __init__(self, nr, nc, buf, out, land, crossland, sends, recvs):
        self.nr, self.nc = nr, nc
        self.buf, self.out, self.land, self.crossland = buf, out, land, crossland
        self.sends, self.recvs = sends, recvs
        self.r, self.c = lax.axis_index("row"), lax.axis_index("col")
        self.size = buf.shape[0] // nr
        self.mine = rows_at(self.r * self.size, self.size)

    def part(self, shift):
        return pl.ds((shift - 1) * self.size, self.size)

    def down(self, shift):
        to = lax.rem(self.r + shift, self.nr)
        return remote(
            self.buf.at[rows_at(to * self.size, self.size)], self.land.at[self.part(shift)],
            self.sends.at[0], self.recvs.at[0], {"row": to},
        )

    def over(self, shift):
        return remote(
            self.buf.at[self.mine], self.crossland.at[self.part(shift)],
            self.sends.at[1], self.recvs.at[1], {"col": lax.rem(self.c + shift, self.nc)},
        )

    def up(self, shift):
        rows = self.out.at[self.mine]
        return remote(rows, rows, self.sends.at[2], self.recvs.at[2], {"row": lax.rem(self.r + shift, self.nr)})

    def begin(self):
        for shift in range(1, self.nr):
            self.down(shift).start()

    def all_of(self, group, count, land):
        part = pl.ds(0, (count - 1) * self.size)
        remote(self.buf.at[part], land.at[part], self.sends.at[group], self.recvs.at[group], {"row": self.r}).wait()

    def total(self, group, count, land):
        self.all_of(group, count, land)
        value = self.buf[self.mine]
        for shift in range(1, count):
            value = value + land[self.part(shift)]
        return value

    def cross(self):
        self.buf[self.mine] = self.total(0, self.nr, self.land)
        for shift in range(1, self.nc):
            self.over(shift).start()

    def crossed(self):
        self.out[self.mine] = self.total(1, self.nc, self.crossland)
        self.raise_all()

    def flat(self):
        self.out[self.mine] = self.total(0, self.nr, self.land)
        self.raise_all()

    def raise_all(self):
        for shift in range(1, self.nr):
            self.up(shift).start()

    def end(self):
        self.all_of(2, self.nr, self.out)


def direct_scratch(size, width, nr, nc):
    part = size // nr
    dma = pltpu.SemaphoreType.DMA
    return [
        pltpu.VMEM(((nr - 1) * part, width), jnp.float32),
        pltpu.VMEM(((nc - 1) * part, width), jnp.float32),
        dma((3,)), dma((3,)),
    ]


def spread_scratch(size, width, dtype, nr, nc=None):
    half, n = size // 2, nr.bit_length() - 1
    dma = pltpu.SemaphoreType.DMA
    out = [pltpu.VMEM((2, half, width), dtype), dma((2, 2 * n)), dma((2, 2 * n))]
    if nc is not None:
        out += [pltpu.VMEM((2, (nc - 1) * (half // nr), width), dtype), dma((2, nc)), dma((2, nc))]
    return out


def choose(owner, wanted, value, otherwise):
    return jnp.where(jnp.full(value.shape, owner, jnp.int32) == wanted, value, otherwise)


def encode(x, top):
    part = jnp.sqrt(jnp.abs(x) * (1.0 / jnp.maximum(top, TINY)))
    code = (part * CODE + 0.5).astype(jnp.int32)
    return jnp.where(x < 0.0, -code, code).astype(jnp.int16)


def decode(code, top):
    part = code.astype(jnp.int32).astype(jnp.float32) * (1.0 / CODE)
    return part * jnp.abs(part) * top


def largest(x):
    top = jnp.max(jnp.abs(x), axis=0, keepdims=True)
    return jnp.max(top, axis=1, keepdims=True)


def front_kernel(
    nr, nc, own_ref, idx_ref, cov, inn,
    cols_o, tops_o, rowp_o, v_o, vs_o, f_o, z_o, x_o,
    w, wsem, vin, vinsem, outsem, zsem, fsem,
    cbuf, cols, rin, lin, rtx, ltx, rs, rr, ls, lr, tops, topland, topsend, toprecv, topsum,
    rbuf, rowp, rhop, rsend, rrecv,
    d0buf, d0pack, d0, d0land, d0over, d0s, d0r,
    d1buf, d1, d1hop, d1send, d1recv, d1over, d1s, d1r,
    vsbuf, vs, vsland, vsover, vss, vsr,
    vt, vst, vq, v, vtop, vtst, vtq, v1send, v1recv, v2send, v2recv, t1send, t1recv, t2send, t2recv,
    a_ref, s_ref, p_ref, u_ref, f_ref, z_ref, x_ref, picks,
):
    r = lax.axis_index("row")
    c = lax.axis_index("col")
    rows, width = w.shape
    rb, cb = rows // B, width // B
    load = pltpu.make_async_copy(cov, w, wsem)
    vload = pltpu.make_async_copy(inn, vin, vinsem)
    vload.start()
    load.start()
    barrier = pltpu.get_barrier_semaphore()
    for shift in range(1, nr):
        pl.semaphore_signal(barrier, inc=1, device_id={"row": lax.rem(r + shift, nr)}, device_id_type=MESH)
    for shift in range(1, nc):
        pl.semaphore_signal(barrier, inc=1, device_id={"col": lax.rem(c + shift, nc)}, device_id_type=MESH)

    part_p, iw = inn.shape[0], inn.shape[2]
    ratio = nr // nc
    h = ratio * part_p

    def first_stop(shift):
        to = {"row": lax.rem(r + shift, nr)}
        return (
            remote(vt.at[lax.rem(r + shift, nr)], vst.at[rows_at(r * part_p, part_p)], v1send.at[shift], v1recv.at[shift], to),
            remote(vtop, vtst.at[rows_at(r * 8, 8)], t1send.at[shift], t1recv.at[shift], to),
        )

    def second_stop(shift):
        at = lax.rem(c + shift, nc)
        to = {"col": at}
        return (
            remote(vst.at[rows_at(at * h, h)], vq.at[:, rows_at(c * iw, iw)], v2send.at[shift], v2recv.at[shift], to),
            remote(
                vtst.at[rows_at(at * ratio * 8, ratio * 8)], vtq.at[rows_at(c * ratio * 8, ratio * 8)],
                t2send.at[shift], t2recv.at[shift], to,
            ),
        )

    def code_innovations():
        vload.wait()
        top = largest(vin[:, 0, :])
        for group in range(1, nr):
            top = jnp.maximum(top, largest(vin[:, group, :]))
        vtop[...] = jnp.broadcast_to(top, vtop.shape)
        for group in range(nr):
            vt[group] = encode(vin[:, group, :], top)

    g = idx_ref[0]
    d0buf[...] = jnp.zeros_like(d0buf)
    d1buf[...] = jnp.zeros_like(d1buf)
    zero = jnp.zeros((B, B), jnp.float32)

    @pl.when(c == 0)
    def _():
        rin[...] = jnp.zeros_like(rin)

    @pl.when(c == nc - 1)
    def _():
        lin[...] = jnp.zeros_like(lin)

    with jax.named_scope("load"):
        load.wait()

    def pick_cols(i, carry):
        span = rows_at(i * B, B)
        own = own_ref[r * rb + i]
        picked = []
        for t in range(PANELS):
            tile = zero
            for j in range(cb):
                tile = choose(own_ref[c * cb + j], g + t, w[span, j * B : (j + 1) * B], tile)
            picks[span, t * B : (t + 1) * B] = tile
            picked.append(tile)
        d0buf[...] = choose(own, g, picked[0], d0buf[...])
        d1buf[:B] = choose(own, g + 1, picked[0], d1buf[:B])
        d1buf[B:] = choose(own, g + 1, picked[1], d1buf[B:])
        return carry

    def code_cols(i, carry):
        span = rows_at(i * B, B)
        for t in range(PANELS):
            tile = picks[span, t * B : (t + 1) * B]
            top = largest(tile)
            tops[pl.ds(i * PANELS + t, 1), :] = jnp.broadcast_to(top, (1, LANES))
            cbuf[span, t * B : (t + 1) * B] = encode(tile, top)
        return carry

    with jax.named_scope("columns"):
        lax.fori_loop(0, rb, pick_cols, 0)
    H = B // 2
    d0pack[: H // 2, :H] = d0buf[: H // 2, :H]
    d0pack[: H // 2, H:] = d0buf[H // 2 : H, :H]
    d0pack[H // 2 : H // 2 + H, :] = d0buf[H:, :]
    if d0pack.shape[0] > H // 2 + H:
        d0pack[H // 2 + H :, :] = jnp.zeros((d0pack.shape[0] - H // 2 - H, B), jnp.float32)
    first = Direct(nr, nc, d0pack, d0, d0land, d0over, d0s, d0r)
    second = spread_pair(d1buf, d1, d1hop, d1send, d1recv, 2 * B, nr, (d1over, d1s, d1r, nc))
    with jax.named_scope("barrier"):
        pl.semaphore_wait(barrier, nr - 1 + nc - 1)
    first.begin()
    second[0]()
    with jax.named_scope("code"):
        lax.fori_loop(0, rb, code_cols, 0)

    size = rows // CHUNKS

    def chunk(q):
        return rows_at(q * size, size)

    def right(src, q):
        return remote(src.at[chunk(q)], rin.at[chunk(q)], rs, rr.at[q], {"col": c + 1})

    def left(src, q):
        return remote(src.at[chunk(q)], lin.at[chunk(q)], ls, lr.at[q], {"col": c - 1})

    def push(begin, end):
        def one(q, carry):
            @pl.when(c == 0)
            def _():
                right(cbuf, q).start()

            @pl.when(c == nc - 1)
            def _():
                left(cbuf, q).start()

            return carry

        lax.fori_loop(begin, end, one, 0)

    def relay(t, carry):
        q = t - LAG * (c - 1)

        @pl.when((q >= 0) & (q < CHUNKS) & (c > 0))
        def _():
            right(cbuf, q).wait_recv()

            @pl.when(c < nc - 1)
            def _():
                rtx[chunk(q)] = rin[chunk(q)] + cbuf[chunk(q)]
                right(rtx, q).start()

        p = t - LAG * (nc - 2 - c)

        @pl.when((p >= 0) & (p < CHUNKS) & (c < nc - 1))
        def _():
            left(cbuf, p).wait_recv()

            @pl.when(c > 0)
            def _():
                ltx[chunk(p)] = lin[chunk(p)] + cbuf[chunk(p)]
                left(ltx, p).start()

        return carry

    def share_top(shift):
        count = tops.shape[0]
        return remote(
            tops, topland.at[pl.ds((shift - 1) * count, count)], topsend.at[shift], toprecv.at[shift],
            {"col": lax.rem(c + shift, nc)},
        )

    def fill_rows(i, carry):
        span = rows_at(i * B, B)
        for t in range(PANELS):
            tile = zero
            for k in range(rb):
                tile = choose(own_ref[r * rb + k], g + t, w[k * B : (k + 1) * B, span], tile)
            rbuf[t * B : (t + 1) * B, span] = tile.astype(jnp.bfloat16)
        return carry

    act_rows = spread_pair(rbuf, rowp, rhop, rsend, rrecv, PANELS * B, nr)

    def leave():
        for shift in range(1, nr):
            for copy in first_stop(shift):
                copy.start()
        vst[rows_at(r * part_p, part_p)] = vt[r]
        vtst[rows_at(r * 8, 8)] = vtop[...]
        for shift in range(1, nc):
            share_top(shift).start()

    def pass_on():
        for shift in range(1, nr):
            for copy in first_stop(shift):
                copy.wait()
        for shift in range(1, nc):
            for copy in second_stop(shift):
                copy.start()
        vq[:, rows_at(c * iw, iw)] = vst[rows_at(c * h, h)]
        vtq[rows_at(c * ratio * 8, ratio * 8)] = vtst[rows_at(c * ratio * 8, ratio * 8)]

    early = 0

    def relays(count):
        nonlocal early
        lax.fori_loop(early, early + count, relay, 0)
        early += count

    with jax.named_scope("first1"):
        push(0, 1)
        first.cross()
        second[1]()
    with jax.named_scope("innovations"):
        code_innovations()
        push(1, 2)
    with jax.named_scope("rows"):
        lax.fori_loop(0, cb, fill_rows, 0)
        act_rows[0]()
    with jax.named_scope("early1"):
        relays(1)
        second[2]()
    with jax.named_scope("first2"):
        first.crossed()
        push(2, 3)
    with jax.named_scope("second1"):
        second[3]()
        push(3, 5)
    with jax.named_scope("early2"):
        relays(1)
    with jax.named_scope("first3"):
        first.end()
    with jax.named_scope("early3"):
        act_rows[1]()
        leave()
        push(5, CHUNKS)
        relays(1)

    outs = [
        pltpu.make_async_copy(src, dst, outsem.at[i])
        for i, (src, dst) in enumerate(
            [(rowp, rowp_o), (v, v_o), (vs, vs_o), (x_ref, x_o), (cols, cols_o), (topsum, tops_o)]
        )
    ]
    heads = Direct(nr, nc, vsbuf, vs, vsland, vsover, vss, vsr)

    def arrived():
        for shift in range(1, nc):
            for copy in second_stop(shift):
                copy.wait()
        for b in range(nc):
            for a in range(ratio):
                at, block = slice(a * part_p, (a + 1) * part_p), slice(b * iw, (b + 1) * iw)
                n = (b * ratio + a) * 8
                v[at, block] = decode(vq[at, block], vtq[n : n + 1, :1])
        outs[1].start()
        for t in range(PANELS):
            part = jnp.zeros((h, B), jnp.float32)
            for k in range(rb):
                part = choose(own_ref[r * rb + k], g + t, v[:, k * B : (k + 1) * B], part)
            vsbuf[t * h : (t + 1) * h] = part
        heads.begin()

    events = [[] for _ in range(STEPS)]
    half = STEPS // PANELS
    later = second[4:]
    for i, act in enumerate(later):
        events[i * half // len(later)].append(act)
    events[1].append(pass_on)
    later = act_rows[2:-1]
    for i, act in enumerate(later):
        events[2 + i * (STEPS - 2) // len(later)].append(act)
    events[half].append(arrived)
    events[half + 2].append(heads.flat)
    total = CHUNKS + LAG * (nc - 2)
    each = min(1, -(-(total - early) // STEPS))
    row_i = lax.broadcasted_iota(jnp.int32, (B, B), 0)
    col_i = lax.broadcasted_iota(jnp.int32, (B, B), 1)
    a_ref[: H // 2, :H] = d0[: H // 2, :H]
    a_ref[H // 2 : H, :H] = d0[: H // 2, H:]
    a_ref[H:, :] = d0[H // 2 : H // 2 + H, :]
    a_ref[:H, H:] = d0[H // 2 : H // 2 + H, :H].T

    def panel(turn, carry):
        s_ref[:, :B] = a_ref[...]
        s_ref[:, B:] = ones_at((B, WIDE - B), 0)

        def step(k, carry):
            now = turn * (B // SUB) + k
            with jax.named_scope("factor"):
                factor_step(k, s_ref, p_ref)
            at = early + now * each
            with jax.named_scope("relay"):
                lax.fori_loop(at, at + each, relay, 0)
            for i, acts in enumerate(events):
                if acts:
                    @pl.when(now == i)
                    def _():
                        for m, act in enumerate(acts):
                            with jax.named_scope(f"event{i}_{m}"):
                                act()
            return carry

        lax.fori_loop(0, B // SUB, step, 0)
        for k in range(B // SUB):
            span = slice(k * SUB, (k + 1) * SUB)
            u_ref[span, :] = pltpu.roll(p_ref[k, :, :B], k * SUB, 1) if k else p_ref[k, :, :B]
            z_ref[turn, span, :] = pltpu.roll(p_ref[k], WIDE - B + k * SUB, 1)[:, :B]
        z_ref[turn] = jnp.where(row_i >= col_i, z_ref[turn], 0.0)
        f_ref[turn] = jnp.where(row_i >= col_i, u_ref[...].T, 0.0)
        pltpu.make_async_copy(z_ref.at[turn], z_o.at[turn], zsem.at[turn]).start()
        pltpu.make_async_copy(f_ref.at[turn], f_o.at[turn], fsem.at[turn]).start()

        @pl.when(turn == 0)
        def _():
            low = dot3(d1[:B], z_ref[0], LAST)
            half = low.astype(jnp.bfloat16)
            x_ref[...] = half
            a_ref[...] = d1[B:] - dot(half, half, LAST)

        return carry

    lax.fori_loop(0, PANELS, panel, 0)
    outs[3].start()
    with jax.named_scope("late"):
        lax.fori_loop(early + STEPS * each, total, relay, 0)
    with jax.named_scope("rowend"):
        act_rows[-1]()
        outs[0].start()
    with jax.named_scope("headend"):
        heads.end()
        outs[2].start()

    with jax.named_scope("sum"):
        def add(q, carry):
            cols[chunk(q)] = cbuf[chunk(q)] + (rin[chunk(q)] + lin[chunk(q)])
            return carry

        lax.fori_loop(0, CHUNKS, add, 0)
        outs[4].start()
        count = tops.shape[0]
        top = tops[...]
        for shift in range(1, nc):
            share_top(shift).wait()
            top = top + topland[pl.ds((shift - 1) * count, count)]
        topsum[...] = top
        outs[5].start()

    with jax.named_scope("sent"):
        @pl.when(c < nc - 1)
        def _():
            remote(cbuf, rin, rs, rr.at[0], {"col": c + 1}).wait_send()

        @pl.when(c > 0)
        def _():
            remote(cbuf, lin, ls, lr.at[0], {"col": c - 1}).wait_send()

    with jax.named_scope("written"):
        for turn in range(PANELS):
            pltpu.make_async_copy(z_ref.at[turn], z_o.at[turn], zsem.at[turn]).wait()
            pltpu.make_async_copy(f_ref.at[turn], f_o.at[turn], fsem.at[turn]).wait()
        for out in outs:
            out.wait()


def front(nr, nc, owner, index, cov, inn):
    rows, width = cov.shape
    part_p, groups, iw = inn.shape
    ratio = nr // nc
    h = ratio * part_p
    f32, bf16, i16 = jnp.float32, jnp.bfloat16, jnp.int16
    smem = pl.BlockSpec(memory_space=pltpu.SMEM)
    anywhere = pl.BlockSpec(memory_space=pl.ANY)
    vmem = pltpu.VMEM
    dma = pltpu.SemaphoreType.DMA
    both = PANELS * B
    count = PANELS * (rows // B)
    scratch = [vmem((rows, width), f32), dma, vmem(inn.shape, f32), dma, dma((6,)), dma((PANELS,)), dma((PANELS,))]
    scratch += [vmem((rows, both), i16)] * 6 + [dma, dma((CHUNKS,))] * 2
    scratch += [vmem((count, LANES), f32), vmem(((nc - 1) * count, LANES), f32), dma((nc,)), dma((nc,)), vmem((count, LANES), f32)]
    scratch += [vmem((both, width), bf16)] * 2 + spread_scratch(both, width, bf16, nr)
    packed = nr * (-(-(B // 4 * 3) // (8 * nr)) * 8)
    scratch += [vmem((B, B), f32)] + [vmem((packed, B), f32)] * 2 + direct_scratch(packed, B, nr, nc)
    scratch += [vmem((2 * B, B), f32)] * 2 + spread_scratch(2 * B, B, f32, nr, nc)
    scratch += [vmem((PANELS * h, B), f32)] * 2 + direct_scratch(PANELS * h, B, nr, nc)
    scratch += [vmem((groups, part_p, iw), i16), vmem((nr * part_p, iw), i16), vmem((h, nc * iw), i16), vmem((h, nc * iw), f32)]
    scratch += [vmem((8, LANES), f32), vmem((nr * 8, LANES), f32), vmem((nr * 8, LANES), f32)]
    scratch += [dma((nr,)), dma((nr,)), dma((nc,)), dma((nc,))] * 2
    scratch += [vmem((B, B), f32), vmem((B, WIDE), f32), vmem((B // SUB, SUB, WIDE), f32), vmem((B, B), f32)]
    scratch += [vmem((PANELS, B, B), f32)] * 2 + [vmem((B, B), bf16), vmem((rows, both), f32)]
    return pl.pallas_call(
        functools.partial(front_kernel, nr, nc),
        out_shape=(
            jax.ShapeDtypeStruct((rows, both), i16),
            jax.ShapeDtypeStruct((count, LANES), f32),
            jax.ShapeDtypeStruct((both, width), bf16),
            jax.ShapeDtypeStruct((h, nc * iw), f32),
            jax.ShapeDtypeStruct((PANELS * h, B), f32),
            jax.ShapeDtypeStruct((PANELS, B, B), f32),
            jax.ShapeDtypeStruct((PANELS, B, B), f32),
            jax.ShapeDtypeStruct((B, B), bf16),
        ),
        in_specs=[smem, smem, anywhere, anywhere],
        out_specs=(anywhere,) * 8,
        scratch_shapes=scratch,
        compiler_params=pltpu.CompilerParams(
            collective_id=0, has_side_effects=True, vmem_limit_bytes=56 * 1024 * 1024
        ),
    )(owner, index, cov, inn)


def tail_kernel(
    own_ref, idx_ref, w_any, cols_any, tops_any, rowp_any, f_any, z_any, x_any, vs_any, v_any,
    o_any, vout_any,
    w_ref, o_ref, cols_ref, tops_ref, rowp_ref, f_ref, z_ref, x_ref, vs_ref, v_ref, vout_ref, q_ref, half_ref,
    insem, wsem, osem, vsem, *, rb, cb,
):
    g = idx_ref[0]
    row0 = lax.axis_index("row") * rb
    col0 = lax.axis_index("col") * cb
    h = v_ref.shape[0]
    pairs = [
        (z_any, z_ref), (x_any, x_ref), (rowp_any, rowp_ref), (tops_any, tops_ref), (cols_any, cols_ref),
        (vs_any, vs_ref), (v_any, v_ref), (f_any, f_ref),
    ]
    ins = [pltpu.make_async_copy(src, dst, insem.at[i]) for i, (src, dst) in enumerate(pairs)]

    def stripe_in(j):
        span = rows_at(j * B, B)
        return pltpu.make_async_copy(w_any.at[:, span], w_ref.at[:, span], wsem.at[j])

    def stripe_out(j):
        span = rows_at(j * B, B)
        return pltpu.make_async_copy(o_ref.at[:, span], o_any.at[:, span], osem.at[j])

    for copy in ins[:5]:
        copy.start()
    for copy in ins[:3]:
        copy.wait()
    for j in range(cb):
        stripe_in(j).start()
    for copy in ins[5:]:
        copy.start()

    with jax.named_scope("qpanels"):
        x = x_ref[...]
        zh0, zl0 = split_bf16(z_ref[0])
        zh1, zl1 = split_bf16(z_ref[1])
        for k in range(cb):
            span = slice(k * B, (k + 1) * B)
            own = own_ref[col0 + k]
            q0 = dot(zh0, rowp_ref[:B, span]) + dot(zl0, rowp_ref[:B, span])
            q0 = jnp.where(own > g, q0, 0.0).astype(jnp.bfloat16)
            r1 = (rowp_ref[B:, span].astype(jnp.float32) - dot(x, q0)).astype(jnp.bfloat16)
            q1 = dot(zh1, r1) + dot(zl1, r1)
            q_ref[:B, span] = q0
            q_ref[B:, span] = jnp.where(own > g + 1, q1, 0.0).astype(jnp.bfloat16)

    for copy in ins[3:5]:
        copy.wait()

    with jax.named_scope("panels"):
        for i in range(rb):
            span = slice(i * B, (i + 1) * B)
            own = own_ref[row0 + i]
            c0 = decode(cols_ref[span, :B], tops_ref[PANELS * i : PANELS * i + 1, :1])
            p0 = dot3(c0, z_ref[0], LAST)
            h0 = jnp.where(own > g, p0, 0.0).astype(jnp.bfloat16)
            c1 = decode(cols_ref[span, B:], tops_ref[PANELS * i + 1 : PANELS * i + 2, :1]) - dot(h0, x, LAST)
            p1 = dot3(c1, z_ref[1], LAST)
            half_ref[span, :B] = h0
            half_ref[span, B:] = jnp.where(own > g + 1, p1, 0.0).astype(jnp.bfloat16)

    for copy in ins[5:]:
        copy.wait()

    def stripe(j, carry):
        span = rows_at(j * B, B)
        cown = own_ref[col0 + j]
        stripe_in(j).wait()
        with jax.named_scope("update"):
            o_ref[:, span] = w_ref[:, span] - dot(half_ref[...], q_ref[:, span])

        @pl.when(cown > g)
        def _():
            for i in range(rb):
                rown = own_ref[row0 + i]

                @pl.when((rown == g) | ((rown == g + 1) & (cown > g + 1)))
                def _():
                    o_ref[i * B : (i + 1) * B, span] = jnp.zeros((B, B), jnp.float32)

        for turn in range(PANELS):
            @pl.when(cown == g + turn)
            def _():
                for i in range(rb):
                    part = slice(i * B, (i + 1) * B)
                    rown = own_ref[row0 + i]

                    @pl.when(rown > g + turn)
                    def _():
                        left = w_ref[part, span]
                        if turn:
                            left = left - dot(half_ref[part, :B], x_ref[...], LAST)
                        o_ref[part, span] = dot3(left, z_ref[turn], LAST)

                    @pl.when(rown == g + turn)
                    def _():
                        o_ref[part, span] = f_ref[turn]

        stripe_out(j).start()
        return carry

    lax.fori_loop(0, cb, stripe, 0)

    with jax.named_scope("solve"):
        w0 = dot3(vs_ref[:h], z_ref[0], LAST)
        w0h = w0.astype(jnp.bfloat16)
        w1 = dot3(vs_ref[h:] - dot(w0h, x, LAST), z_ref[1], LAST)
        w1h = w1.astype(jnp.bfloat16)
        for i in range(rb):
            span = slice(i * B, (i + 1) * B)
            own = own_ref[row0 + i]
            new = v_ref[:, span] - (dot(w0h, half_ref[span, :B], LAST) + dot(w1h, half_ref[span, B:], LAST))
            new = jnp.where(own == g, w0, new)
            vout_ref[:, span] = jnp.where(own == g + 1, w1, new)
        done = pltpu.make_async_copy(vout_ref, vout_any, vsem)
        done.start()

    with jax.named_scope("drain"):
        lax.fori_loop(0, cb, lambda j, k: (stripe_out(j).wait(), k)[1], 0)
        done.wait()


def tail(owner, index, w, cols, tops, rowp, factors, z, x, vs, v):
    rows, width = w.shape
    cb = width // B
    smem = pl.BlockSpec(memory_space=pltpu.SMEM)
    anywhere = pl.BlockSpec(memory_space=pl.ANY)
    dma = pltpu.SemaphoreType.DMA
    arrays = [w, w, cols, tops, rowp, factors, z, x, vs, v, v]
    return pl.pallas_call(
        functools.partial(tail_kernel, rb=rows // B, cb=cb),
        in_specs=[smem, smem] + [anywhere] * 9,
        out_specs=[anywhere] * 2,
        scratch_shapes=[pltpu.VMEM(a.shape, a.dtype) for a in arrays]
        + [pltpu.VMEM((2 * B, width), jnp.bfloat16), pltpu.VMEM((rows, 2 * B), jnp.bfloat16)]
        + [dma((8,)), dma((cb,)), dma((cb,)), dma],
        out_shape=(jax.ShapeDtypeStruct(w.shape, w.dtype), jax.ShapeDtypeStruct(v.shape, v.dtype)),
        compiler_params=pltpu.CompilerParams(vmem_limit_bytes=60 * 1024 * 1024),
    )(owner, index, w, cols, tops, rowp, factors, z, x, vs, v)


def per_device(covariance, innovations, block_owner, panel_index):
    nr, nc = lax.axis_size("row"), lax.axis_size("col")
    cols, tops, rowp, v, vs, factors, z, x = front(nr, nc, block_owner, panel_index, covariance, innovations)
    return tail(block_owner, panel_index, covariance, cols, tops, rowp, factors, z, x, vs, v)


def solution(mesh):
    placed = (P("row", "col"), P("row", None, "col"), P(), P())
    return jax.shard_map(
        per_device,
        mesh=mesh,
        in_specs=placed,
        out_specs=(P("row", "col"), P("col", "row")),
        check_vma=False,
    )
```

```python
import functools

import jax
import jax.numpy as jnp
from jax import lax
from jax.experimental import pallas as pl
from jax.experimental.pallas import tpu as pltpu
from jax.sharding import PartitionSpec as P

B = 256
PANELS = 2
SUB = 64
G8 = SUB // 8
LANES = 128
TW = -(-(B + SUB) // LANES)
WIDE = TW * LANES

LAST = (((1,), (1,)), ((), ()))
FIRST = (((0,), (0,)), ((), ()))
PLAIN = (((1,), (0,)), ((), ()))


def dot(a, b, dims=PLAIN):
    return lax.dot_general(a, b, dims, preferred_element_type=jnp.float32)


def split_bf16(x):
    hi = x.astype(jnp.bfloat16)
    lo = (x - hi.astype(jnp.float32)).astype(jnp.bfloat16)
    return hi, lo


def dot3(a, b, dims=PLAIN):
    ah, al = split_bf16(a)
    bh, bl = split_bf16(b)
    return dot(ah, bh, dims) + (dot(ah, bl, dims) + dot(al, bh, dims))


def lanes(x):
    return jnp.broadcast_to(x, (8, LANES))


def factor_panel(s_ref, p_ref):
    sub_iota = lax.broadcasted_iota(jnp.int32, (8, LANES), 0)
    rows = [[s_ref[8 * g : 8 * g + 8, LANES * t : LANES * (t + 1)] for t in range(TW)] for g in range(G8)]
    for b in range(G8):
        c0 = 8 * b
        col = [[lanes(rows[g][0][:, c0 + j : c0 + j + 1]) for j in range(8)] for g in range(b, G8)]
        e = [[lanes(col[0][j][i : i + 1, :]) for j in range(i + 1)] for i in range(8)]
        r = []
        l = [[None] * 8 for _ in range(8)]
        for j in range(8):
            rj = lax.rsqrt(e[j][j])
            r.append(rj)
            for i in range(j + 1, 8):
                l[i][j] = e[i][j] * rj
            for i in range(j + 1, 8):
                for k in range(j + 1, i + 1):
                    e[i][k] = e[i][k] - l[i][j] * l[k][j]
        y = []
        for i in range(8):
            yi = []
            for t in range(TW):
                v = lanes(rows[b][t][i : i + 1, :])
                for j in range(i):
                    v = v - l[i][j] * y[j][t]
                yi.append(v * r[i])
            y.append(yi)
        for t in range(TW):
            u = y[0][t]
            for i in range(1, 8):
                u = jnp.where(sub_iota == i, y[i][t], u)
            p_ref[8 * b : 8 * b + 8, LANES * t : LANES * (t + 1)] = u
        for g in range(b + 1, G8):
            cs = []
            for j in range(8):
                v = col[g - b][j]
                for k in range(j):
                    v = v - l[j][k] * cs[k]
                cs.append(v * r[j])
            for t in range(TW):
                v = rows[g][t]
                for j in range(8):
                    v = v - cs[j] * y[j][t]
                rows[g][t] = v


MESH = pl.DeviceIdType.MESH
CHUNKS = 8
LAG = 2
CODE = 32767.0
TINY = 1e-37
STEPS = PANELS * (B // SUB)


def ones_at(shape, first):
    row = lax.broadcasted_iota(jnp.int32, shape, 0)
    lane = lax.broadcasted_iota(jnp.int32, shape, 1)
    return jnp.where((lane - first == row) & (lane < first + SUB), 1.0, 0.0)


def factor_step(k, s_ref, p_ref):
    p = p_ref.at[k]
    factor_panel(s_ref, p)
    keep = B - SUB
    rolled = pltpu.roll(p[:, :B], keep, 1)
    lane = lax.broadcasted_iota(jnp.int32, (SUB, B), 1)
    rolled = jnp.where(lane < keep, rolled, 0.0)
    update = dot3(rolled, p[...], FIRST)
    left = pltpu.roll(s_ref[SUB:, :] - update[:keep], WIDE - SUB, 1)
    lane = lax.broadcasted_iota(jnp.int32, (keep, WIDE), 1)
    s_ref[:keep, :] = jnp.where(lane < B, left, ones_at((keep, WIDE), B))


def remote(src, dst, send, recv, where):
    return pltpu.make_async_remote_copy(
        src_ref=src, dst_ref=dst, send_sem=send, recv_sem=recv, device_id=where, device_id_type=MESH
    )


def rows_at(start, count):
    return pl.ds(pl.multiple_of(start, count), count)


class Spread:
    def __init__(self, buf, out, hop, send, recv, base, size, bits, cross=None):
        self.buf, self.out, self.hop, self.send, self.recv = buf, out, hop, send, recv
        self.cross = cross
        self.stages = []
        start, hop_at = base, 0
        for axis, bit, whole in bits:
            me = lax.axis_index(axis)
            digit = lax.rem(me // bit, 2)
            where = {axis: me + bit - 2 * bit * digit}
            if whole:
                count, give = size, start
            else:
                count = size // 2
                give, start = start + (1 - digit) * count, start + digit * count
            self.stages.append((where, give, start, count, hop_at, whole))
            hop_at += count
            size = count
        self.last, self.size = start, size

    def down(self, i):
        where, give, keep, count, at, _ = self.stages[i]
        return remote(self.buf.at[rows_at(give, count)], self.hop.at[pl.ds(at, count)], self.send.at[i], self.recv.at[i], where)

    def up(self, i):
        where, give, keep, count, at, _ = self.stages[i]
        n = len(self.stages) + i
        rows = self.out.at[rows_at(keep, count)]
        return remote(rows, rows, self.send.at[n], self.recv.at[n], where)

    def add(self, i):
        self.down(i).wait()
        _, _, keep, count, at, _ = self.stages[i]
        rows = rows_at(keep, count)
        to = self.out if i == len(self.stages) - 1 and self.cross is None else self.buf
        to[rows] = self.buf[rows] + self.hop[pl.ds(at, count)]

    def over(self, shift):
        land, send, recv, nc = self.cross
        to = lax.rem(lax.axis_index("col") + shift, nc)
        part = pl.ds((shift - 1) * self.size, self.size)
        return remote(
            self.buf.at[rows_at(self.last, self.size)], land.at[part], send.at[shift], recv.at[shift], {"col": to}
        )

    def send_over(self):
        for shift in range(1, self.cross[3]):
            self.over(shift).start()

    def add_over(self):
        rows = rows_at(self.last, self.size)
        total = self.buf[rows]
        for shift in range(1, self.cross[3]):
            self.over(shift).wait()
            total = total + self.cross[0][pl.ds((shift - 1) * self.size, self.size)]
        self.out[rows] = total

    def acts(self):
        count = len(self.stages)
        ends = [functools.partial(self.add, i) for i in range(count)]
        starts = [lambda i=i: self.down(i).start() for i in range(count)]
        if self.cross is not None:
            starts.append(self.send_over)
            ends.append(self.add_over)
        for i in reversed(range(count)):
            if not self.stages[i][5]:
                starts.append(lambda i=i: self.up(i).start())
                ends.append(lambda i=i: self.up(i).wait())
        acts = [starts[0]]
        acts += [lambda a=a, b=b: (a(), b()) for a, b in zip(ends, starts[1:])]
        return acts + [ends[-1]]


def bits_of(axis, size, whole=False):
    return [(axis, 1 << b, whole) for b in range(size.bit_length() - 1)]


def spread_pair(buf, out, hop, send, recv, size, nr, cross=None):
    bits = bits_of("row", nr)
    orders = [bits, bits[:1] + bits[:0:-1]]
    half = size // 2
    both = []
    for part in range(2):
        over = None if cross is None else tuple(ref.at[part] for ref in cross[:3]) + (cross[3],)
        both.append(
            Spread(buf, out, hop.at[part], send.at[part], recv.at[part], part * half, half, orders[part], over).acts()
        )
    return [lambda a=a, b=b: (a(), b()) for a, b in zip(*both)]


class Direct:
    def __init__(self, nr, nc, buf, out, land, crossland, sends, recvs):
        self.nr, self.nc = nr, nc
        self.buf, self.out, self.land, self.crossland = buf, out, land, crossland
        self.sends, self.recvs = sends, recvs
        self.r, self.c = lax.axis_index("row"), lax.axis_index("col")
        self.size = buf.shape[0] // nr
        self.mine = rows_at(self.r * self.size, self.size)

    def part(self, shift):
        return pl.ds((shift - 1) * self.size, self.size)

    def down(self, shift):
        to = lax.rem(self.r + shift, self.nr)
        return remote(
            self.buf.at[rows_at(to * self.size, self.size)], self.land.at[self.part(shift)],
            self.sends.at[0], self.recvs.at[0], {"row": to},
        )

    def over(self, shift):
        return remote(
            self.buf.at[self.mine], self.crossland.at[self.part(shift)],
            self.sends.at[1], self.recvs.at[1], {"col": lax.rem(self.c + shift, self.nc)},
        )

    def up(self, shift):
        rows = self.out.at[self.mine]
        return remote(rows, rows, self.sends.at[2], self.recvs.at[2], {"row": lax.rem(self.r + shift, self.nr)})

    def begin(self):
        for shift in range(1, self.nr):
            self.down(shift).start()

    def all_of(self, group, count, land):
        part = pl.ds(0, (count - 1) * self.size)
        remote(self.buf.at[part], land.at[part], self.sends.at[group], self.recvs.at[group], {"row": self.r}).wait()

    def total(self, group, count, land):
        self.all_of(group, count, land)
        value = self.buf[self.mine]
        for shift in range(1, count):
            value = value + land[self.part(shift)]
        return value

    def cross(self):
        self.buf[self.mine] = self.total(0, self.nr, self.land)
        for shift in range(1, self.nc):
            self.over(shift).start()

    def crossed(self):
        self.out[self.mine] = self.total(1, self.nc, self.crossland)
        self.raise_all()

    def flat(self):
        self.out[self.mine] = self.total(0, self.nr, self.land)
        self.raise_all()

    def raise_all(self):
        for shift in range(1, self.nr):
            self.up(shift).start()

    def end(self):
        self.all_of(2, self.nr, self.out)


def direct_scratch(size, width, nr, nc):
    part = size // nr
    dma = pltpu.SemaphoreType.DMA
    return [
        pltpu.VMEM(((nr - 1) * part, width), jnp.float32),
        pltpu.VMEM(((nc - 1) * part, width), jnp.float32),
        dma((3,)), dma((3,)),
    ]


def spread_scratch(size, width, dtype, nr, nc=None):
    half, n = size // 2, nr.bit_length() - 1
    dma = pltpu.SemaphoreType.DMA
    out = [pltpu.VMEM((2, half, width), dtype), dma((2, 2 * n)), dma((2, 2 * n))]
    if nc is not None:
        out += [pltpu.VMEM((2, (nc - 1) * (half // nr), width), dtype), dma((2, nc)), dma((2, nc))]
    return out


def choose(owner, wanted, value, otherwise):
    return jnp.where(jnp.full(value.shape, owner, jnp.int32) == wanted, value, otherwise)


def encode(x, top):
    part = jnp.sqrt(jnp.abs(x) * (1.0 / jnp.maximum(top, TINY)))
    code = (part * CODE + 0.5).astype(jnp.int32)
    return jnp.where(x < 0.0, -code, code).astype(jnp.int16)


def decode(code, top):
    part = code.astype(jnp.int32).astype(jnp.float32) * (1.0 / CODE)
    return part * jnp.abs(part) * top


def largest(x):
    top = jnp.max(jnp.abs(x), axis=0, keepdims=True)
    return jnp.max(top, axis=1, keepdims=True)


def front_kernel(
    nr, nc, own_ref, idx_ref, cov, inn,
    cols_o, tops_o, rowp_o, v_o, vs_o, f_o, z_o, x_o,
    w, wsem, vin, vinsem, outsem, zsem, fsem,
    cbuf, cols, rin, lin, rtx, ltx, rs, rr, ls, lr, tops, topland, topsend, toprecv, topsum,
    rbuf, rowp, rhop, rsend, rrecv,
    d0buf, d0pack, d0, d0land, d0over, d0s, d0r,
    d1buf, d1, d1hop, d1send, d1recv, d1over, d1s, d1r,
    vsbuf, vs, vsland, vsover, vss, vsr,
    vt, vst, vq, v, vtop, vtst, vtq, v1send, v1recv, v2send, v2recv, t1send, t1recv, t2send, t2recv,
    a_ref, s_ref, p_ref, u_ref, f_ref, z_ref, x_ref, picks,
):
    r = lax.axis_index("row")
    c = lax.axis_index("col")
    rows, width = w.shape
    rb, cb = rows // B, width // B
    load = pltpu.make_async_copy(cov, w, wsem)
    vload = pltpu.make_async_copy(inn, vin, vinsem)
    vload.start()
    load.start()
    barrier = pltpu.get_barrier_semaphore()
    for shift in range(1, nr):
        pl.semaphore_signal(barrier, inc=1, device_id={"row": lax.rem(r + shift, nr)}, device_id_type=MESH)
    for shift in range(1, nc):
        pl.semaphore_signal(barrier, inc=1, device_id={"col": lax.rem(c + shift, nc)}, device_id_type=MESH)

    part_p, iw = inn.shape[0], inn.shape[2]
    ratio = nr // nc
    h = ratio * part_p

    def first_stop(shift):
        to = {"row": lax.rem(r + shift, nr)}
        return (
            remote(vt.at[lax.rem(r + shift, nr)], vst.at[rows_at(r * part_p, part_p)], v1send, v1recv, to),
            remote(vtop, vtst.at[rows_at(r * 8, 8)], t1send, t1recv, to),
        )

    def second_stop(shift):
        at = lax.rem(c + shift, nc)
        to = {"col": at}
        return (
            remote(vst.at[rows_at(at * h, h)], vq.at[:, rows_at(c * iw, iw)], v2send, v2recv, to),
            remote(
                vtst.at[rows_at(at * ratio * 8, ratio * 8)], vtq.at[rows_at(c * ratio * 8, ratio * 8)],
                t2send, t2recv, to,
            ),
        )

    def code_innovations():
        vload.wait()
        top = largest(vin[:, 0, :])
        for group in range(1, nr):
            top = jnp.maximum(top, largest(vin[:, group, :]))
        vtop[...] = jnp.broadcast_to(top, vtop.shape)
        for group in range(nr):
            vt[group] = encode(vin[:, group, :], top)

    g = idx_ref[0]
    d0buf[...] = jnp.zeros_like(d0buf)
    d1buf[...] = jnp.zeros_like(d1buf)
    zero = jnp.zeros((B, B), jnp.float32)

    @pl.when(c == 0)
    def _():
        rin[...] = jnp.zeros_like(rin)

    @pl.when(c == nc - 1)
    def _():
        lin[...] = jnp.zeros_like(lin)

    with jax.named_scope("load"):
        load.wait()

    def pick_cols(i, carry):
        span = rows_at(i * B, B)
        own = own_ref[r * rb + i]
        picked = []
        for t in range(PANELS):
            tile = zero
            for j in range(cb):
                tile = choose(own_ref[c * cb + j], g + t, w[span, j * B : (j + 1) * B], tile)
            picks[span, t * B : (t + 1) * B] = tile
            picked.append(tile)
        d0buf[...] = choose(own, g, picked[0], d0buf[...])
        d1buf[:B] = choose(own, g + 1, picked[0], d1buf[:B])
        d1buf[B:] = choose(own, g + 1, picked[1], d1buf[B:])
        return carry

    def code_cols(i, carry):
        span = rows_at(i * B, B)
        for t in range(PANELS):
            tile = picks[span, t * B : (t + 1) * B]
            top = largest(tile)
            tops[pl.ds(i * PANELS + t, 1), :] = jnp.broadcast_to(top, (1, LANES))
            cbuf[span, t * B : (t + 1) * B] = encode(tile, top)
        return carry

    with jax.named_scope("columns"):
        lax.fori_loop(0, rb, pick_cols, 0)
    H = B // 2
    d0pack[: H // 2, :H] = d0buf[: H // 2, :H]
    d0pack[: H // 2, H:] = d0buf[H // 2 : H, :H]
    d0pack[H // 2 : H // 2 + H, :] = d0buf[H:, :]
    if d0pack.shape[0] > H // 2 + H:
        d0pack[H // 2 + H :, :] = jnp.zeros((d0pack.shape[0] - H // 2 - H, B), jnp.float32)
    first = Direct(nr, nc, d0pack, d0, d0land, d0over, d0s, d0r)
    second = spread_pair(d1buf, d1, d1hop, d1send, d1recv, 2 * B, nr, (d1over, d1s, d1r, nc))
    with jax.named_scope("barrier"):
        pl.semaphore_wait(barrier, nr - 1 + nc - 1)
    first.begin()
    second[0]()
    with jax.named_scope("code"):
        lax.fori_loop(0, rb, code_cols, 0)

    size = rows // CHUNKS

    def chunk(q):
        return rows_at(q * size, size)

    def right(src, q):
        return remote(src.at[chunk(q)], rin.at[chunk(q)], rs, rr.at[q], {"col": c + 1})

    def left(src, q):
        return remote(src.at[chunk(q)], lin.at[chunk(q)], ls, lr.at[q], {"col": c - 1})

    def push(begin, end):
        def one(q, carry):
            @pl.when(c == 0)
            def _():
                right(cbuf, q).start()

            @pl.when(c == nc - 1)
            def _():
                left(cbuf, q).start()

            return carry

        lax.fori_loop(begin, end, one, 0)

    def relay(t, carry):
        q = t - LAG * (c - 1)

        @pl.when((q >= 0) & (q < CHUNKS) & (c > 0))
        def _():
            right(cbuf, q).wait_recv()

            @pl.when(c < nc - 1)
            def _():
                rtx[chunk(q)] = rin[chunk(q)] + cbuf[chunk(q)]
                right(rtx, q).start()

        p = t - LAG * (nc - 2 - c)

        @pl.when((p >= 0) & (p < CHUNKS) & (c < nc - 1))
        def _():
            left(cbuf, p).wait_recv()

            @pl.when(c > 0)
            def _():
                ltx[chunk(p)] = lin[chunk(p)] + cbuf[chunk(p)]
                left(ltx, p).start()

        return carry

    def share_top(shift):
        count = tops.shape[0]
        return remote(
            tops, topland.at[pl.ds((shift - 1) * count, count)], topsend, toprecv,
            {"col": lax.rem(c + shift, nc)},
        )

    def fill_rows(i, carry):
        span = rows_at(i * B, B)
        for t in range(PANELS):
            tile = zero
            for k in range(rb):
                tile = choose(own_ref[r * rb + k], g + t, w[k * B : (k + 1) * B, span], tile)
            rbuf[t * B : (t + 1) * B, span] = tile.astype(jnp.bfloat16)
        return carry

    act_rows = spread_pair(rbuf, rowp, rhop, rsend, rrecv, PANELS * B, nr)

    def leave():
        for shift in range(1, nr):
            for copy in first_stop(shift):
                copy.start()
        vst[rows_at(r * part_p, part_p)] = vt[r]
        vtst[rows_at(r * 8, 8)] = vtop[...]
        for shift in range(1, nc):
            share_top(shift).start()

    def pass_on():
        part = vst.at[pl.ds(0, (nr - 1) * part_p)]
        remote(part, part, v1send, v1recv, {"row": r}).wait()
        part = vtst.at[pl.ds(0, (nr - 1) * 8)]
        remote(part, part, t1send, t1recv, {"row": r}).wait()
        for shift in range(1, nc):
            for copy in second_stop(shift):
                copy.start()
        vq[:, rows_at(c * iw, iw)] = vst[rows_at(c * h, h)]
        vtq[rows_at(c * ratio * 8, ratio * 8)] = vtst[rows_at(c * ratio * 8, ratio * 8)]

    early = 0

    def relays(count):
        nonlocal early
        lax.fori_loop(early, early + count, relay, 0)
        early += count

    with jax.named_scope("first1"):
        push(0, 1)
        first.cross()
        second[1]()
    with jax.named_scope("innovations"):
        code_innovations()
        push(1, 2)
    with jax.named_scope("rows"):
        lax.fori_loop(0, cb, fill_rows, 0)
        act_rows[0]()
    with jax.named_scope("early1"):
        relays(1)
        second[2]()
    with jax.named_scope("first2"):
        first.crossed()
        push(2, 3)
    with jax.named_scope("second1"):
        second[3]()
        push(3, 5)
    with jax.named_scope("early2"):
        relays(1)
    with jax.named_scope("first3"):
        first.end()
    with jax.named_scope("early3"):
        act_rows[1]()
        leave()
        push(5, CHUNKS)
        relays(1)

    outs = [
        pltpu.make_async_copy(src, dst, outsem.at[i])
        for i, (src, dst) in enumerate(
            [(rowp, rowp_o), (v, v_o), (vs, vs_o), (x_ref, x_o), (cols, cols_o), (topsum, tops_o)]
        )
    ]
    heads = Direct(nr, nc, vsbuf, vs, vsland, vsover, vss, vsr)

    def arrived():
        part = vq.at[:, pl.ds(0, (nc - 1) * iw)]
        remote(part, part, v2send, v2recv, {"col": c}).wait()
        part = vtq.at[pl.ds(0, (nc - 1) * ratio * 8)]
        remote(part, part, t2send, t2recv, {"col": c}).wait()
        for b in range(nc):
            for a in range(ratio):
                at, block = slice(a * part_p, (a + 1) * part_p), slice(b * iw, (b + 1) * iw)
                n = (b * ratio + a) * 8
                v[at, block] = decode(vq[at, block], vtq[n : n + 1, :1])
        outs[1].start()
        for t in range(PANELS):
            part = jnp.zeros((h, B), jnp.float32)
            for k in range(rb):
                part = choose(own_ref[r * rb + k], g + t, v[:, k * B : (k + 1) * B], part)
            vsbuf[t * h : (t + 1) * h] = part
        heads.begin()

    events = [[] for _ in range(STEPS)]
    half = STEPS // PANELS
    later = second[4:]
    for i, act in enumerate(later):
        events[i * half // len(later)].append(act)
    events[1].append(pass_on)
    later = act_rows[2:-1]
    for i, act in enumerate(later):
        events[2 + i * (STEPS - 2) // len(later)].append(act)
    events[half].append(arrived)
    events[half + 2].append(heads.flat)
    total = CHUNKS + LAG * (nc - 2)
    each = min(1, -(-(total - early) // STEPS))
    row_i = lax.broadcasted_iota(jnp.int32, (B, B), 0)
    col_i = lax.broadcasted_iota(jnp.int32, (B, B), 1)
    a_ref[: H // 2, :H] = d0[: H // 2, :H]
    a_ref[H // 2 : H, :H] = d0[: H // 2, H:]
    a_ref[H:, :] = d0[H // 2 : H // 2 + H, :]
    a_ref[:H, H:] = d0[H // 2 : H // 2 + H, :H].T

    def panel(turn, carry):
        s_ref[:, :B] = a_ref[...]
        s_ref[:, B:] = ones_at((B, WIDE - B), 0)

        def step(k, carry):
            now = turn * (B // SUB) + k
            with jax.named_scope("factor"):
                factor_step(k, s_ref, p_ref)
            at = early + now * each
            with jax.named_scope("relay"):
                lax.fori_loop(at, at + each, relay, 0)
            for i, acts in enumerate(events):
                if acts:
                    @pl.when(now == i)
                    def _():
                        for m, act in enumerate(acts):
                            with jax.named_scope(f"event{i}_{m}"):
                                act()
            return carry

        lax.fori_loop(0, B // SUB, step, 0)
        for k in range(B // SUB):
            span = slice(k * SUB, (k + 1) * SUB)
            u_ref[span, :] = pltpu.roll(p_ref[k, :, :B], k * SUB, 1) if k else p_ref[k, :, :B]
            z_ref[turn, span, :] = pltpu.roll(p_ref[k], WIDE - B + k * SUB, 1)[:, :B]
        z_ref[turn] = jnp.where(row_i >= col_i, z_ref[turn], 0.0)
        f_ref[turn] = jnp.where(row_i >= col_i, u_ref[...].T, 0.0)
        pltpu.make_async_copy(z_ref.at[turn], z_o.at[turn], zsem.at[turn]).start()
        pltpu.make_async_copy(f_ref.at[turn], f_o.at[turn], fsem.at[turn]).start()

        @pl.when(turn == 0)
        def _():
            low = dot3(d1[:B], z_ref[0], LAST)
            half = low.astype(jnp.bfloat16)
            x_ref[...] = half
            a_ref[...] = d1[B:] - dot(half, half, LAST)

        return carry

    lax.fori_loop(0, PANELS, panel, 0)
    outs[3].start()
    with jax.named_scope("late"):
        lax.fori_loop(early + STEPS * each, total, relay, 0)
    with jax.named_scope("sum"):
        def add(q, carry):
            cols[chunk(q)] = cbuf[chunk(q)] + (rin[chunk(q)] + lin[chunk(q)])
            return carry

        lax.fori_loop(0, CHUNKS, add, 0)
        outs[4].start()
        count = tops.shape[0]
        top = tops[...]
        remote(topland, topland, topsend, toprecv, {"col": c}).wait()
        for shift in range(1, nc):
            top = top + topland[pl.ds((shift - 1) * count, count)]
        topsum[...] = top
        outs[5].start()

    with jax.named_scope("rowend"):
        act_rows[-1]()
        outs[0].start()
    with jax.named_scope("headend"):
        heads.end()
        outs[2].start()

    with jax.named_scope("sent"):
        @pl.when(c < nc - 1)
        def _():
            remote(cbuf, rin, rs, rr.at[0], {"col": c + 1}).wait_send()

        @pl.when(c > 0)
        def _():
            remote(cbuf, lin, ls, lr.at[0], {"col": c - 1}).wait_send()

    with jax.named_scope("written"):
        for turn in range(PANELS):
            pltpu.make_async_copy(z_ref.at[turn], z_o.at[turn], zsem.at[turn]).wait()
            pltpu.make_async_copy(f_ref.at[turn], f_o.at[turn], fsem.at[turn]).wait()
        for out in outs:
            out.wait()


def front(nr, nc, owner, index, cov, inn):
    rows, width = cov.shape
    part_p, groups, iw = inn.shape
    ratio = nr // nc
    h = ratio * part_p
    f32, bf16, i16 = jnp.float32, jnp.bfloat16, jnp.int16
    smem = pl.BlockSpec(memory_space=pltpu.SMEM)
    anywhere = pl.BlockSpec(memory_space=pl.ANY)
    vmem = pltpu.VMEM
    dma = pltpu.SemaphoreType.DMA
    both = PANELS * B
    count = PANELS * (rows // B)
    scratch = [vmem((rows, width), f32), dma, vmem(inn.shape, f32), dma, dma((6,)), dma((PANELS,)), dma((PANELS,))]
    scratch += [vmem((rows, both), i16)] * 6 + [dma, dma((CHUNKS,))] * 2
    scratch += [vmem((count, LANES), f32), vmem(((nc - 1) * count, LANES), f32), dma, dma, vmem((count, LANES), f32)]
    scratch += [vmem((both, width), bf16)] * 2 + spread_scratch(both, width, bf16, nr)
    packed = nr * (-(-(B // 4 * 3) // (8 * nr)) * 8)
    scratch += [vmem((B, B), f32)] + [vmem((packed, B), f32)] * 2 + direct_scratch(packed, B, nr, nc)
    scratch += [vmem((2 * B, B), f32)] * 2 + spread_scratch(2 * B, B, f32, nr, nc)
    scratch += [vmem((PANELS * h, B), f32)] * 2 + direct_scratch(PANELS * h, B, nr, nc)
    scratch += [vmem((groups, part_p, iw), i16), vmem((nr * part_p, iw), i16), vmem((h, nc * iw), i16), vmem((h, nc * iw), f32)]
    scratch += [vmem((8, LANES), f32), vmem((nr * 8, LANES), f32), vmem((nr * 8, LANES), f32)]
    scratch += [dma] * 8
    scratch += [vmem((B, B), f32), vmem((B, WIDE), f32), vmem((B // SUB, SUB, WIDE), f32), vmem((B, B), f32)]
    scratch += [vmem((PANELS, B, B), f32)] * 2 + [vmem((B, B), bf16), vmem((rows, both), f32)]
    return pl.pallas_call(
        functools.partial(front_kernel, nr, nc),
        out_shape=(
            jax.ShapeDtypeStruct((rows, both), i16),
            jax.ShapeDtypeStruct((count, LANES), f32),
            jax.ShapeDtypeStruct((both, width), bf16),
            jax.ShapeDtypeStruct((h, nc * iw), f32),
            jax.ShapeDtypeStruct((PANELS * h, B), f32),
            jax.ShapeDtypeStruct((PANELS, B, B), f32),
            jax.ShapeDtypeStruct((PANELS, B, B), f32),
            jax.ShapeDtypeStruct((B, B), bf16),
        ),
        in_specs=[smem, smem, anywhere, anywhere],
        out_specs=(anywhere,) * 8,
        scratch_shapes=scratch,
        compiler_params=pltpu.CompilerParams(
            collective_id=0, has_side_effects=True, vmem_limit_bytes=56 * 1024 * 1024
        ),
    )(owner, index, cov, inn)


def tail_kernel(
    own_ref, idx_ref, w_any, cols_any, tops_any, rowp_any, f_any, z_any, x_any, vs_any, v_any,
    o_any, vout_any,
    w_ref, o_ref, cols_ref, tops_ref, rowp_ref, f_ref, z_ref, x_ref, vs_ref, v_ref, vout_ref, q_ref, half_ref,
    insem, wsem, osem, vsem, *, rb, cb,
):
    g = idx_ref[0]
    row0 = lax.axis_index("row") * rb
    col0 = lax.axis_index("col") * cb
    h = v_ref.shape[0]
    pairs = [
        (z_any, z_ref), (x_any, x_ref), (rowp_any, rowp_ref), (tops_any, tops_ref), (cols_any, cols_ref),
        (vs_any, vs_ref), (v_any, v_ref), (f_any, f_ref),
    ]
    ins = [pltpu.make_async_copy(src, dst, insem.at[i]) for i, (src, dst) in enumerate(pairs)]

    def stripe_in(j):
        span = rows_at(j * B, B)
        return pltpu.make_async_copy(w_any.at[:, span], w_ref.at[:, span], wsem.at[j])

    def stripe_out(j):
        span = rows_at(j * B, B)
        return pltpu.make_async_copy(o_ref.at[:, span], o_any.at[:, span], osem.at[j])

    for copy in ins[:5]:
        copy.start()
    for copy in ins[:3]:
        copy.wait()
    for j in range(cb):
        stripe_in(j).start()
    for copy in ins[5:]:
        copy.start()

    with jax.named_scope("qpanels"):
        x = x_ref[...]
        zh0, zl0 = split_bf16(z_ref[0])
        zh1, zl1 = split_bf16(z_ref[1])
        for k in range(cb):
            span = slice(k * B, (k + 1) * B)
            own = own_ref[col0 + k]
            q0 = dot(zh0, rowp_ref[:B, span]) + dot(zl0, rowp_ref[:B, span])
            q0 = jnp.where(own > g, q0, 0.0).astype(jnp.bfloat16)
            r1 = (rowp_ref[B:, span].astype(jnp.float32) - dot(x, q0)).astype(jnp.bfloat16)
            q1 = dot(zh1, r1) + dot(zl1, r1)
            q_ref[:B, span] = q0
            q_ref[B:, span] = jnp.where(own > g + 1, q1, 0.0).astype(jnp.bfloat16)

    for copy in ins[3:5]:
        copy.wait()

    with jax.named_scope("panels"):
        for i in range(rb):
            span = slice(i * B, (i + 1) * B)
            own = own_ref[row0 + i]
            c0 = decode(cols_ref[span, :B], tops_ref[PANELS * i : PANELS * i + 1, :1])
            p0 = dot3(c0, z_ref[0], LAST)
            h0 = jnp.where(own > g, p0, 0.0).astype(jnp.bfloat16)
            c1 = decode(cols_ref[span, B:], tops_ref[PANELS * i + 1 : PANELS * i + 2, :1]) - dot(h0, x, LAST)
            p1 = dot3(c1, z_ref[1], LAST)
            half_ref[span, :B] = h0
            half_ref[span, B:] = jnp.where(own > g + 1, p1, 0.0).astype(jnp.bfloat16)

    for copy in ins[5:]:
        copy.wait()

    def stripe(j, carry):
        span = rows_at(j * B, B)
        cown = own_ref[col0 + j]
        stripe_in(j).wait()
        with jax.named_scope("update"):
            o_ref[:, span] = w_ref[:, span] - dot(half_ref[...], q_ref[:, span])

        @pl.when(cown > g)
        def _():
            for i in range(rb):
                rown = own_ref[row0 + i]

                @pl.when((rown == g) | ((rown == g + 1) & (cown > g + 1)))
                def _():
                    o_ref[i * B : (i + 1) * B, span] = jnp.zeros((B, B), jnp.float32)

        for turn in range(PANELS):
            @pl.when(cown == g + turn)
            def _():
                for i in range(rb):
                    part = slice(i * B, (i + 1) * B)
                    rown = own_ref[row0 + i]

                    @pl.when(rown > g + turn)
                    def _():
                        left = w_ref[part, span]
                        if turn:
                            left = left - dot(half_ref[part, :B], x_ref[...], LAST)
                        o_ref[part, span] = dot3(left, z_ref[turn], LAST)

                    @pl.when(rown == g + turn)
                    def _():
                        o_ref[part, span] = f_ref[turn]

        stripe_out(j).start()
        return carry

    lax.fori_loop(0, cb, stripe, 0)

    with jax.named_scope("solve"):
        w0 = dot3(vs_ref[:h], z_ref[0], LAST)
        w0h = w0.astype(jnp.bfloat16)
        w1 = dot3(vs_ref[h:] - dot(w0h, x, LAST), z_ref[1], LAST)
        w1h = w1.astype(jnp.bfloat16)
        for i in range(rb):
            span = slice(i * B, (i + 1) * B)
            own = own_ref[row0 + i]
            new = v_ref[:, span] - (dot(w0h, half_ref[span, :B], LAST) + dot(w1h, half_ref[span, B:], LAST))
            new = jnp.where(own == g, w0, new)
            vout_ref[:, span] = jnp.where(own == g + 1, w1, new)
        done = pltpu.make_async_copy(vout_ref, vout_any, vsem)
        done.start()

    with jax.named_scope("drain"):
        lax.fori_loop(0, cb, lambda j, k: (stripe_out(j).wait(), k)[1], 0)
        done.wait()


def tail(owner, index, w, cols, tops, rowp, factors, z, x, vs, v):
    rows, width = w.shape
    cb = width // B
    smem = pl.BlockSpec(memory_space=pltpu.SMEM)
    anywhere = pl.BlockSpec(memory_space=pl.ANY)
    dma = pltpu.SemaphoreType.DMA
    arrays = [w, w, cols, tops, rowp, factors, z, x, vs, v, v]
    return pl.pallas_call(
        functools.partial(tail_kernel, rb=rows // B, cb=cb),
        in_specs=[smem, smem] + [anywhere] * 9,
        out_specs=[anywhere] * 2,
        scratch_shapes=[pltpu.VMEM(a.shape, a.dtype) for a in arrays]
        + [pltpu.VMEM((2 * B, width), jnp.bfloat16), pltpu.VMEM((rows, 2 * B), jnp.bfloat16)]
        + [dma((8,)), dma((cb,)), dma((cb,)), dma],
        out_shape=(jax.ShapeDtypeStruct(w.shape, w.dtype), jax.ShapeDtypeStruct(v.shape, v.dtype)),
        compiler_params=pltpu.CompilerParams(vmem_limit_bytes=60 * 1024 * 1024),
    )(owner, index, w, cols, tops, rowp, factors, z, x, vs, v)


def per_device(covariance, innovations, block_owner, panel_index):
    nr, nc = lax.axis_size("row"), lax.axis_size("col")
    cols, tops, rowp, v, vs, factors, z, x = front(nr, nc, block_owner, panel_index, covariance, innovations)
    return tail(block_owner, panel_index, covariance, cols, tops, rowp, factors, z, x, vs, v)


def solution(mesh):
    placed = (P("row", "col"), P("row", None, "col"), P(), P())
    return jax.shard_map(
        per_device,
        mesh=mesh,
        in_specs=placed,
        out_specs=(P("row", "col"), P("col", "row")),
        check_vma=False,
    )
```

```python
import functools

import jax
import jax.numpy as jnp
from jax import lax
from jax.experimental import pallas as pl
from jax.experimental.pallas import tpu as pltpu
from jax.sharding import PartitionSpec as P

B = 256
PANELS = 2
SUB = 64
G8 = SUB // 8
LANES = 128
TW = -(-(B + SUB) // LANES)
WIDE = TW * LANES

LAST = (((1,), (1,)), ((), ()))
FIRST = (((0,), (0,)), ((), ()))
PLAIN = (((1,), (0,)), ((), ()))


def dot(a, b, dims=PLAIN):
    return lax.dot_general(a, b, dims, preferred_element_type=jnp.float32)


def split_bf16(x):
    hi = x.astype(jnp.bfloat16)
    lo = (x - hi.astype(jnp.float32)).astype(jnp.bfloat16)
    return hi, lo


def dot3(a, b, dims=PLAIN):
    ah, al = split_bf16(a)
    bh, bl = split_bf16(b)
    return dot(ah, bh, dims) + (dot(ah, bl, dims) + dot(al, bh, dims))


def lanes(x):
    return jnp.broadcast_to(x, (8, LANES))


def factor_panel(s_ref, p_ref):
    sub_iota = lax.broadcasted_iota(jnp.int32, (8, LANES), 0)
    rows = [[s_ref[8 * g : 8 * g + 8, LANES * t : LANES * (t + 1)] for t in range(TW)] for g in range(G8)]
    for b in range(G8):
        c0 = 8 * b
        col = [[lanes(rows[g][0][:, c0 + j : c0 + j + 1]) for j in range(8)] for g in range(b, G8)]
        e = [[lanes(col[0][j][i : i + 1, :]) for j in range(i + 1)] for i in range(8)]
        r = []
        l = [[None] * 8 for _ in range(8)]
        for j in range(8):
            rj = lax.rsqrt(e[j][j])
            r.append(rj)
            for i in range(j + 1, 8):
                l[i][j] = e[i][j] * rj
            for i in range(j + 1, 8):
                for k in range(j + 1, i + 1):
                    e[i][k] = e[i][k] - l[i][j] * l[k][j]
        y = []
        for i in range(8):
            yi = []
            for t in range(TW):
                v = lanes(rows[b][t][i : i + 1, :])
                for j in range(i):
                    v = v - l[i][j] * y[j][t]
                yi.append(v * r[i])
            y.append(yi)
        for t in range(TW):
            u = y[0][t]
            for i in range(1, 8):
                u = jnp.where(sub_iota == i, y[i][t], u)
            p_ref[8 * b : 8 * b + 8, LANES * t : LANES * (t + 1)] = u
        for g in range(b + 1, G8):
            cs = []
            for j in range(8):
                v = col[g - b][j]
                for k in range(j):
                    v = v - l[j][k] * cs[k]
                cs.append(v * r[j])
            for t in range(TW):
                v = rows[g][t]
                for j in range(8):
                    v = v - cs[j] * y[j][t]
                rows[g][t] = v


MESH = pl.DeviceIdType.MESH
CHUNKS = 8
LAG = 2
CODE = 32767.0
TINY = 1e-37
STEPS = PANELS * (B // SUB)


def ones_at(shape, first):
    row = lax.broadcasted_iota(jnp.int32, shape, 0)
    lane = lax.broadcasted_iota(jnp.int32, shape, 1)
    return jnp.where((lane - first == row) & (lane < first + SUB), 1.0, 0.0)


def factor_step(k, s_ref, p_ref):
    p = p_ref.at[k]
    factor_panel(s_ref, p)
    keep = B - SUB
    rolled = pltpu.roll(p[:, :B], keep, 1)
    lane = lax.broadcasted_iota(jnp.int32, (SUB, B), 1)
    rolled = jnp.where(lane < keep, rolled, 0.0)
    update = dot3(rolled, p[...], FIRST)
    left = pltpu.roll(s_ref[SUB:, :] - update[:keep], WIDE - SUB, 1)
    lane = lax.broadcasted_iota(jnp.int32, (keep, WIDE), 1)
    s_ref[:keep, :] = jnp.where(lane < B, left, ones_at((keep, WIDE), B))


def remote(src, dst, send, recv, where):
    return pltpu.make_async_remote_copy(
        src_ref=src, dst_ref=dst, send_sem=send, recv_sem=recv, device_id=where, device_id_type=MESH
    )


def rows_at(start, count):
    return pl.ds(pl.multiple_of(start, count), count)


class Spread:
    def __init__(self, buf, out, hop, send, recv, base, size, bits, cross=None):
        self.buf, self.out, self.hop, self.send, self.recv = buf, out, hop, send, recv
        self.cross = cross
        self.stages = []
        start, hop_at = base, 0
        for axis, bit, whole in bits:
            me = lax.axis_index(axis)
            digit = lax.rem(me // bit, 2)
            where = {axis: me + bit - 2 * bit * digit}
            if whole:
                count, give = size, start
            else:
                count = size // 2
                give, start = start + (1 - digit) * count, start + digit * count
            self.stages.append((where, give, start, count, hop_at, whole))
            hop_at += count
            size = count
        self.last, self.size = start, size

    def down(self, i):
        where, give, keep, count, at, _ = self.stages[i]
        return remote(self.buf.at[rows_at(give, count)], self.hop.at[pl.ds(at, count)], self.send.at[i], self.recv.at[i], where)

    def up(self, i):
        where, give, keep, count, at, _ = self.stages[i]
        n = len(self.stages) + i
        rows = self.out.at[rows_at(keep, count)]
        return remote(rows, rows, self.send.at[n], self.recv.at[n], where)

    def add(self, i):
        self.down(i).wait()
        _, _, keep, count, at, _ = self.stages[i]
        rows = rows_at(keep, count)
        to = self.out if i == len(self.stages) - 1 and self.cross is None else self.buf
        to[rows] = self.buf[rows] + self.hop[pl.ds(at, count)]

    def over(self, shift):
        land, send, recv, nc = self.cross
        to = lax.rem(lax.axis_index("col") + shift, nc)
        part = pl.ds((shift - 1) * self.size, self.size)
        return remote(
            self.buf.at[rows_at(self.last, self.size)], land.at[part], send.at[shift], recv.at[shift], {"col": to}
        )

    def send_over(self):
        for shift in range(1, self.cross[3]):
            self.over(shift).start()

    def add_over(self):
        rows = rows_at(self.last, self.size)
        total = self.buf[rows]
        for shift in range(1, self.cross[3]):
            self.over(shift).wait()
            total = total + self.cross[0][pl.ds((shift - 1) * self.size, self.size)]
        self.out[rows] = total

    def acts(self):
        count = len(self.stages)
        ends = [functools.partial(self.add, i) for i in range(count)]
        starts = [lambda i=i: self.down(i).start() for i in range(count)]
        if self.cross is not None:
            starts.append(self.send_over)
            ends.append(self.add_over)
        for i in reversed(range(count)):
            if not self.stages[i][5]:
                starts.append(lambda i=i: self.up(i).start())
                ends.append(lambda i=i: self.up(i).wait())
        acts = [starts[0]]
        acts += [lambda a=a, b=b: (a(), b()) for a, b in zip(ends, starts[1:])]
        return acts + [ends[-1]]


def bits_of(axis, size, whole=False):
    return [(axis, 1 << b, whole) for b in range(size.bit_length() - 1)]


def spread_pair(buf, out, hop, send, recv, size, nr, cross=None):
    bits = bits_of("row", nr)
    orders = [bits, bits[:1] + bits[:0:-1]]
    half = size // 2
    both = []
    for part in range(2):
        over = None if cross is None else tuple(ref.at[part] for ref in cross[:3]) + (cross[3],)
        both.append(
            Spread(buf, out, hop.at[part], send.at[part], recv.at[part], part * half, half, orders[part], over).acts()
        )
    return [lambda a=a, b=b: (a(), b()) for a, b in zip(*both)]


class Direct:
    def __init__(self, nr, nc, buf, out, land, crossland, sends, recvs):
        self.nr, self.nc = nr, nc
        self.buf, self.out, self.land, self.crossland = buf, out, land, crossland
        self.sends, self.recvs = sends, recvs
        self.r, self.c = lax.axis_index("row"), lax.axis_index("col")
        self.size = buf.shape[0] // nr
        self.mine = rows_at(self.r * self.size, self.size)

    def part(self, shift):
        return pl.ds((shift - 1) * self.size, self.size)

    def down(self, shift):
        to = lax.rem(self.r + shift, self.nr)
        return remote(
            self.buf.at[rows_at(to * self.size, self.size)], self.land.at[self.part(shift)],
            self.sends.at[0], self.recvs.at[0], {"row": to},
        )

    def over(self, shift):
        return remote(
            self.buf.at[self.mine], self.crossland.at[self.part(shift)],
            self.sends.at[1], self.recvs.at[1], {"col": lax.rem(self.c + shift, self.nc)},
        )

    def up(self, shift):
        rows = self.out.at[self.mine]
        return remote(rows, rows, self.sends.at[2], self.recvs.at[2], {"row": lax.rem(self.r + shift, self.nr)})

    def begin(self):
        for shift in range(1, self.nr):
            self.down(shift).start()

    def all_of(self, group, count, land):
        part = pl.ds(0, (count - 1) * self.size)
        remote(self.buf.at[part], land.at[part], self.sends.at[group], self.recvs.at[group], {"row": self.r}).wait()

    def total(self, group, count, land):
        self.all_of(group, count, land)
        value = self.buf[self.mine]
        for shift in range(1, count):
            value = value + land[self.part(shift)]
        return value

    def cross(self):
        self.buf[self.mine] = self.total(0, self.nr, self.land)
        for shift in range(1, self.nc):
            self.over(shift).start()

    def crossed(self):
        self.out[self.mine] = self.total(1, self.nc, self.crossland)
        self.raise_all()

    def flat(self):
        self.out[self.mine] = self.total(0, self.nr, self.land)
        self.raise_all()

    def raise_all(self):
        for shift in range(1, self.nr):
            self.up(shift).start()

    def end(self):
        self.all_of(2, self.nr, self.out)


def direct_scratch(size, width, nr, nc):
    part = size // nr
    dma = pltpu.SemaphoreType.DMA
    return [
        pltpu.VMEM(((nr - 1) * part, width), jnp.float32),
        pltpu.VMEM(((nc - 1) * part, width), jnp.float32),
        dma((3,)), dma((3,)),
    ]


def spread_scratch(size, width, dtype, nr, nc=None):
    half, n = size // 2, nr.bit_length() - 1
    dma = pltpu.SemaphoreType.DMA
    out = [pltpu.VMEM((2, half, width), dtype), dma((2, 2 * n)), dma((2, 2 * n))]
    if nc is not None:
        out += [pltpu.VMEM((2, (nc - 1) * (half // nr), width), dtype), dma((2, nc)), dma((2, nc))]
    return out


def choose(owner, wanted, value, otherwise):
    return jnp.where(jnp.full(value.shape, owner, jnp.int32) == wanted, value, otherwise)


def encode(x, top):
    part = jnp.sqrt(jnp.abs(x) * (1.0 / jnp.maximum(top, TINY)))
    code = (part * CODE + 0.5).astype(jnp.int32)
    return jnp.where(x < 0.0, -code, code).astype(jnp.int16)


def decode(code, top):
    part = code.astype(jnp.int32).astype(jnp.float32) * (1.0 / CODE)
    return part * jnp.abs(part) * top


def largest(x):
    top = jnp.max(jnp.abs(x), axis=0, keepdims=True)
    return jnp.max(top, axis=1, keepdims=True)


def front_kernel(
    nr, nc, own_ref, idx_ref, cov, inn,
    cols_o, tops_o, rowp_o, v_o, vs_o, f_o, z_o, x_o,
    w, wsem, vin, vinsem, outsem, zsem, fsem, rowsem,
    cbuf, cols, rin, lin, rtx, ltx, rs, rr, ls, lr, tops, topland, topsend, toprecv, topsum,
    rbuf, rowp, rhop, rsend, rrecv,
    d0buf, d0pack, d0, d0land, d0over, d0s, d0r,
    d1buf, d1, d1hop, d1send, d1recv, d1over, d1s, d1r,
    vsbuf, vs, vsland, vsover, vss, vsr,
    vt, vst, vq, v, vtop, vtst, vtq, v1send, v1recv, v2send, v2recv, t1send, t1recv, t2send, t2recv,
    a_ref, s_ref, p_ref, u_ref, f_ref, z_ref, x_ref, picks,
):
    r = lax.axis_index("row")
    c = lax.axis_index("col")
    rows, width = w.shape
    rb, cb = rows // B, width // B
    load = pltpu.make_async_copy(cov, w, wsem)
    vload = pltpu.make_async_copy(inn, vin, vinsem)
    vload.start()
    load.start()
    barrier = pltpu.get_barrier_semaphore()
    for shift in range(1, nr):
        pl.semaphore_signal(barrier, inc=1, device_id={"row": lax.rem(r + shift, nr)}, device_id_type=MESH)
    for shift in range(1, nc):
        pl.semaphore_signal(barrier, inc=1, device_id={"col": lax.rem(c + shift, nc)}, device_id_type=MESH)

    part_p, iw = inn.shape[0], inn.shape[2]
    ratio = nr // nc
    h = ratio * part_p

    def first_stop(shift):
        to = {"row": lax.rem(r + shift, nr)}
        return (
            remote(vt.at[lax.rem(r + shift, nr)], vst.at[rows_at(r * part_p, part_p)], v1send, v1recv, to),
            remote(vtop, vtst.at[rows_at(r * 8, 8)], t1send, t1recv, to),
        )

    def second_stop(shift):
        at = lax.rem(c + shift, nc)
        to = {"col": at}
        return (
            remote(vst.at[rows_at(at * h, h)], vq.at[:, rows_at(c * iw, iw)], v2send, v2recv, to),
            remote(
                vtst.at[rows_at(at * ratio * 8, ratio * 8)], vtq.at[rows_at(c * ratio * 8, ratio * 8)],
                t2send, t2recv, to,
            ),
        )

    def code_innovations():
        vload.wait()
        top = largest(vin[:, 0, :])
        for group in range(1, nr):
            top = jnp.maximum(top, largest(vin[:, group, :]))
        vtop[...] = jnp.broadcast_to(top, vtop.shape)
        for group in range(nr):
            vt[group] = encode(vin[:, group, :], top)

    g = idx_ref[0]
    d0buf[...] = jnp.zeros_like(d0buf)
    d1buf[...] = jnp.zeros_like(d1buf)
    zero = jnp.zeros((B, B), jnp.float32)

    @pl.when(c == 0)
    def _():
        rin[...] = jnp.zeros_like(rin)

    @pl.when(c == nc - 1)
    def _():
        lin[...] = jnp.zeros_like(lin)

    with jax.named_scope("load"):
        load.wait()

    def pick_cols(i, carry):
        span = rows_at(i * B, B)
        own = own_ref[r * rb + i]
        picked = []
        for t in range(PANELS):
            tile = zero
            for j in range(cb):
                tile = choose(own_ref[c * cb + j], g + t, w[span, j * B : (j + 1) * B], tile)
            picks[span, t * B : (t + 1) * B] = tile
            picked.append(tile)
        d0buf[...] = choose(own, g, picked[0], d0buf[...])
        d1buf[:B] = choose(own, g + 1, picked[0], d1buf[:B])
        d1buf[B:] = choose(own, g + 1, picked[1], d1buf[B:])
        return carry

    def code_cols(i, carry):
        span = rows_at(i * B, B)
        for t in range(PANELS):
            tile = picks[span, t * B : (t + 1) * B]
            top = largest(tile)
            tops[pl.ds(i * PANELS + t, 1), :] = jnp.broadcast_to(top, (1, LANES))
            cbuf[span, t * B : (t + 1) * B] = encode(tile, top)
        return carry

    with jax.named_scope("columns"):
        lax.fori_loop(0, rb, pick_cols, 0)
    H = B // 2
    d0pack[: H // 2, :H] = d0buf[: H // 2, :H]
    d0pack[: H // 2, H:] = d0buf[H // 2 : H, :H]
    d0pack[H // 2 : H // 2 + H, :] = d0buf[H:, :]
    if d0pack.shape[0] > H // 2 + H:
        d0pack[H // 2 + H :, :] = jnp.zeros((d0pack.shape[0] - H // 2 - H, B), jnp.float32)
    first = Direct(nr, nc, d0pack, d0, d0land, d0over, d0s, d0r)
    second = spread_pair(d1buf, d1, d1hop, d1send, d1recv, 2 * B, nr, (d1over, d1s, d1r, nc))
    with jax.named_scope("barrier"):
        pl.semaphore_wait(barrier, nr - 1 + nc - 1)
    first.begin()
    second[0]()
    with jax.named_scope("code"):
        lax.fori_loop(0, rb, code_cols, 0)

    size = rows // CHUNKS

    def chunk(q):
        return rows_at(q * size, size)

    def right(src, q):
        return remote(src.at[chunk(q)], rin.at[chunk(q)], rs, rr.at[q], {"col": c + 1})

    def left(src, q):
        return remote(src.at[chunk(q)], lin.at[chunk(q)], ls, lr.at[q], {"col": c - 1})

    def push(begin, end):
        def one(q, carry):
            @pl.when(c == 0)
            def _():
                right(cbuf, q).start()

            @pl.when(c == nc - 1)
            def _():
                left(cbuf, q).start()

            return carry

        lax.fori_loop(begin, end, one, 0)

    def relay(t, carry):
        q = t - LAG * (c - 1)

        @pl.when((q >= 0) & (q < CHUNKS) & (c > 0))
        def _():
            right(cbuf, q).wait_recv()

            @pl.when(c < nc - 1)
            def _():
                rtx[chunk(q)] = rin[chunk(q)] + cbuf[chunk(q)]
                right(rtx, q).start()

        p = t - LAG * (nc - 2 - c)

        @pl.when((p >= 0) & (p < CHUNKS) & (c < nc - 1))
        def _():
            left(cbuf, p).wait_recv()

            @pl.when(c > 0)
            def _():
                ltx[chunk(p)] = lin[chunk(p)] + cbuf[chunk(p)]
                left(ltx, p).start()

        return carry

    def share_top(shift):
        count = tops.shape[0]
        return remote(
            tops, topland.at[pl.ds((shift - 1) * count, count)], topsend, toprecv,
            {"col": lax.rem(c + shift, nc)},
        )

    def fill_rows(i, carry):
        span = rows_at(i * B, B)
        for t in range(PANELS):
            tile = zero
            for k in range(rb):
                tile = choose(own_ref[r * rb + k], g + t, w[k * B : (k + 1) * B, span], tile)
            rbuf[t * B : (t + 1) * B, span] = tile.astype(jnp.bfloat16)
        return carry

    act_rows = spread_pair(rbuf, rowp, rhop, rsend, rrecv, PANELS * B, nr)

    def leave():
        for shift in range(1, nr):
            for copy in first_stop(shift):
                copy.start()
        vst[rows_at(r * part_p, part_p)] = vt[r]
        vtst[rows_at(r * 8, 8)] = vtop[...]
        for shift in range(1, nc):
            share_top(shift).start()

    def pass_on():
        part = vst.at[pl.ds(0, (nr - 1) * part_p)]
        remote(part, part, v1send, v1recv, {"row": r}).wait()
        part = vtst.at[pl.ds(0, (nr - 1) * 8)]
        remote(part, part, t1send, t1recv, {"row": r}).wait()
        for shift in range(1, nc):
            for copy in second_stop(shift):
                copy.start()
        vq[:, rows_at(c * iw, iw)] = vst[rows_at(c * h, h)]
        vtq[rows_at(c * ratio * 8, ratio * 8)] = vtst[rows_at(c * ratio * 8, ratio * 8)]

    early = 0

    def relays(count):
        nonlocal early
        lax.fori_loop(early, early + count, relay, 0)
        early += count

    with jax.named_scope("first1"):
        push(0, 1)
        first.cross()
        second[1]()
    with jax.named_scope("innovations"):
        code_innovations()
        push(1, 2)
    with jax.named_scope("rows"):
        lax.fori_loop(0, cb, fill_rows, 0)
        act_rows[0]()
    with jax.named_scope("early1"):
        relays(1)
        second[2]()
    with jax.named_scope("first2"):
        first.crossed()
        push(2, 3)
    with jax.named_scope("second1"):
        second[3]()
        push(3, 5)
    with jax.named_scope("early2"):
        relays(1)
    with jax.named_scope("first3"):
        first.end()
    with jax.named_scope("early3"):
        act_rows[1]()
        leave()
        push(5, CHUNKS)
        relays(1)

    outs = [
        pltpu.make_async_copy(src, dst, outsem.at[i])
        for i, (src, dst) in enumerate(
            [(v, v_o), (vs, vs_o), (x_ref, x_o), (cols, cols_o), (topsum, tops_o)]
        )
    ]
    heads = Direct(nr, nc, vsbuf, vs, vsland, vsover, vss, vsr)

    def arrived():
        part = vq.at[:, pl.ds(0, (nc - 1) * iw)]
        remote(part, part, v2send, v2recv, {"col": c}).wait()
        part = vtq.at[pl.ds(0, (nc - 1) * ratio * 8)]
        remote(part, part, t2send, t2recv, {"col": c}).wait()
        for b in range(nc):
            for a in range(ratio):
                at, block = slice(a * part_p, (a + 1) * part_p), slice(b * iw, (b + 1) * iw)
                n = (b * ratio + a) * 8
                v[at, block] = decode(vq[at, block], vtq[n : n + 1, :1])
        outs[0].start()
        for t in range(PANELS):
            part = jnp.zeros((h, B), jnp.float32)
            for k in range(rb):
                part = choose(own_ref[r * rb + k], g + t, v[:, k * B : (k + 1) * B], part)
            vsbuf[t * h : (t + 1) * h] = part
        heads.begin()

    def row_outs(other):
        digit = lax.rem(r + other, 2)
        spans = [rows_at(t * B + digit * (B // 2), B // 2) for t in range(PANELS)]
        return [
            pltpu.make_async_copy(rowp.at[span], rowp_o.at[span], rowsem.at[2 * other + t]) for t, span in enumerate(spans)
        ]

    events = [[] for _ in range(STEPS)]
    half = STEPS // PANELS
    later = second[4:]
    for i, act in enumerate(later):
        events[i * half // len(later)].append(act)
    events[1].append(pass_on)
    later = act_rows[2:-1]
    for i, act in enumerate(later):
        events[2 + i * (STEPS - 2) // len(later)].append(act)
    events[STEPS - 1].append(lambda: [copy.start() for copy in row_outs(0)])
    events[half].append(arrived)
    events[half + 2].append(heads.flat)
    total = CHUNKS + LAG * (nc - 2)
    each = min(1, -(-(total - early) // STEPS))
    row_i = lax.broadcasted_iota(jnp.int32, (B, B), 0)
    col_i = lax.broadcasted_iota(jnp.int32, (B, B), 1)
    a_ref[: H // 2, :H] = d0[: H // 2, :H]
    a_ref[H // 2 : H, :H] = d0[: H // 2, H:]
    a_ref[H:, :] = d0[H // 2 : H // 2 + H, :]
    a_ref[:H, H:] = d0[H // 2 : H // 2 + H, :H].T

    def panel(turn, carry):
        s_ref[:, :B] = a_ref[...]
        s_ref[:, B:] = ones_at((B, WIDE - B), 0)

        def step(k, carry):
            now = turn * (B // SUB) + k
            with jax.named_scope("factor"):
                factor_step(k, s_ref, p_ref)
            at = early + now * each
            with jax.named_scope("relay"):
                lax.fori_loop(at, at + each, relay, 0)
            for i, acts in enumerate(events):
                if acts:
                    @pl.when(now == i)
                    def _():
                        for m, act in enumerate(acts):
                            with jax.named_scope(f"event{i}_{m}"):
                                act()
            return carry

        lax.fori_loop(0, B // SUB, step, 0)
        for k in range(B // SUB):
            span = slice(k * SUB, (k + 1) * SUB)
            u_ref[span, :] = pltpu.roll(p_ref[k, :, :B], k * SUB, 1) if k else p_ref[k, :, :B]
            z_ref[turn, span, :] = pltpu.roll(p_ref[k], WIDE - B + k * SUB, 1)[:, :B]
        z_ref[turn] = jnp.where(row_i >= col_i, z_ref[turn], 0.0)
        f_ref[turn] = jnp.where(row_i >= col_i, u_ref[...].T, 0.0)
        pltpu.make_async_copy(z_ref.at[turn], z_o.at[turn], zsem.at[turn]).start()
        pltpu.make_async_copy(f_ref.at[turn], f_o.at[turn], fsem.at[turn]).start()

        @pl.when(turn == 0)
        def _():
            low = dot3(d1[:B], z_ref[0], LAST)
            half = low.astype(jnp.bfloat16)
            x_ref[...] = half
            a_ref[...] = d1[B:] - dot(half, half, LAST)

        return carry

    lax.fori_loop(0, PANELS, panel, 0)
    outs[2].start()
    with jax.named_scope("late"):
        lax.fori_loop(early + STEPS * each, total, relay, 0)
    with jax.named_scope("sum"):
        def add(q, carry):
            cols[chunk(q)] = cbuf[chunk(q)] + (rin[chunk(q)] + lin[chunk(q)])
            return carry

        lax.fori_loop(0, CHUNKS, add, 0)
        outs[3].start()
        count = tops.shape[0]
        top = tops[...]
        remote(topland, topland, topsend, toprecv, {"col": c}).wait()
        for shift in range(1, nc):
            top = top + topland[pl.ds((shift - 1) * count, count)]
        topsum[...] = top
        outs[4].start()

    with jax.named_scope("rowend"):
        act_rows[-1]()
        for copy in row_outs(1):
            copy.start()
    with jax.named_scope("headend"):
        heads.end()
        outs[1].start()

    with jax.named_scope("sent"):
        @pl.when(c < nc - 1)
        def _():
            remote(cbuf, rin, rs, rr.at[0], {"col": c + 1}).wait_send()

        @pl.when(c > 0)
        def _():
            remote(cbuf, lin, ls, lr.at[0], {"col": c - 1}).wait_send()

    with jax.named_scope("written"):
        for turn in range(PANELS):
            pltpu.make_async_copy(z_ref.at[turn], z_o.at[turn], zsem.at[turn]).wait()
            pltpu.make_async_copy(f_ref.at[turn], f_o.at[turn], fsem.at[turn]).wait()
        for out in outs + row_outs(0) + row_outs(1):
            out.wait()


def front(nr, nc, owner, index, cov, inn):
    rows, width = cov.shape
    part_p, groups, iw = inn.shape
    ratio = nr // nc
    h = ratio * part_p
    f32, bf16, i16 = jnp.float32, jnp.bfloat16, jnp.int16
    smem = pl.BlockSpec(memory_space=pltpu.SMEM)
    anywhere = pl.BlockSpec(memory_space=pl.ANY)
    vmem = pltpu.VMEM
    dma = pltpu.SemaphoreType.DMA
    both = PANELS * B
    count = PANELS * (rows // B)
    scratch = [vmem((rows, width), f32), dma, vmem(inn.shape, f32), dma, dma((5,)), dma((PANELS,)), dma((PANELS,)), dma((4,))]
    scratch += [vmem((rows, both), i16)] * 6 + [dma, dma((CHUNKS,))] * 2
    scratch += [vmem((count, LANES), f32), vmem(((nc - 1) * count, LANES), f32), dma, dma, vmem((count, LANES), f32)]
    scratch += [vmem((both, width), bf16)] * 2 + spread_scratch(both, width, bf16, nr)
    packed = nr * (-(-(B // 4 * 3) // (8 * nr)) * 8)
    scratch += [vmem((B, B), f32)] + [vmem((packed, B), f32)] * 2 + direct_scratch(packed, B, nr, nc)
    scratch += [vmem((2 * B, B), f32)] * 2 + spread_scratch(2 * B, B, f32, nr, nc)
    scratch += [vmem((PANELS * h, B), f32)] * 2 + direct_scratch(PANELS * h, B, nr, nc)
    scratch += [vmem((groups, part_p, iw), i16), vmem((nr * part_p, iw), i16), vmem((h, nc * iw), i16), vmem((h, nc * iw), f32)]
    scratch += [vmem((8, LANES), f32), vmem((nr * 8, LANES), f32), vmem((nr * 8, LANES), f32)]
    scratch += [dma] * 8
    scratch += [vmem((B, B), f32), vmem((B, WIDE), f32), vmem((B // SUB, SUB, WIDE), f32), vmem((B, B), f32)]
    scratch += [vmem((PANELS, B, B), f32)] * 2 + [vmem((B, B), bf16), vmem((rows, both), f32)]
    return pl.pallas_call(
        functools.partial(front_kernel, nr, nc),
        out_shape=(
            jax.ShapeDtypeStruct((rows, both), i16),
            jax.ShapeDtypeStruct((count, LANES), f32),
            jax.ShapeDtypeStruct((both, width), bf16),
            jax.ShapeDtypeStruct((h, nc * iw), f32),
            jax.ShapeDtypeStruct((PANELS * h, B), f32),
            jax.ShapeDtypeStruct((PANELS, B, B), f32),
            jax.ShapeDtypeStruct((PANELS, B, B), f32),
            jax.ShapeDtypeStruct((B, B), bf16),
        ),
        in_specs=[smem, smem, anywhere, anywhere],
        out_specs=(anywhere,) * 8,
        scratch_shapes=scratch,
        compiler_params=pltpu.CompilerParams(
            collective_id=0, has_side_effects=True, vmem_limit_bytes=56 * 1024 * 1024
        ),
    )(owner, index, cov, inn)


def tail_kernel(
    own_ref, idx_ref, w_any, cols_any, tops_any, rowp_any, f_any, z_any, x_any, vs_any, v_any,
    o_any, vout_any,
    w_ref, o_ref, cols_ref, tops_ref, rowp_ref, f_ref, z_ref, x_ref, vs_ref, v_ref, vout_ref, q_ref, half_ref,
    insem, wsem, osem, vsem, *, rb, cb,
):
    g = idx_ref[0]
    row0 = lax.axis_index("row") * rb
    col0 = lax.axis_index("col") * cb
    h = v_ref.shape[0]
    pairs = [
        (z_any, z_ref), (x_any, x_ref), (rowp_any, rowp_ref), (tops_any, tops_ref), (cols_any, cols_ref),
        (vs_any, vs_ref), (v_any, v_ref), (f_any, f_ref),
    ]
    ins = [pltpu.make_async_copy(src, dst, insem.at[i]) for i, (src, dst) in enumerate(pairs)]

    def stripe_in(j):
        span = rows_at(j * B, B)
        return pltpu.make_async_copy(w_any.at[:, span], w_ref.at[:, span], wsem.at[j])

    def stripe_out(j):
        span = rows_at(j * B, B)
        return pltpu.make_async_copy(o_ref.at[:, span], o_any.at[:, span], osem.at[j])

    for copy in ins[:5]:
        copy.start()
    for copy in ins[:3]:
        copy.wait()
    for j in range(cb):
        stripe_in(j).start()
    for copy in ins[5:]:
        copy.start()

    with jax.named_scope("qpanels"):
        x = x_ref[...]
        zh0, zl0 = split_bf16(z_ref[0])
        zh1, zl1 = split_bf16(z_ref[1])
        for k in range(cb):
            span = slice(k * B, (k + 1) * B)
            own = own_ref[col0 + k]
            q0 = dot(zh0, rowp_ref[:B, span]) + dot(zl0, rowp_ref[:B, span])
            q0 = jnp.where(own > g, q0, 0.0).astype(jnp.bfloat16)
            r1 = (rowp_ref[B:, span].astype(jnp.float32) - dot(x, q0)).astype(jnp.bfloat16)
            q1 = dot(zh1, r1) + dot(zl1, r1)
            q_ref[:B, span] = q0
            q_ref[B:, span] = jnp.where(own > g + 1, q1, 0.0).astype(jnp.bfloat16)

    for copy in ins[3:5]:
        copy.wait()

    with jax.named_scope("panels"):
        for i in range(rb):
            span = slice(i * B, (i + 1) * B)
            own = own_ref[row0 + i]
            c0 = decode(cols_ref[span, :B], tops_ref[PANELS * i : PANELS * i + 1, :1])
            p0 = dot3(c0, z_ref[0], LAST)
            h0 = jnp.where(own > g, p0, 0.0).astype(jnp.bfloat16)
            c1 = decode(cols_ref[span, B:], tops_ref[PANELS * i + 1 : PANELS * i + 2, :1]) - dot(h0, x, LAST)
            p1 = dot3(c1, z_ref[1], LAST)
            half_ref[span, :B] = h0
            half_ref[span, B:] = jnp.where(own > g + 1, p1, 0.0).astype(jnp.bfloat16)

    for copy in ins[5:]:
        copy.wait()

    def stripe(j, carry):
        span = rows_at(j * B, B)
        cown = own_ref[col0 + j]
        stripe_in(j).wait()
        with jax.named_scope("update"):
            o_ref[:, span] = w_ref[:, span] - dot(half_ref[...], q_ref[:, span])

        @pl.when(cown > g)
        def _():
            for i in range(rb):
                rown = own_ref[row0 + i]

                @pl.when((rown == g) | ((rown == g + 1) & (cown > g + 1)))
                def _():
                    o_ref[i * B : (i + 1) * B, span] = jnp.zeros((B, B), jnp.float32)

        for turn in range(PANELS):
            @pl.when(cown == g + turn)
            def _():
                for i in range(rb):
                    part = slice(i * B, (i + 1) * B)
                    rown = own_ref[row0 + i]

                    @pl.when(rown > g + turn)
                    def _():
                        left = w_ref[part, span]
                        if turn:
                            left = left - dot(half_ref[part, :B], x_ref[...], LAST)
                        o_ref[part, span] = dot3(left, z_ref[turn], LAST)

                    @pl.when(rown == g + turn)
                    def _():
                        o_ref[part, span] = f_ref[turn]

        stripe_out(j).start()
        return carry

    lax.fori_loop(0, cb, stripe, 0)

    with jax.named_scope("solve"):
        w0 = dot3(vs_ref[:h], z_ref[0], LAST)
        w0h = w0.astype(jnp.bfloat16)
        w1 = dot3(vs_ref[h:] - dot(w0h, x, LAST), z_ref[1], LAST)
        w1h = w1.astype(jnp.bfloat16)
        for i in range(rb):
            span = slice(i * B, (i + 1) * B)
            own = own_ref[row0 + i]
            new = v_ref[:, span] - (dot(w0h, half_ref[span, :B], LAST) + dot(w1h, half_ref[span, B:], LAST))
            new = jnp.where(own == g, w0, new)
            vout_ref[:, span] = jnp.where(own == g + 1, w1, new)
        done = pltpu.make_async_copy(vout_ref, vout_any, vsem)
        done.start()

    with jax.named_scope("drain"):
        lax.fori_loop(0, cb, lambda j, k: (stripe_out(j).wait(), k)[1], 0)
        done.wait()


def tail(owner, index, w, cols, tops, rowp, factors, z, x, vs, v):
    rows, width = w.shape
    cb = width // B
    smem = pl.BlockSpec(memory_space=pltpu.SMEM)
    anywhere = pl.BlockSpec(memory_space=pl.ANY)
    dma = pltpu.SemaphoreType.DMA
    arrays = [w, w, cols, tops, rowp, factors, z, x, vs, v, v]
    return pl.pallas_call(
        functools.partial(tail_kernel, rb=rows // B, cb=cb),
        in_specs=[smem, smem] + [anywhere] * 9,
        out_specs=[anywhere] * 2,
        scratch_shapes=[pltpu.VMEM(a.shape, a.dtype) for a in arrays]
        + [pltpu.VMEM((2 * B, width), jnp.bfloat16), pltpu.VMEM((rows, 2 * B), jnp.bfloat16)]
        + [dma((8,)), dma((cb,)), dma((cb,)), dma],
        out_shape=(jax.ShapeDtypeStruct(w.shape, w.dtype), jax.ShapeDtypeStruct(v.shape, v.dtype)),
        compiler_params=pltpu.CompilerParams(vmem_limit_bytes=60 * 1024 * 1024),
    )(owner, index, w, cols, tops, rowp, factors, z, x, vs, v)


def per_device(covariance, innovations, block_owner, panel_index):
    nr, nc = lax.axis_size("row"), lax.axis_size("col")
    cols, tops, rowp, v, vs, factors, z, x = front(nr, nc, block_owner, panel_index, covariance, innovations)
    return tail(block_owner, panel_index, covariance, cols, tops, rowp, factors, z, x, vs, v)


def solution(mesh):
    placed = (P("row", "col"), P("row", None, "col"), P(), P())
    return jax.shard_map(
        per_device,
        mesh=mesh,
        in_specs=placed,
        out_specs=(P("row", "col"), P("col", "row")),
        check_vma=False,
    )
```
